32 devices in a mesh: rows: 8 (over z, x), sub: 4 (over y, core).
Axes of the slice: x: 2, y: 2, z: 4, core: 2. Of those that a mesh axis runs over, the one named last changes fastest.
Arguments:
- queries: float32 [16384, 256], P(('rows', 'sub')), may hold values from -6 to 6
- row_scale: float32 [16384], P(('rows', 'sub')), may hold values from 0.6 to 1.6
- leaf_basis: float32 [16384, 128], P(('rows', 'sub')), may hold values from -6 to 6
- leaf_cores: float32 [8, 128, 128], P('rows'), as said below
- level_basis: float32 [3, 16384, 128], P(None, ('rows', 'sub')), may hold values from -6 to 6
- level_cores: float32 [14, 128, 128], replicated, as said below
Outputs:
- solution: float32 [16384, 256], P(('rows', 'sub'))
The draws below stay inside these ranges and needn't reach their ends.
Inputs may be any that keep to these rules, and one draw needn't show every extreme that they name: `leaf_cores`: each core is divided by the rows of its block: every entry lies within 3 / (512 * 4) of zero. `level_cores`: each core is divided by the rows of its node: every entry of a level-l core lies within 3 * 2 ** l / 16384 of zero.
All inputs are finite; a program needn't handle non-finite values.
Results may differ from the reference program's by a relative error of at most 0.0001.
Values sent between devices are 32-bit elements; how exact they have to be, the bound alone decides.
No kernel may reach another device: no remote copies, remote signals or barrier semaphores. Data moves between devices by JAX's collectives and lax.ppermute only.
A program may use at most 64 MiB of HBM per device.

```python
import math
import jax
import jax.numpy as jnp
from jax import lax

RANK = 128
QUERIES = 256
LEVELS = 3
ORDER = 16384
N_ROWS = 8


def core_block(key, pieces, node_rows):
    key_diag, key_off = jax.random.split(jax.random.fold_in(key, 17))
    diagonal_part = jax.random.uniform(key_diag, (pieces, RANK), jnp.float32, 0.4, 1.5)
    off_normal = jnp.clip(jax.random.normal(key_off, (pieces, RANK, RANK), jnp.float32), -4.0, 4.0)
    off_part = off_normal * (0.35 / RANK ** 0.5)
    identity_block = jnp.eye(RANK, dtype=jnp.float32)
    return (diagonal_part[:, :, None] * identity_block[None] + off_part) / node_rows


def draw_leaf_cores(key, part):
    return core_block(key, N_ROWS, ORDER // N_ROWS)


def draw_level_cores(key, part):
    blocks = []
    for height in range(LEVELS):
        pieces = 2 ** (height + 1)
        blocks.append(core_block(jax.random.fold_in(key, height + 1), pieces, ORDER // pieces))
    return jnp.concatenate(blocks, axis=0)


def shard_levels(stream_key, extent, cuts, least, high):
    gain, own = 1.0, jax.random.fold_in(stream_key, 6)
    for dim, parts in cuts:
        heights = jnp.exp(jax.random.uniform(jax.random.fold_in(own, dim), (parts,), jnp.float32, least / len(cuts), high / len(cuts)))
        gain = gain * jnp.repeat(heights, extent[dim] // parts).reshape([-1 if axis == dim else 1 for axis in range(len(extent))])
    return gain


def normal_values(rng, dims, scale, most, cuts=(), kind=jnp.bfloat16):
    array = scale * jax.random.normal(rng, dims, jnp.float32)
    if cuts:
        array = array * shard_levels(rng, dims, cuts, -0.22, 0.18)
    return jnp.clip(array, -most, most).astype(kind)


def setup_inputs(seed: int = 0) -> dict:
    arg_keys = jax.random.split(jax.random.key(seed), 7)
    return {
        "queries": normal_values(arg_keys[0], (ORDER, QUERIES), 1.0, 6.0, ((0, 32),), jnp.float32),
        "row_scale": jnp.clip(jnp.exp(math.log(1.6) - 0.98082923 * jax.random.uniform(arg_keys[1], (ORDER,), jnp.float32) ** shard_levels(arg_keys[1], (ORDER,), ((0, 32),), -0.2, 0.2)), 0.6, 1.6),
        "leaf_basis": normal_values(arg_keys[2], (ORDER, RANK), 1.0, 6.0, ((0, 32),), jnp.float32),
        "leaf_cores": draw_leaf_cores(jax.random.fold_in(arg_keys[6], 71), 0),
        "level_basis": normal_values(arg_keys[4], (LEVELS, ORDER, RANK), 1.0, 6.0, ((1, 32),), jnp.float32),
        "level_cores": draw_level_cores(jax.random.fold_in(arg_keys[6], 71), 0),
    }


precise = lax.Precision.HIGHEST


def apply_factor(values, vectors, cores, pieces, transposed):
    row_count, col_count = values.shape
    blocks = values.reshape(pieces, row_count // pieces, col_count)
    bases = vectors.reshape(pieces, row_count // pieces, vectors.shape[1])
    moments = jnp.einsum("nrk,nrq->nkq", bases, blocks, precision=precise)
    used_cores = jnp.swapaxes(cores, 1, 2) if transposed else cores
    inner_core = jnp.einsum("nkj,njq->nkq", used_cores, moments, precision=precise)
    result = blocks - jnp.einsum("nrk,nkq->nrq", bases, inner_core, precision=precise)
    return result.reshape(row_count, col_count)


def reference(queries, row_scale, leaf_basis, leaf_cores, level_basis, level_cores):
    row_weights = row_scale[:, None]
    current = row_weights * apply_factor(queries, leaf_basis, leaf_cores, N_ROWS, False)
    for height in range(LEVELS, 0, -1):
        offset = 2 ** height - 2
        current = apply_factor(current, level_basis[height - 1], level_cores[offset:offset + 2 ** height], 2 ** height, False)
    for height in range(1, LEVELS + 1):
        offset = 2 ** height - 2
        current = apply_factor(current, level_basis[height - 1], level_cores[offset:offset + 2 ** height], 2 ** height, True)
    current = row_weights * current
    return apply_factor(current, leaf_basis, leaf_cores, N_ROWS, True)
```

```python
import functools

import jax
import jax.numpy as jnp
from jax import lax
from jax.experimental import pallas as pl
from jax.experimental.pallas import tpu as pltpu
from jax.sharding import PartitionSpec as P


FLOAT = jnp.float32


def halves(value):
    high = value.astype(jnp.bfloat16)
    return high, (value - high.astype(FLOAT)).astype(jnp.bfloat16)


def dot(left, right, left_dim=1):
    mult = functools.partial(
        lax.dot_general,
        dimension_numbers=(((left_dim,), (0,)), ((), ())),
        preferred_element_type=FLOAT,
    )
    left_high, left_low = halves(left)
    right_high, right_low = halves(right)
    return mult(left_high, right_high) + (mult(left_high, right_low) + mult(left_low, right_high))


def column_scale(scale_ref, width):
    lanes = scale_ref.shape[1]
    blocks = [
        jnp.broadcast_to(scale_ref[i : i + 1, :], (lanes, lanes)).T for i in range(scale_ref.shape[0])
    ]
    block = jnp.concatenate(blocks, axis=0)
    return block if width == lanes else jnp.concatenate([block] * (width // lanes), axis=1)


def core_side():
    return lax.rem(lax.axis_index("sub"), 2)


def store_halves(value, axis, keep_ref, send_ref, offset):
    size = value.shape[axis] // 2
    first = lax.slice_in_dim(value, 0, size, axis=axis)
    second = lax.slice_in_dim(value, size, 2 * size, axis=axis)
    where = pl.ds(offset, first.shape[0])
    side = core_side()

    @pl.when(side == 0)
    def _():
        keep_ref[where, :] = first
        send_ref[where, :] = second

    @pl.when(side == 1)
    def _():
        keep_ref[where, :] = second
        send_ref[where, :] = first


def join(own, other, axis):
    first = core_side() == 0
    return jnp.concatenate([jnp.where(first, own, other), jnp.where(first, other, own)], axis=axis)


def call(body, out_shapes, *operands, name, flops):
    space = pl.BlockSpec(memory_space=pltpu.VMEM)
    size = sum(4 * a.size for a in operands)
    outs = [jax.ShapeDtypeStruct(shape, FLOAT) for shape in out_shapes]
    return pl.pallas_call(
        body,
        out_shape=outs,
        in_specs=[space] * len(operands),
        out_specs=[space] * len(outs),
        name=name,
        cost_estimate=pl.CostEstimate(flops=flops, bytes_accessed=size, transcendentals=0),
    )(*operands)


def swap(array, axis, bit):
    return lax.ppermute(array, axis, [(i, i ^ 1 << bit) for i in range(lax.axis_size(axis))])


def partial_sums(array, axis, bits):
    bits = list(bits)
    if not bits:
        return [array]
    for bit in bits[:-1]:
        array = array + swap(array, axis, bit)
    return [array, swap(array, axis, bits[-1])]


def add_all(parts):
    return functools.reduce(lambda a, b: a + b, parts)


def shards(queries, row_scale, leaf_basis, leaf_cores, level_basis, level_cores):
    levels = level_basis.shape[0]
    count = levels + 1
    top = levels
    rows_here, rank = leaf_basis.shape
    columns = queries.shape[1]
    wide = columns // 2
    groups, sub = lax.axis_size("rows"), lax.axis_size("sub")
    heights = [None] + [levels + 1 - e for e in range(1, count)]
    widths = [1] + [groups // 2 ** heights[e] for e in range(1, count)]
    head = sum(w == 1 for w in widths)
    bits = [range(0)] + [
        range(widths[e - 1].bit_length() - 1, widths[e].bit_length() - 1) for e in range(1, count)
    ]
    blocks = [list(range(e + 1 if e < head else e, count)) for e in range(count)]
    leaf_bits = range(1, sub.bit_length() - 1)
    small = 2 * 3 * rank**3

    scale = row_scale.reshape(-1, rank)
    index = lax.axis_index("rows")
    cores = [leaf_cores[0]] + [
        lax.dynamic_index_in_dim(level_cores, 2 ** heights[e] - 2 + index // widths[e], 0, keepdims=False)
        for e in range(1, count)
    ]

    half_rows = [len(b) * rank // 2 for b in blocks]
    starts = [sum(half_rows[:e]) for e in range(count + 1)]

    def gram_body(scale_ref, leaf_ref, level_ref, keep_ref, send_ref):
        vectors = [column_scale(scale_ref, rank) * leaf_ref[...]]
        vectors += [level_ref[levels - e] for e in range(1, count)]
        for e in range(count):
            left = jnp.concatenate([vectors[f] for f in blocks[e]], axis=1)
            store_halves(dot(left, vectors[e], 0), 0, keep_ref, send_ref, starts[e])

    gram_shape = (starts[count], rank)
    gram_keep, gram_send = call(
        gram_body,
        [gram_shape] * 2,
        scale,
        leaf_basis,
        level_basis,
        name="gram",
        flops=small * sum(map(len, blocks)) * rows_here // rank,
    )
    gram_chip = gram_keep + swap(gram_send, "sub", 0)
    gram_leaf = add_all(partial_sums(gram_chip, "sub", leaf_bits))

    def moment_body(scale_ref, queries_ref, leaf_ref, level_ref, keep_ref, send_ref):
        values = queries_ref[...]
        store_halves(dot(leaf_ref[...], values, 0), 1, keep_ref, send_ref, 0)
        values = column_scale(scale_ref, columns) * values
        for e in range(1, count):
            store_halves(dot(level_ref[levels - e], values, 0), 1, keep_ref, send_ref, e * rank)

    moment_keep, moment_send = call(
        moment_body,
        [(count * rank, wide)] * 2,
        scale,
        queries,
        leaf_basis,
        level_basis,
        name="moment",
        flops=small * count * 2 * rows_here // rank,
    )
    moment_chip = moment_keep + swap(moment_send, "sub", 0)
    moment_parts = partial_sums(moment_chip, "sub", leaf_bits)

    def late_body(scale_ref, queries_ref, leaf_ref, level_ref, keep_ref, send_ref):
        spread = column_scale(scale_ref, rank)
        vectors = spread * leaf_ref[...]
        store_halves(dot(spread * vectors, queries_ref[...], 0), 1, keep_ref, send_ref, 0)
        for e in range(head):
            basis = vectors if e == 0 else level_ref[levels - e]
            store_halves(dot(basis, basis, 0), 0, keep_ref, send_ref, rank + e * rank // 2)

    late_keep, late_send = call(
        late_body,
        [(rank + head * rank // 2, rank)] * 2,
        scale,
        queries,
        leaf_basis,
        level_basis,
        name="late",
        flops=small * (2 + head) * rows_here // rank,
    )
    late_chip = late_keep + swap(late_send, "sub", 0)
    late_leaf = add_all(partial_sums(late_chip, "sub", leaf_bits))
    late_other = swap(late_leaf[rank:], "sub", 0)

    def product_body(group, own_ref, other_ref, *refs):
        core_refs, out_refs = refs[: len(group)], refs[len(group) :]
        base = starts[group[0]]
        for place, e in enumerate(group):
            where = pl.ds(starts[e] - base, half_rows[e])
            out_refs[place][...] = dot(join(own_ref[where, :], other_ref[where, :], 0), core_refs[place][...])

    def products(group, own):
        return call(
            functools.partial(product_body, group),
            [(2 * half_rows[e], rank) for e in group],
            own,
            swap(own, "sub", 0),
            *[cores[e] for e in group],
            name=f"product{group[0]}",
            flops=small * sum(len(blocks[e]) for e in group),
        )

    factors = products(list(range(head)), gram_leaf[: starts[head]])
    remaining = gram_leaf[starts[head] :]
    for e in range(head, count):
        remaining = add_all(partial_sums(remaining, "rows", bits[e]))
        factors += products([e], remaining[: half_rows[e]])
        remaining = remaining[half_rows[e] :]

    def head_body(*refs):
        part_refs, factor_refs = refs[: len(moment_parts)], refs[len(moment_parts) : -2]
        own_ref, rest_ref = refs[-2:]
        rest = add_all([part[...] for part in part_refs])
        for e in range(head):
            own, rest = rest[:rank], rest[rank:]
            own_ref[e * rank : (e + 1) * rank, :] = own
            rest = rest - dot(factor_refs[e][...], own)
        rest_ref[...] = rest

    head_moments, rest = call(
        head_body,
        [(head * rank, wide), ((count - head) * rank, wide)],
        *moment_parts,
        *factors[:head],
        name="head",
        flops=small * sum(map(len, blocks[:head])),
    )

    def step_body(size, *refs):
        part_refs, factor_ref, own_ref, rest_ref = refs[:size], refs[size], refs[-2], refs[-1]
        total = add_all([part[...] for part in part_refs])
        own_ref[...] = total[:rank]
        rest_ref[...] = total[rank:] - dot(factor_ref[rank:, :], total[:rank])

    moments = []
    for e in range(head, top):
        parts = partial_sums(rest, "rows", bits[e])
        own, rest = call(
            functools.partial(step_body, len(parts)),
            [(rank, wide), ((top - e) * rank, wide)],
            *parts,
            factors[e],
            name=f"step{e}",
            flops=small * (top - e),
        )
        moments.append([own, swap(own, "sub", 0)])
    parts = partial_sums(rest, "rows", bits[top])
    moments.append(parts + [swap(part, "sub", 0) for part in parts])

    def own_body(moment_ref, late_ref, other_ref, *refs):
        core_refs, factor_refs, out_ref = refs[:head], refs[head:-1], refs[-1]
        coefficients = [None] * head
        for e in reversed(range(head)):
            core = core_refs[e][...]
            where = slice(e * rank // 2, (e + 1) * rank // 2)
            gram = join(late_ref[rank:, :][where], other_ref[where, :], 0)
            moment = moment_ref[e * rank : (e + 1) * rank, :]
            first = dot(core, moment)
            target = (late_ref[:rank, :] if e == 0 else moment) - dot(gram, first)
            value = dot(core, target, 0)
            if e:
                value = value + first
            else:
                out_ref[head * rank :, :] = first
            for f in range(e + 1, head):
                block = factor_refs[e][(f - e - 1) * rank : (f - e) * rank, :]
                value = value - dot(block, coefficients[f], 0)
            coefficients[e] = value
            out_ref[e * rank : (e + 1) * rank, :] = value

    (own,) = call(
        own_body,
        [((head + 1) * rank, wide)],
        head_moments,
        late_leaf,
        late_other,
        *cores[:head],
        *factors[:head],
        name="own",
        flops=small * 6,
    )
    other = swap(own, "sub", 0)

    def start_body(scale_ref, queries_ref, leaf_ref, level_ref, own_ref, other_ref, out_ref):
        spread = column_scale(scale_ref, rank)
        whole = join(own_ref[...], other_ref[...], 1)
        left = [spread * (spread * leaf_ref[...])] + [spread * level_ref[levels - e] for e in range(1, head)]
        right = [whole[head * rank :]] + [whole[e * rank : (e + 1) * rank] for e in range(1, head)]
        left.append(leaf_ref[...])
        right.append(whole[:rank])
        total = dot(jnp.concatenate(left, axis=1), jnp.concatenate(right, axis=0))
        square = spread * spread
        square = jnp.concatenate([square] * (columns // rank), axis=1)
        out_ref[...] = square * queries_ref[...] - total

    (base,) = call(
        start_body,
        [(rows_here, columns)],
        scale,
        queries,
        leaf_basis,
        level_basis,
        own,
        other,
        name="start",
        flops=small * 2 * (head + 1) * rows_here // rank,
    )

    def response_body(scale_ref, leaf_ref, level_ref, *refs):
        core_refs, factor_refs, out_ref = refs[:levels], refs[levels:-1], refs[-1]
        spread = column_scale(scale_ref, rank)
        for e in range(head, count):
            core = core_refs[e - 1][...]
            gains = {e: core + core.T - dot(core, factor_refs[e][:rank, :], 0)}
            for f in reversed(range(e)):
                at = (0 if f < head else 1) * rank
                block = factor_refs[f][at : at + (e - f) * rank, :]
                stack = jnp.concatenate([gains[g] for g in range(f + 1, e + 1)], axis=0)
                gains[f] = -dot(block, stack, 0)
            left = [spread * level_ref[levels - f] for f in range(1, e + 1)] + [leaf_ref[...]]
            right = [gains[f] for f in range(1, e + 1)] + [gains[0]]
            out_ref[:, (e - head) * rank : (e - head + 1) * rank] = dot(
                jnp.concatenate(left, axis=1), jnp.concatenate(right, axis=0)
            )

    (response,) = call(
        response_body,
        [(rows_here, (count - head) * rank)],
        scale,
        leaf_basis,
        level_basis,
        *cores[1:],
        *factors,
        name="response",
        flops=small * (count - head) * count * rows_here // rank,
    )

    flat = [part for parts in moments for part in parts]
    sizes = [len(parts) // 2 for parts in moments]

    def last_body(base_ref, response_ref, *refs):
        part_refs, out_ref = refs[:-1], refs[-1]
        stack, at = [], 0
        for size in sizes:
            own = add_all([part[...] for part in part_refs[at : at + size]])
            other = add_all([part[...] for part in part_refs[at + size : at + 2 * size]])
            stack.append(join(own, other, 1))
            at += 2 * size
        out_ref[...] = base_ref[...] - dot(response_ref[...], jnp.concatenate(stack, axis=0))

    (out,) = call(
        last_body,
        [(rows_here, columns)],
        base,
        response,
        *flat,
        name="last",
        flops=small * 2 * (count - head) * rows_here // rank,
    )
    return out


def solution(mesh):
    in_specs = (
        P(("rows", "sub"), None),
        P(("rows", "sub")),
        P(("rows", "sub"), None),
        P("rows", None, None),
        P(None, ("rows", "sub"), None),
        P(),
    )
    out_specs = P(("rows", "sub"), None)
    return jax.shard_map(shards, mesh=mesh, in_specs=in_specs, out_specs=out_specs, check_vma=False)
```

```python
import functools

import jax
import jax.numpy as jnp
from jax import lax
from jax.experimental import pallas as pl
from jax.experimental.pallas import tpu as pltpu
from jax.sharding import PartitionSpec as P


FLOAT = jnp.float32
VMEM_LIMIT = 16 << 20


def halves(value):
    high = value.astype(jnp.bfloat16)
    return high, (value - high.astype(FLOAT)).astype(jnp.bfloat16)


def dot(left, right, left_dim=1):
    mult = functools.partial(
        lax.dot_general,
        dimension_numbers=(((left_dim,), (0,)), ((), ())),
        preferred_element_type=FLOAT,
    )
    left_high, left_low = halves(left)
    right_high, right_low = halves(right)
    return mult(left_high, right_high) + (mult(left_high, right_low) + mult(left_low, right_high))


def column_scale(scale_ref, width):
    lanes = scale_ref.shape[1]
    blocks = [
        jnp.broadcast_to(scale_ref[i : i + 1, :], (lanes, lanes)).T for i in range(scale_ref.shape[0])
    ]
    block = jnp.concatenate(blocks, axis=0)
    return block if width == lanes else jnp.concatenate([block] * (width // lanes), axis=1)


def core_side():
    return lax.rem(lax.axis_index("sub"), 2)


def store_halves(value, axis, keep_ref, send_ref, offset):
    size = value.shape[axis] // 2
    first = lax.slice_in_dim(value, 0, size, axis=axis)
    second = lax.slice_in_dim(value, size, 2 * size, axis=axis)
    where = pl.ds(offset, first.shape[0])
    side = core_side()

    @pl.when(side == 0)
    def _():
        keep_ref[where, :] = first
        send_ref[where, :] = second

    @pl.when(side == 1)
    def _():
        keep_ref[where, :] = second
        send_ref[where, :] = first


def join(own, other, axis):
    first = core_side() == 0
    return jnp.concatenate([jnp.where(first, own, other), jnp.where(first, other, own)], axis=axis)


def call(body, out_shapes, *operands, name, flops):
    space = pl.BlockSpec(memory_space=pltpu.VMEM)
    size = sum(4 * a.size for a in operands)
    outs = [jax.ShapeDtypeStruct(shape, FLOAT) for shape in out_shapes]
    return pl.pallas_call(
        body,
        out_shape=outs,
        in_specs=[space] * len(operands),
        out_specs=[space] * len(outs),
        name=name,
        compiler_params=pltpu.CompilerParams(vmem_limit_bytes=VMEM_LIMIT),
        cost_estimate=pl.CostEstimate(flops=flops, bytes_accessed=size, transcendentals=0),
    )(*operands)


def swap(array, axis, bit):
    return lax.ppermute(array, axis, [(i, i ^ 1 << bit) for i in range(lax.axis_size(axis))])


def partial_sums(array, axis, bits):
    bits = list(bits)
    if not bits:
        return [array]
    for bit in bits[:-1]:
        array = array + swap(array, axis, bit)
    return [array, swap(array, axis, bits[-1])]


def add_all(parts):
    return functools.reduce(lambda a, b: a + b, parts)


def shards(queries, row_scale, leaf_basis, leaf_cores, level_basis, level_cores):
    levels = level_basis.shape[0]
    count = levels + 1
    top = levels
    rows_here, rank = leaf_basis.shape
    columns = queries.shape[1]
    wide = columns // 2
    groups, sub = lax.axis_size("rows"), lax.axis_size("sub")
    heights = [None] + [levels + 1 - e for e in range(1, count)]
    widths = [1] + [groups // 2 ** heights[e] for e in range(1, count)]
    head = sum(w == 1 for w in widths)
    bits = [range(0)] + [
        range(widths[e - 1].bit_length() - 1, widths[e].bit_length() - 1) for e in range(1, count)
    ]
    blocks = [list(range(e + 1 if e < head else e, count)) for e in range(count)]
    leaf_bits = range(1, sub.bit_length() - 1)
    small = 2 * 3 * rank**3

    scale = row_scale.reshape(-1, rank)
    index = lax.axis_index("rows")
    cores = [leaf_cores[0]] + [
        lax.dynamic_index_in_dim(level_cores, 2 ** heights[e] - 2 + index // widths[e], 0, keepdims=False)
        for e in range(1, count)
    ]

    half_rows = [len(b) * rank // 2 for b in blocks]
    starts = [sum(half_rows[:e]) for e in range(count + 1)]

    def gram_body(scale_ref, leaf_ref, level_ref, keep_ref, send_ref):
        vectors = [column_scale(scale_ref, rank) * leaf_ref[...]]
        vectors += [level_ref[levels - e] for e in range(1, count)]
        for e in range(count):
            left = jnp.concatenate([vectors[f] for f in blocks[e]], axis=1)
            store_halves(dot(left, vectors[e], 0), 0, keep_ref, send_ref, starts[e])

    gram_shape = (starts[count], rank)
    gram_keep, gram_send = call(
        gram_body,
        [gram_shape] * 2,
        scale,
        leaf_basis,
        level_basis,
        name="gram",
        flops=small * sum(map(len, blocks)) * rows_here // rank,
    )
    gram_chip = gram_keep + swap(gram_send, "sub", 0)
    gram_leaf = add_all(partial_sums(gram_chip, "sub", leaf_bits))

    def moment_body(scale_ref, queries_ref, leaf_ref, level_ref, keep_ref, send_ref):
        values = queries_ref[...]
        store_halves(dot(leaf_ref[...], values, 0), 1, keep_ref, send_ref, 0)
        values = column_scale(scale_ref, columns) * values
        for e in range(1, count):
            store_halves(dot(level_ref[levels - e], values, 0), 1, keep_ref, send_ref, e * rank)

    moment_keep, moment_send = call(
        moment_body,
        [(count * rank, wide)] * 2,
        scale,
        queries,
        leaf_basis,
        level_basis,
        name="moment",
        flops=small * count * 2 * rows_here // rank,
    )
    moment_chip = moment_keep + swap(moment_send, "sub", 0)
    moment_parts = partial_sums(moment_chip, "sub", leaf_bits)

    def late_body(scale_ref, queries_ref, leaf_ref, level_ref, keep_ref, send_ref):
        spread = column_scale(scale_ref, rank)
        vectors = spread * leaf_ref[...]
        store_halves(dot(spread * vectors, queries_ref[...], 0), 1, keep_ref, send_ref, 0)
        for e in range(head):
            basis = vectors if e == 0 else level_ref[levels - e]
            store_halves(dot(basis, basis, 0), 0, keep_ref, send_ref, rank + e * rank // 2)

    late_keep, late_send = call(
        late_body,
        [(rank + head * rank // 2, rank)] * 2,
        scale,
        queries,
        leaf_basis,
        level_basis,
        name="late",
        flops=small * (2 + head) * rows_here // rank,
    )
    late_chip = late_keep + swap(late_send, "sub", 0)
    late_leaf = add_all(partial_sums(late_chip, "sub", leaf_bits))
    late_other = swap(late_leaf[rank:], "sub", 0)

    def product_body(group, own_ref, other_ref, *refs):
        core_refs, out_refs = refs[: len(group)], refs[len(group) :]
        base = starts[group[0]]
        for place, e in enumerate(group):
            where = pl.ds(starts[e] - base, half_rows[e])
            out_refs[place][...] = dot(join(own_ref[where, :], other_ref[where, :], 0), core_refs[place][...])

    def products(group, own):
        return call(
            functools.partial(product_body, group),
            [(2 * half_rows[e], rank) for e in group],
            own,
            swap(own, "sub", 0),
            *[cores[e] for e in group],
            name=f"product{group[0]}",
            flops=small * sum(len(blocks[e]) for e in group),
        )

    factors = products(list(range(head)), gram_leaf[: starts[head]])
    remaining = gram_leaf[starts[head] :]
    for e in range(head, count):
        remaining = add_all(partial_sums(remaining, "rows", bits[e]))
        factors += products([e], remaining[: half_rows[e]])
        remaining = remaining[half_rows[e] :]

    def head_body(*refs):
        part_refs, factor_refs = refs[: len(moment_parts)], refs[len(moment_parts) : -2]
        own_ref, rest_ref = refs[-2:]
        rest = add_all([part[...] for part in part_refs])
        for e in range(head):
            own, rest = rest[:rank], rest[rank:]
            own_ref[e * rank : (e + 1) * rank, :] = own
            rest = rest - dot(factor_refs[e][...], own)
        rest_ref[...] = rest

    head_moments, rest = call(
        head_body,
        [(head * rank, wide), ((count - head) * rank, wide)],
        *moment_parts,
        *factors[:head],
        name="head",
        flops=small * sum(map(len, blocks[:head])),
    )

    def step_body(size, *refs):
        part_refs, factor_ref, own_ref, rest_ref = refs[:size], refs[size], refs[-2], refs[-1]
        total = add_all([part[...] for part in part_refs])
        own_ref[...] = total[:rank]
        rest_ref[...] = total[rank:] - dot(factor_ref[rank:, :], total[:rank])

    moments = []
    for e in range(head, top):
        parts = partial_sums(rest, "rows", bits[e])
        own, rest = call(
            functools.partial(step_body, len(parts)),
            [(rank, wide), ((top - e) * rank, wide)],
            *parts,
            factors[e],
            name=f"step{e}",
            flops=small * (top - e),
        )
        moments.append([own, swap(own, "sub", 0)])
    parts = partial_sums(rest, "rows", bits[top])
    moments.append(parts + [swap(part, "sub", 0) for part in parts])

    def own_body(moment_ref, late_ref, other_ref, *refs):
        core_refs, factor_refs, out_ref = refs[:head], refs[head:-1], refs[-1]
        coefficients = [None] * head
        for e in reversed(range(head)):
            core = core_refs[e][...]
            where = slice(e * rank // 2, (e + 1) * rank // 2)
            gram = join(late_ref[rank:, :][where], other_ref[where, :], 0)
            moment = moment_ref[e * rank : (e + 1) * rank, :]
            first = dot(core, moment)
            target = (late_ref[:rank, :] if e == 0 else moment) - dot(gram, first)
            value = dot(core, target, 0)
            if e:
                value = value + first
            else:
                out_ref[head * rank :, :] = first
            for f in range(e + 1, head):
                block = factor_refs[e][(f - e - 1) * rank : (f - e) * rank, :]
                value = value - dot(block, coefficients[f], 0)
            coefficients[e] = value
            out_ref[e * rank : (e + 1) * rank, :] = value

    (own,) = call(
        own_body,
        [((head + 1) * rank, wide)],
        head_moments,
        late_leaf,
        late_other,
        *cores[:head],
        *factors[:head],
        name="own",
        flops=small * 6,
    )
    other = swap(own, "sub", 0)

    def start_body(scale_ref, queries_ref, leaf_ref, level_ref, own_ref, other_ref, out_ref):
        spread = column_scale(scale_ref, rank)
        whole = join(own_ref[...], other_ref[...], 1)
        left = [spread * (spread * leaf_ref[...])] + [spread * level_ref[levels - e] for e in range(1, head)]
        right = [whole[head * rank :]] + [whole[e * rank : (e + 1) * rank] for e in range(1, head)]
        left.append(leaf_ref[...])
        right.append(whole[:rank])
        total = dot(jnp.concatenate(left, axis=1), jnp.concatenate(right, axis=0))
        square = spread * spread
        square = jnp.concatenate([square] * (columns // rank), axis=1)
        out_ref[...] = square * queries_ref[...] - total

    (base,) = call(
        start_body,
        [(rows_here, columns)],
        scale,
        queries,
        leaf_basis,
        level_basis,
        own,
        other,
        name="start",
        flops=small * 2 * (head + 1) * rows_here // rank,
    )

    def response_body(scale_ref, leaf_ref, level_ref, *refs):
        core_refs, factor_refs, out_ref = refs[:levels], refs[levels:-1], refs[-1]
        spread = column_scale(scale_ref, rank)
        for e in range(head, count):
            core = core_refs[e - 1][...]
            gains = {e: core + core.T - dot(core, factor_refs[e][:rank, :], 0)}
            for f in reversed(range(e)):
                at = (0 if f < head else 1) * rank
                block = factor_refs[f][at : at + (e - f) * rank, :]
                stack = jnp.concatenate([gains[g] for g in range(f + 1, e + 1)], axis=0)
                gains[f] = -dot(block, stack, 0)
            left = [spread * level_ref[levels - f] for f in range(1, e + 1)] + [leaf_ref[...]]
            right = [gains[f] for f in range(1, e + 1)] + [gains[0]]
            out_ref[:, (e - head) * rank : (e - head + 1) * rank] = dot(
                jnp.concatenate(left, axis=1), jnp.concatenate(right, axis=0)
            )

    (response,) = call(
        response_body,
        [(rows_here, (count - head) * rank)],
        scale,
        leaf_basis,
        level_basis,
        *cores[1:],
        *factors,
        name="response",
        flops=small * (count - head) * count * rows_here // rank,
    )

    flat = [part for parts in moments for part in parts]
    sizes = [len(parts) // 2 for parts in moments]

    def last_body(base_ref, response_ref, *refs):
        part_refs, out_ref = refs[:-1], refs[-1]
        stack, at = [], 0
        for size in sizes:
            own = add_all([part[...] for part in part_refs[at : at + size]])
            other = add_all([part[...] for part in part_refs[at + size : at + 2 * size]])
            stack.append(join(own, other, 1))
            at += 2 * size
        out_ref[...] = base_ref[...] - dot(response_ref[...], jnp.concatenate(stack, axis=0))

    (out,) = call(
        last_body,
        [(rows_here, columns)],
        base,
        response,
        *flat,
        name="last",
        flops=small * 2 * (count - head) * rows_here // rank,
    )
    return out


def solution(mesh):
    in_specs = (
        P(("rows", "sub"), None),
        P(("rows", "sub")),
        P(("rows", "sub"), None),
        P("rows", None, None),
        P(None, ("rows", "sub"), None),
        P(),
    )
    out_specs = P(("rows", "sub"), None)
    return jax.shard_map(shards, mesh=mesh, in_specs=in_specs, out_specs=out_specs, check_vma=False)
```

```python
import functools

import jax
import jax.numpy as jnp
from jax import lax
from jax.experimental import pallas as pl
from jax.experimental.pallas import tpu as pltpu
from jax.sharding import PartitionSpec as P


FLOAT = jnp.float32
VMEM_LIMIT = 16 << 20


def halves(value):
    high = value.astype(jnp.bfloat16)
    return high, (value - high.astype(FLOAT)).astype(jnp.bfloat16)


def dot_parts(left, right, right_dim=0):
    mult = functools.partial(
        lax.dot_general,
        dimension_numbers=(((1,), (right_dim,)), ((), ())),
        preferred_element_type=FLOAT,
    )
    return mult(left[0], right[0]) + (mult(left[0], right[1]) + mult(left[1], right[0]))


def dot(left, right, right_dim=0):
    return dot_parts(halves(left), halves(right), right_dim)


def lanes(values):
    return values[0] if len(values) == 1 else jnp.concatenate(values, axis=1)


def column_scale(scale):
    size = scale.shape[1]
    return jnp.concatenate(
        [jnp.broadcast_to(scale[i : i + 1, :], (size, size)).T for i in range(scale.shape[0])], axis=0
    )


def core_side():
    return lax.rem(lax.axis_index("sub"), 2)


def own_block():
    place, value = lax.axis_index("sub"), 0
    for _ in range(lax.axis_size("sub").bit_length() - 1):
        value = value * 2 + lax.rem(place, 2)
        place = place // 2
    return value


def at(index, size):
    return pl.ds(pl.multiple_of(index * size, 8), size)


def call(body, out_shapes, *operands, name, flops, spaces=None, scratch=()):
    spaces = spaces or [pltpu.VMEM] * len(operands)
    size = sum(4 * a.size for a in operands)
    outs = [jax.ShapeDtypeStruct(shape, FLOAT) for shape in out_shapes]
    return pl.pallas_call(
        body,
        out_shape=outs,
        in_specs=[pl.BlockSpec(memory_space=space) for space in spaces],
        out_specs=[pl.BlockSpec(memory_space=pltpu.VMEM)] * len(outs),
        scratch_shapes=list(scratch),
        name=name,
        compiler_params=pltpu.CompilerParams(vmem_limit_bytes=VMEM_LIMIT),
        cost_estimate=pl.CostEstimate(flops=flops, bytes_accessed=size, transcendentals=0),
    )(*operands)


def swap(array, axis, bit):
    return lax.ppermute(array, axis, [(i, i ^ 1 << bit) for i in range(lax.axis_size(axis))])


def partial_sums(array, axis, bits):
    bits = list(bits)
    if not bits:
        return [array]
    for bit in bits[:-1]:
        array = array + swap(array, axis, bit)
    return [array, swap(array, axis, bits[-1])]


def add_all(parts):
    return functools.reduce(lambda a, b: a + b, parts)


def shards(queries, row_scale, leaf_basis, leaf_cores, level_basis, level_cores):
    levels = level_basis.shape[0]
    count = levels + 1
    top = levels
    rows_here, rank = leaf_basis.shape
    columns = queries.shape[1]
    groups, sub = lax.axis_size("rows"), lax.axis_size("sub")
    heights = [None] + [levels + 1 - e for e in range(1, count)]
    widths = [1] + [groups // 2 ** heights[e] for e in range(1, count)]
    head = sum(w == 1 for w in widths)
    bits = [range(0)] + [
        range(widths[e - 1].bit_length() - 1, widths[e].bit_length() - 1) for e in range(1, count)
    ]
    blocks = [list(range(e + 1 if e < head else e, count)) for e in range(count)]
    sub_bits = sub.bit_length() - 1
    leaf_bits = range(1, sub_bits)
    mine = columns // sub
    half = rank // 2
    small = 2 * 3 * rank**3

    scale = row_scale.reshape(-1, rank)
    index = lax.axis_index("rows")
    cores = [leaf_cores[0]] + [
        lax.dynamic_index_in_dim(level_cores, 2 ** heights[e] - 2 + index // widths[e], 0, keepdims=False)
        for e in range(1, count)
    ]
    starts = [sum(len(b) for b in blocks[:e]) * rank for e in range(count + 1)]

    def gram_body(scale_hbm, leaf_hbm, level_hbm, out_ref, scale_ref, leaf_ref, level_ref, sems):
        copies = [
            pltpu.make_async_copy(scale_hbm, scale_ref, sems.at[0]),
            pltpu.make_async_copy(leaf_hbm, leaf_ref, sems.at[1]),
        ]
        copies += [
            pltpu.make_async_copy(level_hbm.at[e], level_ref.at[e], sems.at[2 + e]) for e in range(levels)
        ]
        for copy in copies:
            copy.start()
        for copy in copies:
            copy.wait()
        vectors = [column_scale(scale_ref[...]) * leaf_ref[...]]
        vectors += [level_ref[levels - e] for e in range(1, count)]
        parts = [halves(v) for v in vectors]
        side = core_side()
        for e in range(count):
            right = [lanes([parts[f][i] for f in blocks[e]]) for i in range(2)]
            value = dot_parts(halves(vectors[e].T), right)
            for h in range(2):
                out_ref[at(h ^ side, half), starts[e] : starts[e + 1]] = value[h * half : (h + 1) * half]

    (gram,) = call(
        gram_body,
        [(rank, starts[count])],
        scale,
        leaf_basis,
        level_basis,
        name="gram",
        flops=small * sum(map(len, blocks)) * rows_here // rank,
        spaces=[pltpu.HBM] * 3,
        scratch=[
            pltpu.VMEM(scale.shape, FLOAT),
            pltpu.VMEM(leaf_basis.shape, FLOAT),
            pltpu.VMEM(level_basis.shape, FLOAT),
            pltpu.SemaphoreType.DMA((2 + levels,)),
        ],
    )
    gram_chip = gram[:half] + swap(gram[half:], "sub", 0)
    gram_leaf = add_all(partial_sums(gram_chip, "sub", leaf_bits))

    def moment_body(scale_ref, queries_ref, leaf_ref, level_ref, out_ref):
        spread = column_scale(scale_ref[...])
        right = lanes([leaf_ref[...]] + [spread * level_ref[levels - e] for e in range(1, count)])
        value = dot(queries_ref[...].T, right)
        own = own_block()
        for i in range(sub):
            out_ref[at(i ^ own, mine), :] = value[i * mine : (i + 1) * mine]

    (value,) = call(
        moment_body,
        [(columns, count * rank)],
        scale,
        queries,
        leaf_basis,
        level_basis,
        name="moment",
        flops=small * count * 2 * rows_here // rank,
    )
    size = columns
    for bit in range(sub_bits):
        size //= 2
        moment_parts = [value[:size], swap(value[size:], "sub", bit)]
        value = add_all(moment_parts)

    late_rows = columns // 2 + head * half

    def late_body(scale_ref, queries_ref, leaf_ref, level_ref, out_ref):
        spread = column_scale(scale_ref[...])
        vectors = spread * leaf_ref[...]
        side = core_side()
        value = dot(queries_ref[...].T, spread * vectors)
        for h in range(2):
            base = (h ^ side) * late_rows
            part = value[h * columns // 2 : (h + 1) * columns // 2]
            out_ref[pl.ds(pl.multiple_of(base, 8), columns // 2), :] = part
        for e in range(head):
            basis = vectors if e == 0 else level_ref[levels - e]
            value = dot(basis.T, basis)
            for h in range(2):
                base = (h ^ side) * late_rows + columns // 2 + e * half
                out_ref[pl.ds(pl.multiple_of(base, 8), half), :] = value[h * half : (h + 1) * half]

    (late,) = call(
        late_body,
        [(2 * late_rows, rank)],
        scale,
        queries,
        leaf_basis,
        level_basis,
        name="late",
        flops=small * (2 + head) * rows_here // rank,
    )
    late_keep, late_got = late[:late_rows], swap(late[late_rows:], "sub", 0)

    def product_body(group, own_ref, other_ref, *refs):
        core_refs, out_refs, stack_ref = refs[: len(group)], refs[len(group) : -1], refs[-1]
        side = core_side()
        stack_ref[at(side, half), :] = own_ref[...]
        stack_ref[at(1 - side, half), :] = other_ref[...]
        base = starts[group[0]]
        for place, e in enumerate(group):
            out_refs[place][...] = dot(
                core_refs[place][...].T, stack_ref[:, starts[e] - base : starts[e + 1] - base]
            )

    def products(group, own):
        return call(
            functools.partial(product_body, group),
            [(rank, starts[e + 1] - starts[e]) for e in group],
            own,
            swap(own, "sub", 0),
            *[cores[e] for e in group],
            name=f"product{group[0]}",
            flops=small * sum(len(blocks[e]) for e in group),
            scratch=[pltpu.VMEM((rank, own.shape[1]), FLOAT)],
        )

    factors = products(list(range(head)), gram_leaf[:, : starts[head]])
    remaining = gram_leaf[:, starts[head] :]
    for e in range(head, count):
        remaining = add_all(partial_sums(remaining, "rows", bits[e]))
        size = starts[e + 1] - starts[e]
        factors += products([e], remaining[:, :size])
        remaining = remaining[:, size:]

    def head_body(*refs):
        part_refs, factor_refs = refs[: len(moment_parts)], refs[len(moment_parts) : -5]
        keep_ref, got_ref, own_ref, rest_ref, late_ref = refs[-5:]
        rest = add_all([part[...] for part in part_refs])
        for e in range(head):
            own, rest = rest[:, :rank], rest[:, rank:]
            own_ref[:, e * rank : (e + 1) * rank] = own
            rest = rest - dot(own, factor_refs[e][...])
        rest_ref[...] = rest
        late_ref[...] = keep_ref[...] + got_ref[...]

    head_moments, rest, late_chip = call(
        head_body,
        [(mine, head * rank), (mine, (count - head) * rank), (late_rows, rank)],
        *moment_parts,
        *factors[:head],
        late_keep,
        late_got,
        name="head",
        flops=small * sum(map(len, blocks[:head])),
    )

    def step_body(number, *refs):
        part_refs, factor_ref, own_ref, rest_ref = refs[:number], refs[number], refs[-2], refs[-1]
        total = add_all([part[...] for part in part_refs])
        own_ref[...] = total[:, :rank]
        rest_ref[...] = total[:, rank:] - dot(total[:, :rank], factor_ref[:, rank:])

    def gather(own):
        for bit in reversed(range(1, sub_bits)):
            own = jnp.concatenate([own, swap(own, "sub", bit)], axis=0)
        return [own, swap(own, "sub", 0)]

    def scatter(parts, stack_ref, where):
        own, slot = own_block(), 0
        for part in parts:
            for i in range(part.shape[0] // mine):
                stack_ref[at(slot ^ own, mine), where] = part[i * mine : (i + 1) * mine, :]
                slot += 1

    late_leaf = add_all(partial_sums(late_chip, "sub", leaf_bits))
    late_other = swap(late_leaf, "sub", 0)
    head_parts = gather(head_moments)

    coarse_parts = []
    for e in range(head, top):
        parts = partial_sums(rest, "rows", bits[e])
        own, rest = call(
            functools.partial(step_body, len(parts)),
            [(mine, rank), (mine, (top - e) * rank)],
            *parts,
            factors[e],
            name=f"step{e}",
            flops=small * (top - e),
        )
        coarse_parts.append(gather(own))
    coarse_parts.append(gather(add_all(partial_sums(rest, "rows", bits[top]))))

    def response(e, spread, leaf_ref, level_ref, core_refs, factor_refs, diagonal):
        core = core_refs[e][...]
        if e == 0:
            right = [core, -dot(diagonal, core)]
            left = [spread * (spread * leaf_ref[...]), leaf_ref[...]]
        else:
            gains = {e: core + core.T - dot(diagonal, core)}
            for f in reversed(range(e)):
                start = (0 if f < head else 1) * rank
                stack = jnp.concatenate([gains[g] for g in range(f + 1, e + 1)], axis=0)
                gains[f] = -dot(factor_refs[f][:, start : start + (e - f) * rank], stack)
            left = [spread * level_ref[levels - f] for f in range(1, e + 1)] + [leaf_ref[...]]
            right = [gains[f] for f in range(1, e + 1)] + [gains[0]]
        return dot(lanes(left), jnp.concatenate(right, axis=0))

    def coarse_body(scale_ref, leaf_ref, level_ref, *refs):
        core_refs, factor_refs, out_ref = refs[:count], refs[count:-1], refs[-1]
        spread = column_scale(scale_ref[...])
        for e in range(head, count):
            out_ref[:, (e - head) * rank : (e - head + 1) * rank] = response(
                e, spread, leaf_ref, level_ref, core_refs, factor_refs, factor_refs[e][:, :rank]
            )

    (coarse,) = call(
        coarse_body,
        [(rows_here, (count - head) * rank)],
        scale,
        leaf_basis,
        level_basis,
        *cores,
        *factors,
        name="coarse",
        flops=small * (count - head) * count * rows_here // rank,
    )

    def base_body(scale_ref, queries_ref, leaf_ref, level_ref, own_ref, other_ref, *refs):
        core_refs, factor_refs = refs[:head], refs[head : 2 * head]
        part_refs, out_ref, stack_ref, gram_ref = refs[2 * head : -3], refs[-3], refs[-2], refs[-1]
        spread = column_scale(scale_ref[...])
        scatter(part_refs, stack_ref, pl.ds(0, head * rank))
        side = core_side()
        for late_ref, place in ((own_ref, side), (other_ref, 1 - side)):
            stack_ref[at(place, columns // 2), head * rank :] = late_ref[: columns // 2]
            for e in range(head):
                start = columns // 2 + e * half
                gram_ref[at(place, half), e * rank : (e + 1) * rank] = late_ref[start : start + half]
        left = []
        for e in range(head):
            diagonal = dot(core_refs[e][...].T, gram_ref[:, e * rank : (e + 1) * rank])
            left.append(response(e, spread, leaf_ref, level_ref, core_refs, factor_refs, diagonal))
        left.append(dot(leaf_ref[...], core_refs[0][...].T))
        square = spread * spread
        out_ref[...] = lanes([square] * (columns // rank)) * queries_ref[...] - dot(
            lanes(left), stack_ref[...], 1
        )

    (base,) = call(
        base_body,
        [(rows_here, columns)],
        scale,
        queries,
        leaf_basis,
        level_basis,
        late_leaf,
        late_other,
        *cores[:head],
        *factors[:head],
        *head_parts,
        name="base",
        flops=small * 2 * (head + 1) * rows_here // rank,
        scratch=[pltpu.VMEM((columns, (head + 1) * rank), FLOAT), pltpu.VMEM((rank, head * rank), FLOAT)],
    )

    def last_body(base_ref, coarse_ref, *refs):
        part_refs, out_ref, stack_ref = refs[:-2], refs[-2], refs[-1]
        at_part = 0
        for e, parts in enumerate(coarse_parts):
            scatter(part_refs[at_part : at_part + len(parts)], stack_ref, pl.ds(e * rank, rank))
            at_part += len(parts)
        out_ref[...] = base_ref[...] - dot(coarse_ref[...], stack_ref[...], 1)

    (out,) = call(
        last_body,
        [(rows_here, columns)],
        base,
        coarse,
        *[part for parts in coarse_parts for part in parts],
        name="last",
        flops=small * 2 * (count - head) * rows_here // rank,
        scratch=[pltpu.VMEM((columns, (count - head) * rank), FLOAT)],
    )
    return out


def solution(mesh):
    in_specs = (
        P(("rows", "sub"), None),
        P(("rows", "sub")),
        P(("rows", "sub"), None),
        P("rows", None, None),
        P(None, ("rows", "sub"), None),
        P(),
    )
    out_specs = P(("rows", "sub"), None)
    return jax.shard_map(shards, mesh=mesh, in_specs=in_specs, out_specs=out_specs, check_vma=False)
```

```python
import functools

import jax
import jax.numpy as jnp
from jax import lax
from jax.experimental import pallas as pl
from jax.experimental.pallas import tpu as pltpu
from jax.sharding import PartitionSpec as P


FLOAT = jnp.float32
VMEM_LIMIT = 16 << 20


def halves(value):
    high = value.astype(jnp.bfloat16)
    return high, (value - high.astype(FLOAT)).astype(jnp.bfloat16)


def dot_parts(left, right, right_dim=0):
    mult = functools.partial(
        lax.dot_general,
        dimension_numbers=(((1,), (right_dim,)), ((), ())),
        preferred_element_type=FLOAT,
    )
    return mult(left[0], right[0]) + (mult(left[0], right[1]) + mult(left[1], right[0]))


def dot(left, right, right_dim=0):
    return dot_parts(halves(left), halves(right), right_dim)


def lanes(values):
    return values[0] if len(values) == 1 else jnp.concatenate(values, axis=1)


def column_scale(scale):
    size = scale.shape[1]
    return jnp.concatenate(
        [jnp.broadcast_to(scale[i : i + 1, :], (size, size)).T for i in range(scale.shape[0])], axis=0
    )


def core_side():
    return lax.rem(lax.axis_index("sub"), 2)


def own_block():
    place, value = lax.axis_index("sub"), 0
    for _ in range(lax.axis_size("sub").bit_length() - 1):
        value = value * 2 + lax.rem(place, 2)
        place = place // 2
    return value


def at(index, size):
    return pl.ds(pl.multiple_of(index * size, 8), size)


def call(body, out_shapes, *operands, flops, spaces=None, scratch=()):
    spaces = spaces or [pltpu.VMEM] * len(operands)
    size = sum(4 * a.size for a in operands)
    outs = [jax.ShapeDtypeStruct(shape, FLOAT) for shape in out_shapes]
    return pl.pallas_call(
        body,
        out_shape=outs,
        in_specs=[pl.BlockSpec(memory_space=space) for space in spaces],
        out_specs=[pl.BlockSpec(memory_space=pltpu.VMEM)] * len(outs),
        scratch_shapes=list(scratch),
        compiler_params=pltpu.CompilerParams(vmem_limit_bytes=VMEM_LIMIT),
        cost_estimate=pl.CostEstimate(flops=flops, bytes_accessed=size, transcendentals=0),
    )(*operands)


def swap(array, axis, bit):
    return lax.ppermute(array, axis, [(i, i ^ 1 << bit) for i in range(lax.axis_size(axis))])


def swap_both(array, row_bit, sub_bit):
    sub = lax.axis_size("sub")
    mask = (1 << row_bit) * sub + (1 << sub_bit)
    pairs = [(i, i ^ mask) for i in range(lax.axis_size("rows") * sub)]
    return lax.ppermute(array, ("rows", "sub"), pairs)


def partial_sums(array, axis, bits):
    bits = list(bits)
    if not bits:
        return [array]
    for bit in bits[:-1]:
        array = array + swap(array, axis, bit)
    return [array, swap(array, axis, bits[-1])]


def add_all(parts):
    return functools.reduce(lambda a, b: a + b, parts)


def shards(queries, row_scale, leaf_basis, leaf_cores, level_basis, level_cores):
    levels = level_basis.shape[0]
    count = levels + 1
    top = levels
    rows_here, rank = leaf_basis.shape
    columns = queries.shape[1]
    groups, sub = lax.axis_size("rows"), lax.axis_size("sub")
    heights = [None] + [levels + 1 - e for e in range(1, count)]
    widths = [1] + [groups // 2 ** heights[e] for e in range(1, count)]
    head = sum(w == 1 for w in widths)
    bits = [range(0)] + [
        range(widths[e - 1].bit_length() - 1, widths[e].bit_length() - 1) for e in range(1, count)
    ]
    blocks = [list(range(e + 1 if e < head else e, count)) for e in range(count)]
    sub_bits = sub.bit_length() - 1
    leaf_bits = range(1, sub_bits)
    mine = columns // sub
    half = rank // 2
    small = 2 * 3 * rank**3

    scale = row_scale.reshape(-1, rank)
    index = lax.axis_index("rows")
    cores = [leaf_cores[0]] + [
        lax.dynamic_index_in_dim(level_cores, 2 ** heights[e] - 2 + index // widths[e], 0, keepdims=False)
        for e in range(1, count)
    ]
    starts = [sum(len(b) for b in blocks[:e]) * rank for e in range(count + 1)]

    def gram_body(scale_hbm, leaf_hbm, level_hbm, out_ref, scale_ref, leaf_ref, level_ref, sems):
        copies = [
            pltpu.make_async_copy(scale_hbm, scale_ref, sems.at[0]),
            pltpu.make_async_copy(leaf_hbm, leaf_ref, sems.at[1]),
        ]
        copies += [
            pltpu.make_async_copy(level_hbm.at[e], level_ref.at[e], sems.at[2 + e]) for e in range(levels)
        ]
        for copy in copies:
            copy.start()
        for copy in copies:
            copy.wait()
        vectors = [column_scale(scale_ref[...]) * leaf_ref[...]]
        vectors += [level_ref[levels - e] for e in range(1, count)]
        parts = [halves(v) for v in vectors]
        side = core_side()
        for e in range(count):
            right = [lanes([parts[f][i] for f in blocks[e]]) for i in range(2)]
            value = dot_parts(halves(vectors[e].T), right)
            for h in range(2):
                out_ref[at(h ^ side, half), starts[e] : starts[e + 1]] = value[h * half : (h + 1) * half]

    (gram,) = call(
        gram_body,
        [(rank, starts[count])],
        scale,
        leaf_basis,
        level_basis,
        flops=small * sum(map(len, blocks)) * rows_here // rank,
        spaces=[pltpu.HBM] * 3,
        scratch=[
            pltpu.VMEM(scale.shape, FLOAT),
            pltpu.VMEM(leaf_basis.shape, FLOAT),
            pltpu.VMEM(level_basis.shape, FLOAT),
            pltpu.SemaphoreType.DMA((2 + levels,)),
        ],
    )
    gram_chip = gram[:half] + swap(gram[half:], "sub", 0)
    tail_leaf = add_all(partial_sums(gram_chip[:, starts[head] :], "sub", leaf_bits))
    head_leaf = add_all(partial_sums(gram_chip[:, : starts[head]], "sub", leaf_bits))

    def moment_body(scale_ref, queries_ref, leaf_ref, level_ref, out_ref):
        spread = column_scale(scale_ref[...])
        right = lanes([leaf_ref[...]] + [spread * level_ref[levels - e] for e in range(1, count)])
        value = dot(queries_ref[...].T, right)
        own = own_block()
        for i in range(sub):
            out_ref[at(i ^ own, mine), :] = value[i * mine : (i + 1) * mine]

    (value,) = call(
        moment_body,
        [(columns, count * rank)],
        scale,
        queries,
        leaf_basis,
        level_basis,
        flops=small * count * 2 * rows_here // rank,
    )
    size = columns
    for bit in range(sub_bits):
        size //= 2
        moment_parts = [value[:size], swap(value[size:], "sub", bit)]
        value = add_all(moment_parts)

    late_rows = columns // 2 + head * half

    def late_body(scale_ref, queries_ref, leaf_ref, level_ref, out_ref):
        spread = column_scale(scale_ref[...])
        vectors = spread * leaf_ref[...]
        side = core_side()
        value = dot(queries_ref[...].T, spread * vectors)
        for h in range(2):
            base = (h ^ side) * late_rows
            part = value[h * columns // 2 : (h + 1) * columns // 2]
            out_ref[pl.ds(pl.multiple_of(base, 8), columns // 2), :] = part
        for e in range(head):
            basis = vectors if e == 0 else level_ref[levels - e]
            value = dot(basis.T, basis)
            for h in range(2):
                base = (h ^ side) * late_rows + columns // 2 + e * half
                out_ref[pl.ds(pl.multiple_of(base, 8), half), :] = value[h * half : (h + 1) * half]

    (late,) = call(
        late_body,
        [(2 * late_rows, rank)],
        scale,
        queries,
        leaf_basis,
        level_basis,
        flops=small * (2 + head) * rows_here // rank,
    )
    late_keep, late_got = late[:late_rows], swap(late[late_rows:], "sub", 0)

    def product_body(group, own_ref, other_ref, *refs):
        core_refs, out_refs, stack_ref = refs[: len(group)], refs[len(group) : -1], refs[-1]
        side = core_side()
        stack_ref[at(side, half), :] = own_ref[...]
        stack_ref[at(1 - side, half), :] = other_ref[...]
        base = starts[group[0]]
        for place, e in enumerate(group):
            out_refs[place][...] = dot(
                core_refs[place][...].T, stack_ref[:, starts[e] - base : starts[e + 1] - base]
            )

    def products(group, own):
        return call(
            functools.partial(product_body, group),
            [(rank, starts[e + 1] - starts[e]) for e in group],
            own,
            swap(own, "sub", 0),
            *[cores[e] for e in group],
            flops=small * sum(len(blocks[e]) for e in group),
            scratch=[pltpu.VMEM((rank, own.shape[1]), FLOAT)],
        )

    factors = products(list(range(head)), head_leaf)
    remaining, sums = tail_leaf, []
    for e in range(head, count):
        remaining = add_all(partial_sums(remaining, "rows", bits[e]))
        size = starts[e + 1] - starts[e]
        sums.append(remaining[:, :size])
        remaining = remaining[:, size:]
    factors += products(list(range(head, count)), lanes(sums))

    def head_body(*refs):
        part_refs, factor_refs = refs[: len(moment_parts)], refs[len(moment_parts) : -4]
        keep_ref, got_ref, rest_ref, late_ref = refs[-4:]
        rest = add_all([part[...] for part in part_refs])
        for e in range(head):
            own, rest = rest[:, :rank], rest[:, rank:]
            late_ref[late_rows + e * mine : late_rows + (e + 1) * mine, :] = own
            rest = rest - dot(own, factor_refs[e][...])
        rest_ref[...] = rest
        late_ref[:late_rows] = keep_ref[...] + got_ref[...]

    rest, late = call(
        head_body,
        [(mine, (count - head) * rank), (late_rows + head * mine, rank)],
        *moment_parts,
        *factors[:head],
        late_keep,
        late_got,
        flops=small * sum(map(len, blocks[:head])),
    )

    def step_body(number, *refs):
        part_refs, factor_ref, own_ref, rest_ref = refs[:number], refs[number], refs[-2], refs[-1]
        total = add_all([part[...] for part in part_refs])
        own_ref[...] = total[:, :rank]
        rest_ref[...] = total[:, rank:] - dot(total[:, :rank], factor_ref[:, rank:])

    def scatter(parts, number, stack_ref):
        own, slot = own_block(), 0
        for part in parts:
            for i in range(part.shape[0] // (number * mine)):
                for e in range(number):
                    start = (i * number + e) * mine
                    stack_ref[at(slot ^ own, mine), e * rank : (e + 1) * rank] = part[start : start + mine, :]
                slot += 1

    for bit in reversed(leaf_bits):
        got = swap(late, "sub", bit)
        late = jnp.concatenate([late[:late_rows] + got[:late_rows], late[late_rows:], got[late_rows:]], axis=0)
    late_parts = [late, swap(late, "sub", 0)]

    coarse = []
    for e in range(head, top):
        parts = partial_sums(rest, "rows", bits[e])
        own, rest = call(
            functools.partial(step_body, len(parts)),
            [(mine, rank), (mine, (top - e) * rank)],
            *parts,
            factors[e],
            flops=small * (top - e),
        )
        coarse.append(own)
    coarse.append(rest)
    if len(bits[top]) == 1 and len(leaf_bits) == 1:
        row_bit, sub_bit = bits[top][0], leaf_bits[0]
        across = swap(rest, "rows", row_bit)
        beside = swap(jnp.concatenate(coarse, axis=0), "sub", sub_bit)
        corner = swap_both(rest, row_bit, sub_bit)
        end = (count - head - 1) * mine
        coarse = jnp.concatenate([*coarse[:-1], rest + across, beside[:end], beside[end:] + corner], axis=0)
    else:
        coarse[-1] = add_all(partial_sums(rest, "rows", bits[top]))
        coarse = jnp.concatenate(coarse, axis=0)
        for bit in reversed(leaf_bits):
            coarse = jnp.concatenate([coarse, swap(coarse, "sub", bit)], axis=0)
    coarse_parts = [coarse, swap(coarse, "sub", 0)]

    def response(e, spread, leaf_ref, level_ref, core_refs, factor_refs, diagonal):
        core = core_refs[e][...]
        if e == 0:
            right = [core, -dot(diagonal, core)]
            left = [spread * (spread * leaf_ref[...]), leaf_ref[...]]
        else:
            gains = {e: core + core.T - dot(diagonal, core)}
            for f in reversed(range(e)):
                start = (0 if f < head else 1) * rank
                stack = jnp.concatenate([gains[g] for g in range(f + 1, e + 1)], axis=0)
                gains[f] = -dot(factor_refs[f][:, start : start + (e - f) * rank], stack)
            left = [spread * level_ref[levels - f] for f in range(1, e + 1)] + [leaf_ref[...]]
            right = [gains[f] for f in range(1, e + 1)] + [gains[0]]
        return dot(lanes(left), jnp.concatenate(right, axis=0))

    def answer_body(scale_ref, leaf_ref, level_ref, *refs):
        core_refs, factor_refs, out_ref = refs[:count], refs[count:-1], refs[-1]
        spread = column_scale(scale_ref[...])
        for e in range(head, count):
            out_ref[:, (e - head) * rank : (e - head + 1) * rank] = response(
                e, spread, leaf_ref, level_ref, core_refs, factor_refs, factor_refs[e][:, :rank]
            )

    (answer,) = call(
        answer_body,
        [(rows_here, (count - head) * rank)],
        scale,
        leaf_basis,
        level_basis,
        *cores,
        *factors,
        flops=small * (count - head) * count * rows_here // rank,
    )

    def base_body(scale_ref, queries_ref, leaf_ref, level_ref, own_ref, other_ref, *refs):
        core_refs, factor_refs = refs[:head], refs[head : 2 * head]
        out_ref, stack_ref, gram_ref = refs[2 * head :]
        spread = column_scale(scale_ref[...])
        scatter([own_ref.at[late_rows:], other_ref.at[late_rows:]], head, stack_ref)
        side = core_side()
        for late_ref, place in ((own_ref, side), (other_ref, 1 - side)):
            stack_ref[at(place, columns // 2), head * rank :] = late_ref[: columns // 2]
            for e in range(head):
                start = columns // 2 + e * half
                gram_ref[at(place, half), e * rank : (e + 1) * rank] = late_ref[start : start + half]
        left = []
        for e in range(head):
            diagonal = dot(core_refs[e][...].T, gram_ref[:, e * rank : (e + 1) * rank])
            left.append(response(e, spread, leaf_ref, level_ref, core_refs, factor_refs, diagonal))
        left.append(dot(leaf_ref[...], core_refs[0][...].T))
        square = spread * spread
        out_ref[...] = lanes([square] * (columns // rank)) * queries_ref[...] - dot(
            lanes(left), stack_ref[...], 1
        )

    (base,) = call(
        base_body,
        [(rows_here, columns)],
        scale,
        queries,
        leaf_basis,
        level_basis,
        *late_parts,
        *cores[:head],
        *factors[:head],
        flops=small * 2 * (head + 1) * rows_here // rank,
        scratch=[pltpu.VMEM((columns, (head + 1) * rank), FLOAT), pltpu.VMEM((rank, head * rank), FLOAT)],
    )

    def last_body(base_ref, answer_ref, own_ref, other_ref, out_ref, stack_ref):
        scatter([own_ref, other_ref], count - head, stack_ref)
        out_ref[...] = base_ref[...] - dot(answer_ref[...], stack_ref[...], 1)

    (out,) = call(
        last_body,
        [(rows_here, columns)],
        base,
        answer,
        *coarse_parts,
        flops=small * 2 * (count - head) * rows_here // rank,
        scratch=[pltpu.VMEM((columns, (count - head) * rank), FLOAT)],
    )
    return out


def solution(mesh):
    in_specs = (
        P(("rows", "sub"), None),
        P(("rows", "sub")),
        P(("rows", "sub"), None),
        P("rows", None, None),
        P(None, ("rows", "sub"), None),
        P(),
    )
    out_specs = P(("rows", "sub"), None)

    return jax.shard_map(shards, mesh=mesh, in_specs=in_specs, out_specs=out_specs, check_vma=False)
```

```python
import functools

import jax
import jax.numpy as jnp
from jax import lax
from jax.experimental import pallas as pl
from jax.experimental.pallas import tpu as pltpu
from jax.sharding import PartitionSpec as P


FLOAT = jnp.float32
VMEM_LIMIT = 16 << 20


def halves(value):
    high = value.astype(jnp.bfloat16)
    return high, (value - high.astype(FLOAT)).astype(jnp.bfloat16)


def dot_parts(left, right, right_dim=0):
    mult = functools.partial(
        lax.dot_general,
        dimension_numbers=(((1,), (right_dim,)), ((), ())),
        preferred_element_type=FLOAT,
    )
    return mult(left[0], right[0]) + (mult(left[0], right[1]) + mult(left[1], right[0]))


def dot(left, right, right_dim=0):
    return dot_parts(halves(left), halves(right), right_dim)


def lanes(values):
    return values[0] if len(values) == 1 else jnp.concatenate(values, axis=1)


def column_scale(scale):
    size = scale.shape[1]
    return jnp.concatenate(
        [jnp.broadcast_to(scale[i : i + 1, :], (size, size)).T for i in range(scale.shape[0])], axis=0
    )


def core_side():
    return lax.rem(lax.axis_index("sub"), 2)


def own_block():
    place, value = lax.axis_index("sub"), 0
    for _ in range(lax.axis_size("sub").bit_length() - 1):
        value = value * 2 + lax.rem(place, 2)
        place = place // 2
    return value


def at(index, size):
    return pl.ds(pl.multiple_of(index * size, 8), size)


def call(body, outs, *operands, flops, spaces=None, out_space=pltpu.VMEM, scratch=()):
    spaces = spaces or [pltpu.VMEM] * len(operands)
    size = sum(a.dtype.itemsize * a.size for a in operands)
    outs = [out if isinstance(out, jax.ShapeDtypeStruct) else jax.ShapeDtypeStruct(out, FLOAT) for out in outs]
    return pl.pallas_call(
        body,
        out_shape=outs,
        in_specs=[pl.BlockSpec(memory_space=space) for space in spaces],
        out_specs=[pl.BlockSpec(memory_space=out_space)] * len(outs),
        scratch_shapes=list(scratch),
        compiler_params=pltpu.CompilerParams(vmem_limit_bytes=VMEM_LIMIT),
        cost_estimate=pl.CostEstimate(flops=flops, bytes_accessed=size, transcendentals=0),
    )(*operands)


def pair(*shape):
    return [jax.ShapeDtypeStruct(shape, jnp.bfloat16)] * 2


def store(refs, value):
    for ref, part in zip(refs, halves(value)):
        ref[...] = part


def swap(array, axis, bit):
    return lax.ppermute(array, axis, [(i, i ^ 1 << bit) for i in range(lax.axis_size(axis))])


def swap_both(array, row_bit, sub_bit):
    sub = lax.axis_size("sub")
    mask = (1 << row_bit) * sub + (1 << sub_bit)
    pairs = [(i, i ^ mask) for i in range(lax.axis_size("rows") * sub)]
    return lax.ppermute(array, ("rows", "sub"), pairs)


def partial_sums(array, axis, bits):
    bits = list(bits)
    if not bits:
        return [array]
    for bit in bits[:-1]:
        array = array + swap(array, axis, bit)
    return [array, swap(array, axis, bits[-1])]


def add_all(parts):
    return functools.reduce(lambda a, b: a + b, parts)


def shards(queries, row_scale, leaf_basis, leaf_cores, level_basis, level_cores):
    levels = level_basis.shape[0]
    count = levels + 1
    top = levels
    rows_here, rank = leaf_basis.shape
    columns = queries.shape[1]
    groups, sub = lax.axis_size("rows"), lax.axis_size("sub")
    heights = [None] + [levels + 1 - e for e in range(1, count)]
    widths = [1] + [groups // 2 ** heights[e] for e in range(1, count)]
    head = sum(w == 1 for w in widths)
    bits = [range(0)] + [
        range(widths[e - 1].bit_length() - 1, widths[e].bit_length() - 1) for e in range(1, count)
    ]
    blocks = [list(range(e + 1 if e < head else e, count)) for e in range(count)]
    sub_bits = sub.bit_length() - 1
    leaf_bits = range(1, sub_bits)
    mine = columns // sub
    half = rank // 2
    small = 2 * 3 * rank**3

    scale = row_scale.reshape(-1, rank)
    starts = [sum(len(b) for b in blocks[:e]) * rank for e in range(count + 1)]

    def gram_body(*refs):
        sources, (out_ref, core_ref), (scale_ref, leaf_ref, level_ref, sems) = refs[:5], refs[5:7], refs[7:]
        scale_hbm, leaf_hbm, level_hbm, leaf_core_hbm, core_hbm = sources
        targets = [(scale_hbm, scale_ref), (leaf_hbm, leaf_ref)]
        targets += [(level_hbm.at[e], level_ref.at[e]) for e in reversed(range(levels))]
        place = lax.axis_index("rows")
        targets.append((leaf_core_hbm.at[0], core_ref.at[0]))
        for e in range(1, count):
            targets.append((core_hbm.at[2 ** heights[e] - 2 + place // widths[e]], core_ref.at[e]))
        copies = [pltpu.make_async_copy(a, b, sems.at[i]) for i, (a, b) in enumerate(targets)]
        for copy in copies:
            copy.start()
        for copy in copies[: 2 + levels]:
            copy.wait()
        vectors = [column_scale(scale_ref[...]) * leaf_ref[...]]
        vectors += [level_ref[levels - e] for e in range(1, count)]
        parts = [halves(v) for v in vectors]
        side = core_side()
        for e in range(count):
            right = [lanes([parts[f][i] for f in blocks[e]]) for i in range(2)]
            value = dot_parts(halves(vectors[e].T), right)
            for h in range(2):
                out_ref[at(h ^ side, half), starts[e] : starts[e + 1]] = value[h * half : (h + 1) * half]
        for copy in copies[2 + levels :]:
            copy.wait()

    gram, cores = call(
        gram_body,
        [(rank, starts[count]), (count, rank, rank)],
        *[
            pltpu.with_memory_space_constraint(array, pltpu.HBM)
            for array in (scale, leaf_basis, level_basis, leaf_cores, level_cores)
        ],
        flops=small * sum(map(len, blocks)) * rows_here // rank,
        spaces=[pltpu.HBM] * 5,
        scratch=[
            pltpu.VMEM(scale.shape, FLOAT),
            pltpu.VMEM(leaf_basis.shape, FLOAT),
            pltpu.VMEM(level_basis.shape, FLOAT),
            pltpu.SemaphoreType.DMA((2 + levels + count,)),
        ],
    )
    gram_chip = gram[:half] + swap(gram[half:], "sub", 0)
    tail_leaf = add_all(partial_sums(gram_chip[:, starts[head] :], "sub", leaf_bits))
    head_leaf = add_all(partial_sums(gram_chip[:, : starts[head]], "sub", leaf_bits))

    def moment_body(scale_ref, queries_ref, leaf_ref, level_ref, out_ref, *basis_refs):
        spread = column_scale(scale_ref[...])
        right = halves(lanes([leaf_ref[...]] + [spread * level_ref[levels - e] for e in range(1, count)]))
        for basis_ref, part in zip(basis_refs, right):
            basis_ref[...] = part
        value = dot_parts(halves(queries_ref[...].T), right)
        own = own_block()
        for i in range(sub):
            out_ref[at(i ^ own, mine), :] = value[i * mine : (i + 1) * mine]

    value, *basis = call(
        moment_body,
        [(columns, count * rank), *pair(rows_here, count * rank)],
        scale,
        queries,
        leaf_basis,
        level_basis,
        flops=small * count * 2 * rows_here // rank,
    )
    size = columns
    for bit in range(sub_bits):
        size //= 2
        moment_parts = [value[:size], swap(value[size:], "sub", bit)]
        value = add_all(moment_parts)

    late_rows = columns // 2 + head * half

    def late_body(scale_ref, queries_ref, leaf_ref, level_ref, out_ref, *scaled_refs):
        spread = column_scale(scale_ref[...])
        vectors = spread * leaf_ref[...]
        side = core_side()
        scaled = halves(spread * vectors)
        for scaled_ref, part in zip(scaled_refs, scaled):
            scaled_ref[...] = part
        value = dot_parts(halves(queries_ref[...].T), scaled)
        for h in range(2):
            base = (h ^ side) * late_rows
            part = value[h * columns // 2 : (h + 1) * columns // 2]
            out_ref[pl.ds(pl.multiple_of(base, 8), columns // 2), :] = part
        for e in range(head):
            basis = vectors if e == 0 else level_ref[levels - e]
            value = dot(basis.T, basis)
            for h in range(2):
                base = (h ^ side) * late_rows + columns // 2 + e * half
                out_ref[pl.ds(pl.multiple_of(base, 8), half), :] = value[h * half : (h + 1) * half]

    late, *scaled = call(
        late_body,
        [(2 * late_rows, rank), *pair(rows_here, rank)],
        scale,
        queries,
        leaf_basis,
        level_basis,
        flops=small * (2 + head) * rows_here // rank,
    )
    late_keep, late_got = late[:late_rows], swap(late[late_rows:], "sub", 0)

    def product_body(group, own_ref, other_ref, core_ref, *refs):
        out_refs, stack_ref = refs[:-1], refs[-1]
        side = core_side()
        stack_ref[at(side, half), :] = own_ref[...]
        stack_ref[at(1 - side, half), :] = other_ref[...]
        base = starts[group[0]]
        for i, e in enumerate(group):
            block = stack_ref[:, starts[e] - base : starts[e + 1] - base]
            store(out_refs[2 * i : 2 * i + 2], dot(core_ref[e].T, block))

    def products(group, own):
        out = call(
            functools.partial(product_body, group),
            [part for e in group for part in pair(rank, starts[e + 1] - starts[e])],
            own,
            swap(own, "sub", 0),
            cores,
            flops=small * sum(len(blocks[e]) for e in group),
            scratch=[pltpu.VMEM((rank, own.shape[1]), FLOAT)],
        )
        return [out[2 * i : 2 * i + 2] for i in range(len(group))]

    factors = products(list(range(head)), head_leaf)
    remaining = tail_leaf
    for e in range(head, count):
        remaining = add_all(partial_sums(remaining, "rows", bits[e]))
        size = starts[e + 1] - starts[e]
        factors += products([e], remaining[:, :size])
        remaining = remaining[:, size:]

    def flat(group):
        return [part for factor in group for part in factor]

    def paired(refs):
        return [refs[i : i + 2] for i in range(0, len(refs), 2)]

    def take(factor, start, size):
        return [ref[:, start : start + size] for ref in factor]

    def head_body(*refs):
        part_refs, factor_refs = refs[: len(moment_parts)], paired(refs[len(moment_parts) : -4])
        keep_ref, got_ref, rest_ref, late_ref = refs[-4:]
        rest = add_all([part[...] for part in part_refs])
        for e in range(head):
            own, rest = rest[:, :rank], rest[:, rank:]
            late_ref[late_rows + e * mine : late_rows + (e + 1) * mine, :] = own
            rest = rest - dot_parts(halves(own), take(factor_refs[e], 0, (count - 1 - e) * rank))
        rest_ref[...] = rest
        late_ref[:late_rows] = keep_ref[...] + got_ref[...]

    rest, late = call(
        head_body,
        [(mine, (count - head) * rank), (late_rows + head * mine, rank)],
        *moment_parts,
        *flat(factors[:head]),
        late_keep,
        late_got,
        flops=small * sum(map(len, blocks[:head])),
    )

    def step_body(number, *refs):
        part_refs, factor, (own_ref, rest_ref) = refs[:number], refs[number:-2], refs[-2:]
        total = add_all([part[...] for part in part_refs])
        own, rest = total[:, :rank], total[:, rank:]
        own_ref[...] = own
        rest_ref[...] = rest - dot_parts(halves(own), take(factor, rank, rest.shape[1]))

    def scatter(parts, number, stack_ref):
        own, slot = own_block(), 0
        for part in parts:
            for i in range(part.shape[0] // (number * mine)):
                for e in range(number):
                    start = (i * number + e) * mine
                    stack_ref[at(slot ^ own, mine), e * rank : (e + 1) * rank] = part[start : start + mine, :]
                slot += 1

    for bit in reversed(leaf_bits):
        got = swap(late, "sub", bit)
        late = jnp.concatenate([late[:late_rows] + got[:late_rows], late[late_rows:], got[late_rows:]], axis=0)
    late_parts = [late, swap(late, "sub", 0)]

    coarse = []
    for e in range(head, top):
        parts = partial_sums(rest, "rows", bits[e])
        own, rest = call(
            functools.partial(step_body, len(parts)),
            [(mine, rank), (mine, (top - e) * rank)],
            *parts,
            *factors[e],
            flops=small * (top - e),
        )
        coarse.append(own)
    coarse.append(rest)
    if len(bits[top]) == 1 and len(leaf_bits) == 1:
        row_bit, sub_bit = bits[top][0], leaf_bits[0]
        across = swap(rest, "rows", row_bit)
        beside = swap(jnp.concatenate(coarse, axis=0), "sub", sub_bit)
        corner = swap_both(rest, row_bit, sub_bit)
        end = (count - head - 1) * mine
        coarse = jnp.concatenate([*coarse[:-1], rest + across, beside[:end], beside[end:] + corner], axis=0)
    else:
        coarse[-1] = add_all(partial_sums(rest, "rows", bits[top]))
        coarse = jnp.concatenate(coarse, axis=0)
        for bit in reversed(leaf_bits):
            coarse = jnp.concatenate([coarse, swap(coarse, "sub", bit)], axis=0)
    coarse_parts = [coarse, swap(coarse, "sub", 0)]

    def answer_body(core_ref, *refs):
        factor_refs, basis_refs, out_refs = paired(refs[:-4]), refs[-4:-2], refs[-2:]
        wide = count - head
        zero = jnp.zeros((rank, rank), FLOAT)
        rows = {}
        for f in reversed(range(count)):
            start = 0 if f < head else rank
            if f + 1 < count:
                stack = jnp.concatenate([rows[g] for g in range(f + 1, count)], axis=0)
                row = -dot_parts(take(factor_refs[f], start, stack.shape[0]), halves(stack))
            else:
                row = jnp.zeros((rank, wide * rank), FLOAT)
            if f >= head:
                core = core_ref[f]
                own = core + core.T - dot_parts(take(factor_refs[f], 0, rank), halves(core))
                pieces = [zero] * (f - head) + [own]
                pieces += [row[:, e * rank : (e + 1) * rank] for e in range(f - head + 1, wide)]
                row = lanes(pieces)
            rows[f] = row
        gains = jnp.concatenate([rows[f] for f in range(count)], axis=0)
        store(out_refs, dot_parts([ref[...] for ref in basis_refs], halves(gains)))

    answer = call(
        answer_body,
        pair(rows_here, (count - head) * rank),
        cores,
        *flat(factors),
        *basis,
        flops=small * (count - head) * count * rows_here // rank,
    )

    def base_body(scale_ref, queries_ref, own_ref, other_ref, core_ref, *refs):
        factor_refs, basis_refs, scaled_refs = paired(refs[: 2 * head]), refs[2 * head : -5], refs[-5:-3]
        out_ref, stack_ref, gram_ref = refs[-3:]
        scatter([own_ref.at[late_rows:], other_ref.at[late_rows:]], head, stack_ref)
        side = core_side()
        for late_ref, place in ((own_ref, side), (other_ref, 1 - side)):
            stack_ref[at(place, columns // 2), head * rank :] = late_ref[: columns // 2]
            for e in range(head):
                start = columns // 2 + e * half
                gram_ref[at(place, half), e * rank : (e + 1) * rank] = late_ref[start : start + half]
        found = [None] * head
        for e in reversed(range(head)):
            core = core_ref[e]
            diagonal = dot(core.T, gram_ref[:, e * rank : (e + 1) * rank])
            moment = stack_ref[:, e * rank : (e + 1) * rank]
            if e:
                value = dot(moment, core + core.T - dot(diagonal, core), 1)
            else:
                first = dot(moment, core, 1)
                value = dot(stack_ref[:, head * rank :], core) - dot(first, diagonal, 1)
            if e + 1 < head:
                value = value - dot_parts(
                    halves(lanes(found[e + 1 :])), take(factor_refs[e], 0, (head - 1 - e) * rank), 1
                )
            found[e] = value
        left = [lanes([a[...], b[:, : head * rank]]) for a, b in zip(scaled_refs, basis_refs)]
        square = column_scale(scale_ref[...] * scale_ref[...])
        square = lanes([square] * (columns // rank))
        out_ref[...] = square * queries_ref[...] - dot_parts(left, halves(lanes([first, *found])), 1)

    (base,) = call(
        base_body,
        [(rows_here, columns)],
        scale,
        queries,
        *late_parts,
        cores,
        *flat(factors[:head]),
        *basis,
        *scaled,
        flops=small * 2 * (head + 1) * rows_here // rank,
        scratch=[pltpu.VMEM((columns, (head + 1) * rank), FLOAT), pltpu.VMEM((rank, head * rank), FLOAT)],
    )

    chunk = rows_here // 4

    def last_body(base_ref, high_ref, low_ref, own_ref, other_ref, out_hbm, stack_ref, out_ref, sems):
        scatter([own_ref, other_ref], count - head, stack_ref)
        right = halves(stack_ref[...])
        copies = []
        for i in range(4):
            rows = pl.ds(i * chunk, chunk)
            out_ref[rows, :] = base_ref[rows, :] - dot_parts([high_ref[rows, :], low_ref[rows, :]], right, 1)
            copies.append(pltpu.make_async_copy(out_ref.at[rows, :], out_hbm.at[rows, :], sems.at[i]))
            copies[-1].start()
        for copy in copies:
            copy.wait()

    (out,) = call(
        last_body,
        [(rows_here, columns)],
        base,
        *answer,
        *coarse_parts,
        flops=small * 2 * (count - head) * rows_here // rank,
        out_space=pltpu.HBM,
        scratch=[
            pltpu.VMEM((columns, (count - head) * rank), FLOAT),
            pltpu.VMEM((rows_here, columns), FLOAT),
            pltpu.SemaphoreType.DMA((4,)),
        ],
    )
    return out


def solution(mesh):
    in_specs = (
        P(("rows", "sub"), None),
        P(("rows", "sub")),
        P(("rows", "sub"), None),
        P("rows", None, None),
        P(None, ("rows", "sub"), None),
        P(),
    )
    out_specs = P(("rows", "sub"), None)

    return jax.shard_map(shards, mesh=mesh, in_specs=in_specs, out_specs=out_specs, check_vma=False)
```

```python
import functools

import jax
import jax.numpy as jnp
from jax import lax
from jax.experimental import pallas as pl
from jax.experimental.pallas import tpu as pltpu
from jax.sharding import PartitionSpec as P


FLOAT = jnp.float32
VMEM_LIMIT = 16 << 20


def halves(value):
    high = value.astype(jnp.bfloat16)
    return high, (value - high.astype(FLOAT)).astype(jnp.bfloat16)


def dot_parts(left, right, right_dim=0):
    mult = functools.partial(
        lax.dot_general,
        dimension_numbers=(((1,), (right_dim,)), ((), ())),
        preferred_element_type=FLOAT,
    )
    return mult(left[0], right[0]) + (mult(left[0], right[1]) + mult(left[1], right[0]))


def dot(left, right, right_dim=0):
    return dot_parts(halves(left), halves(right), right_dim)


def lanes(values):
    return values[0] if len(values) == 1 else jnp.concatenate(values, axis=1)


def column_scale(scale):
    size = scale.shape[1]
    return jnp.concatenate(
        [jnp.broadcast_to(scale[i : i + 1, :], (size, size)).T for i in range(scale.shape[0])], axis=0
    )


def core_side():
    return lax.rem(lax.axis_index("sub"), 2)


def own_block():
    place, value = lax.axis_index("sub"), 0
    for _ in range(lax.axis_size("sub").bit_length() - 1):
        value = value * 2 + lax.rem(place, 2)
        place = place // 2
    return value


def at(index, size):
    return pl.ds(pl.multiple_of(index * size, 8), size)


def call(body, outs, *operands, flops, spaces=None, out_space=pltpu.VMEM, scratch=()):
    spaces = spaces or [pltpu.VMEM] * len(operands)
    size = sum(a.dtype.itemsize * a.size for a in operands)
    outs = [out if isinstance(out, jax.ShapeDtypeStruct) else jax.ShapeDtypeStruct(out, FLOAT) for out in outs]
    return pl.pallas_call(
        body,
        out_shape=outs,
        in_specs=[pl.BlockSpec(memory_space=space) for space in spaces],
        out_specs=[pl.BlockSpec(memory_space=out_space)] * len(outs),
        scratch_shapes=list(scratch),
        compiler_params=pltpu.CompilerParams(vmem_limit_bytes=VMEM_LIMIT),
        cost_estimate=pl.CostEstimate(flops=flops, bytes_accessed=size, transcendentals=0),
    )(*operands)


def pair(*shape):
    return [jax.ShapeDtypeStruct(shape, jnp.bfloat16)] * 2


def store(refs, value):
    for ref, part in zip(refs, halves(value)):
        ref[...] = part


def swap(array, axis, bit):
    return lax.ppermute(array, axis, [(i, i ^ 1 << bit) for i in range(lax.axis_size(axis))])


def swap_both(array, row_bit, sub_bit):
    sub = lax.axis_size("sub")
    mask = (1 << row_bit) * sub + (1 << sub_bit)
    pairs = [(i, i ^ mask) for i in range(lax.axis_size("rows") * sub)]
    return lax.ppermute(array, ("rows", "sub"), pairs)


def partial_sums(array, axis, bits):
    bits = list(bits)
    if not bits:
        return [array]
    for bit in bits[:-1]:
        array = array + swap(array, axis, bit)
    return [array, swap(array, axis, bits[-1])]


def add_all(parts):
    return functools.reduce(lambda a, b: a + b, parts)


def shards(queries, row_scale, leaf_basis, leaf_cores, level_basis, level_cores):
    levels = level_basis.shape[0]
    count = levels + 1
    top = levels
    rows_here, rank = leaf_basis.shape
    columns = queries.shape[1]
    groups, sub = lax.axis_size("rows"), lax.axis_size("sub")
    heights = [None] + [levels + 1 - e for e in range(1, count)]
    widths = [1] + [groups // 2 ** heights[e] for e in range(1, count)]
    head = sum(w == 1 for w in widths)
    bits = [range(0)] + [
        range(widths[e - 1].bit_length() - 1, widths[e].bit_length() - 1) for e in range(1, count)
    ]
    blocks = [list(range(e + 1, count)) for e in range(count)]
    coarse = count - head
    sub_bits = sub.bit_length() - 1
    leaf_bits = range(1, sub_bits)
    mine = columns // sub
    half = rank // 2
    small = 2 * 3 * rank**3

    scale = row_scale.reshape(-1, rank)
    starts = [sum(len(b) for b in blocks[:e]) * rank for e in range(count + 1)]

    def gram_body(*refs):
        sources, (out_ref, core_ref), (scale_ref, leaf_ref, level_ref, sems) = refs[:5], refs[5:7], refs[7:]
        scale_hbm, leaf_hbm, level_hbm, leaf_core_hbm, core_hbm = sources
        targets = [(scale_hbm, scale_ref), (leaf_hbm, leaf_ref)]
        targets += [(level_hbm.at[e], level_ref.at[e]) for e in reversed(range(levels))]
        place = lax.axis_index("rows")
        targets.append((leaf_core_hbm.at[0], core_ref.at[0]))
        for e in range(1, count):
            targets.append((core_hbm.at[2 ** heights[e] - 2 + place // widths[e]], core_ref.at[e]))
        copies = [pltpu.make_async_copy(a, b, sems.at[i]) for i, (a, b) in enumerate(targets)]
        for copy in copies:
            copy.start()
        for copy in copies[: 2 + levels]:
            copy.wait()
        vectors = [column_scale(scale_ref[...]) * leaf_ref[...]]
        vectors += [level_ref[levels - e] for e in range(1, count)]
        parts = [halves(v) for v in vectors]
        side = core_side()
        for e in range(count):
            group = ([e] if e >= head else []) + blocks[e]
            right = [lanes([parts[f][i] for f in group]) for i in range(2)]
            value = dot_parts(halves(vectors[e].T), right)
            for h in range(2):
                rows = value[h * half : (h + 1) * half]
                if e >= head:
                    place = starts[count] + (e - head) * rank
                    out_ref[at(h ^ side, half), place : place + rank] = rows[:, :rank]
                    rows = rows[:, rank:]
                if blocks[e]:
                    out_ref[at(h ^ side, half), starts[e] : starts[e + 1]] = rows
        for copy in copies[2 + levels :]:
            copy.wait()

    gram, cores = call(
        gram_body,
        [(rank, starts[count] + coarse * rank), (count, rank, rank)],
        *[
            pltpu.with_memory_space_constraint(array, pltpu.HBM)
            for array in (scale, leaf_basis, level_basis, leaf_cores, level_cores)
        ],
        flops=small * (starts[count] // rank + coarse) * rows_here // rank,
        spaces=[pltpu.HBM] * 5,
        scratch=[
            pltpu.VMEM(scale.shape, FLOAT),
            pltpu.VMEM(leaf_basis.shape, FLOAT),
            pltpu.VMEM(level_basis.shape, FLOAT),
            pltpu.SemaphoreType.DMA((2 + levels + count,)),
        ],
    )
    gram_chip = gram[:half] + swap(gram[half:], "sub", 0)
    early = add_all(partial_sums(gram_chip[:, : starts[count]], "sub", leaf_bits))
    diagonal = []
    for e in reversed(range(head, count)):
        place = starts[count] + (e - head) * rank
        diagonal = lanes([gram_chip[:, place : place + rank], *diagonal])
        diagonal = [add_all(partial_sums(diagonal, "rows", bits[e]))]
    diagonal = diagonal[0]

    def moment_body(scale_ref, queries_ref, leaf_ref, level_ref, out_ref, *basis_refs):
        spread = column_scale(scale_ref[...])
        right = halves(lanes([leaf_ref[...]] + [spread * level_ref[levels - e] for e in range(1, count)]))
        for basis_ref, part in zip(basis_refs, right):
            basis_ref[...] = part
        value = dot_parts(halves(queries_ref[...].T), right)
        own = own_block()
        for i in range(sub):
            out_ref[at(i ^ own, mine), :] = value[i * mine : (i + 1) * mine]

    value, *basis = call(
        moment_body,
        [(columns, count * rank), *pair(rows_here, count * rank)],
        scale,
        queries,
        leaf_basis,
        level_basis,
        flops=small * count * 2 * rows_here // rank,
    )
    size = columns
    for bit in range(sub_bits):
        size //= 2
        sent, moment_parts = value[size:], [value[:size], swap(value[size:], "sub", bit)]
        value = add_all(moment_parts)
        if bit == 0:
            moment_chip = value

    late_rows = columns // 2 + head * half

    def late_body(scale_ref, queries_ref, leaf_ref, level_ref, out_ref, *scaled_refs):
        spread = column_scale(scale_ref[...])
        vectors = spread * leaf_ref[...]
        side = core_side()
        scaled = halves(spread * vectors)
        for scaled_ref, part in zip(scaled_refs, scaled):
            scaled_ref[...] = part
        value = dot_parts(halves(queries_ref[...].T), scaled)
        for h in range(2):
            base = (h ^ side) * late_rows
            part = value[h * columns // 2 : (h + 1) * columns // 2]
            out_ref[pl.ds(pl.multiple_of(base, 8), columns // 2), :] = part
        for e in range(head):
            basis = vectors if e == 0 else level_ref[levels - e]
            value = dot(basis.T, basis)
            for h in range(2):
                base = (h ^ side) * late_rows + columns // 2 + e * half
                out_ref[pl.ds(pl.multiple_of(base, 8), half), :] = value[h * half : (h + 1) * half]

    late, *scaled = call(
        late_body,
        [(2 * late_rows, rank), *pair(rows_here, rank)],
        scale,
        queries,
        leaf_basis,
        level_basis,
        flops=small * (2 + head) * rows_here // rank,
    )
    late_chip = late[:late_rows] + swap(late[late_rows:], "sub", 0)

    def stacked(array, size):
        return [
            array[i : i + size, j : j + rank]
            for i in range(0, array.shape[0], size)
            for j in range(0, array.shape[1], rank)
        ]

    late_chip = [late_chip, *stacked(diagonal, half)]
    if len(leaf_bits) == 1:
        late = jnp.concatenate([*late_chip, *stacked(moment_parts[0][:, : head * rank], mine)], axis=0)
        got = swap(late, "sub", leaf_bits[0])
        late_size = late_rows + coarse * half
        others = jnp.concatenate(stacked(sent[:, : head * rank], mine), axis=0)
        late = jnp.concatenate(
            [
                late[:late_size] + got[:late_size],
                *stacked(value[:, : head * rank], mine),
                others + got[late_size:],
            ],
            axis=0,
        )
    else:
        late = jnp.concatenate([*late_chip, *stacked(moment_chip[:, : head * rank], mine)], axis=0)
        late_size = late_rows + coarse * half
        late = add_all(partial_sums(late, "sub", leaf_bits))
    late_parts = [late, swap(late, "sub", 0)]

    def product_body(group, own_ref, other_ref, core_ref, *refs):
        out_refs, stack_ref = refs[:-1], refs[-1]
        side = core_side()
        stack_ref[at(side, half), :] = own_ref[...]
        stack_ref[at(1 - side, half), :] = other_ref[...]
        base = starts[group[0]]
        for i, e in enumerate(group):
            block = stack_ref[:, starts[e] - base : starts[e + 1] - base]
            store(out_refs[2 * i : 2 * i + 2], dot(core_ref[e].T, block))

    def products(group, own):
        out = call(
            functools.partial(product_body, group),
            [part for e in group for part in pair(rank, starts[e + 1] - starts[e])],
            own,
            swap(own, "sub", 0),
            cores,
            flops=small * sum(len(blocks[e]) for e in group),
            scratch=[pltpu.VMEM((rank, own.shape[1]), FLOAT)],
        )
        return [out[2 * i : 2 * i + 2] for i in range(len(group))]

    factors = products(list(range(head)), early[:, : starts[head]])
    remaining = early[:, starts[head] :]
    for e in range(head, top):
        remaining = add_all(partial_sums(remaining, "rows", bits[e]))
        size = starts[e + 1] - starts[e]
        factors += products([e], remaining[:, :size])
        remaining = remaining[:, size:]

    def flat(group):
        return [part for factor in group for part in factor]

    def paired(refs):
        return [refs[i : i + 2] for i in range(0, len(refs), 2)]

    def take(factor, start, size):
        return [ref[:, start : start + size] for ref in factor]

    def head_body(*refs):
        part_refs, factor_refs, rest_ref = refs[: len(moment_parts)], paired(refs[len(moment_parts) : -1]), refs[-1]
        rest = add_all([part[...] for part in part_refs])
        for e in range(head):
            own, rest = rest[:, :rank], rest[:, rank:]
            rest = rest - dot_parts(halves(own), take(factor_refs[e], 0, rest.shape[1]))
        rest_ref[...] = rest

    (rest,) = call(
        head_body,
        [(mine, coarse * rank)],
        *moment_parts,
        *flat(factors[:head]),
        flops=small * sum(map(len, blocks[:head])),
    )

    def step_body(number, *refs):
        part_refs, factor, (own_ref, rest_ref) = refs[:number], refs[number:-2], refs[-2:]
        total = add_all([part[...] for part in part_refs])
        own, rest = total[:, :rank], total[:, rank:]
        own_ref[...] = own
        rest_ref[...] = rest - dot_parts(halves(own), take(factor, 0, rest.shape[1]))

    def scatter(parts, number, stack_ref):
        own, slot = own_block(), 0
        for part in parts:
            for i in range(part.shape[0] // (number * mine)):
                for e in range(number):
                    start = (i * number + e) * mine
                    stack_ref[at(slot ^ own, mine), e * rank : (e + 1) * rank] = part[start : start + mine, :]
                slot += 1

    found = []
    for e in range(head, top):
        parts = partial_sums(rest, "rows", bits[e])
        own, rest = call(
            functools.partial(step_body, len(parts)),
            [(mine, rank), (mine, (top - e) * rank)],
            *parts,
            *factors[e],
            flops=small * (top - e),
        )
        found.append(own)
    found.append(rest)
    if len(bits[top]) == 1 and len(leaf_bits) == 1:
        row_bit, sub_bit = bits[top][0], leaf_bits[0]
        across = swap(rest, "rows", row_bit)
        beside = swap(jnp.concatenate(found, axis=0), "sub", sub_bit)
        corner = swap_both(rest, row_bit, sub_bit)
        end = (coarse - 1) * mine
        found = jnp.concatenate([*found[:-1], rest + across, beside[:end], beside[end:] + corner], axis=0)
    else:
        found[-1] = add_all(partial_sums(rest, "rows", bits[top]))
        found = jnp.concatenate(found, axis=0)
        for bit in reversed(leaf_bits):
            found = jnp.concatenate([found, swap(found, "sub", bit)], axis=0)
    found_parts = [found, swap(found, "sub", 0)]

    def answer_body(*refs):
        factor_refs, basis_refs, out_refs = paired(refs[:-4]), refs[-4:-2], refs[-2:]
        rows = {}
        for f in reversed(range(count)):
            if f + 1 < count:
                stack = jnp.concatenate([rows[g] for g in range(f + 1, count)], axis=0)
                row = -dot_parts(take(factor_refs[f], 0, stack.shape[0]), halves(stack))
            else:
                row = jnp.zeros((rank, coarse * rank), FLOAT)
            if f >= head:
                line = lax.broadcasted_iota(jnp.int32, row.shape, 0) + (f - head) * rank
                row = row + jnp.where(line == lax.broadcasted_iota(jnp.int32, row.shape, 1), 1.0, 0.0)
            rows[f] = row
        gains = jnp.concatenate([rows[f] for f in range(count)], axis=0)
        store(out_refs, dot_parts([ref[...] for ref in basis_refs], halves(gains)))

    answer = call(
        answer_body,
        pair(rows_here, coarse * rank),
        *flat(factors),
        *basis,
        flops=small * coarse * count * rows_here // rank,
    )

    def base_body(scale_ref, queries_ref, own_ref, other_ref, core_ref, *refs):
        factor_refs, basis_refs, scaled_refs = paired(refs[: 2 * head]), refs[2 * head : -7], refs[-7:-5]
        out_ref, *gain_refs, stack_ref, gram_ref = refs[-5:]
        scatter([own_ref.at[late_size:], other_ref.at[late_size:]], head, stack_ref)
        side = core_side()
        for late_ref, place in ((own_ref, side), (other_ref, 1 - side)):
            stack_ref[at(place, columns // 2), head * rank :] = late_ref[: columns // 2]
            for e in range(count):
                start = columns // 2 + e * half
                gram_ref[at(place, half), e * rank : (e + 1) * rank] = late_ref[start : start + half]
        products = [dot(core_ref[e].T, gram_ref[:, e * rank : (e + 1) * rank]) for e in range(count)]
        gains = [core_ref[e] + core_ref[e].T - dot(products[e], core_ref[e]) for e in range(1, count)]
        store(gain_refs, lanes(gains[head - 1 :]))
        rest = stack_ref[:, : head * rank]
        moments = []
        for e in range(head):
            own, rest = rest[:, :rank], rest[:, rank:]
            moments.append(own)
            if e + 1 < head:
                rest = rest - dot_parts(halves(own), take(factor_refs[e], 0, rest.shape[1]))
        first = dot(moments[0], core_ref[0], 1)
        found = [dot(stack_ref[:, head * rank :], core_ref[0]) - dot(first, products[0], 1)]
        found += [dot(moments[e], gains[e - 1], 1) for e in range(1, head)]
        for e in reversed(range(head - 1)):
            size = (head - 1 - e) * rank
            found[e] = found[e] - dot_parts(halves(lanes(found[e + 1 :])), take(factor_refs[e], 0, size), 1)
        left = [lanes([a[...], b[:, : head * rank]]) for a, b in zip(scaled_refs, basis_refs)]
        square = column_scale(scale_ref[...] * scale_ref[...])
        square = lanes([square] * (columns // rank))
        out_ref[...] = square * queries_ref[...] - dot_parts(left, halves(lanes([first, *found])), 1)

    base, *gains = call(
        base_body,
        [(rows_here, columns), *pair(rank, coarse * rank)],
        scale,
        queries,
        *late_parts,
        cores,
        *flat(factors[:head]),
        *basis,
        *scaled,
        flops=small * 2 * (head + 1) * rows_here // rank,
        scratch=[pltpu.VMEM((columns, (head + 1) * rank), FLOAT), pltpu.VMEM((rank, count * rank), FLOAT)],
    )

    chunk = rows_here // 4

    def last_body(base_ref, high_ref, low_ref, *refs):
        gain_refs, (own_ref, other_ref, out_hbm, stack_ref, out_ref, sems) = refs[:2], refs[2:]
        scatter([own_ref, other_ref], coarse, stack_ref)
        right = []
        for e in range(coarse):
            where = slice(e * rank, (e + 1) * rank)
            right.append(dot_parts(halves(stack_ref[:, where]), [ref[:, where] for ref in gain_refs], 1))
        right = halves(lanes(right))
        copies = []
        for i in range(4):
            rows = pl.ds(i * chunk, chunk)
            out_ref[rows, :] = base_ref[rows, :] - dot_parts([high_ref[rows, :], low_ref[rows, :]], right, 1)
            copies.append(pltpu.make_async_copy(out_ref.at[rows, :], out_hbm.at[rows, :], sems.at[i]))
            copies[-1].start()
        for copy in copies:
            copy.wait()

    (out,) = call(
        last_body,
        [(rows_here, columns)],
        base,
        *answer,
        *gains,
        *found_parts,
        flops=small * 2 * coarse * rows_here // rank,
        out_space=pltpu.HBM,
        scratch=[
            pltpu.VMEM((columns, coarse * rank), FLOAT),
            pltpu.VMEM((rows_here, columns), FLOAT),
            pltpu.SemaphoreType.DMA((4,)),
        ],
    )
    return out


def solution(mesh):
    in_specs = (
        P(("rows", "sub"), None),
        P(("rows", "sub")),
        P(("rows", "sub"), None),
        P("rows", None, None),
        P(None, ("rows", "sub"), None),
        P(),
    )
    out_specs = P(("rows", "sub"), None)

    return jax.shard_map(shards, mesh=mesh, in_specs=in_specs, out_specs=out_specs, check_vma=False)
```

```python
import functools

import jax
import jax.numpy as jnp
from jax import lax
from jax.experimental import pallas as pl
from jax.experimental.pallas import tpu as pltpu
from jax.sharding import PartitionSpec as P


FLOAT = jnp.float32
VMEM_LIMIT = 16 << 20


def halves(value):
    high = value.astype(jnp.bfloat16)
    return high, (value - high.astype(FLOAT)).astype(jnp.bfloat16)


def dot_parts(left, right, right_dim=0):
    mult = functools.partial(
        lax.dot_general,
        dimension_numbers=(((1,), (right_dim,)), ((), ())),
        preferred_element_type=FLOAT,
    )
    return mult(left[0], right[0]) + (mult(left[0], right[1]) + mult(left[1], right[0]))


def dot(left, right, right_dim=0):
    return dot_parts(halves(left), halves(right), right_dim)


def lanes(values):
    return values[0] if len(values) == 1 else jnp.concatenate(values, axis=1)


def column_scale(scale):
    size = scale.shape[1]
    return jnp.concatenate(
        [jnp.broadcast_to(scale[i : i + 1, :], (size, size)).T for i in range(scale.shape[0])], axis=0
    )


def core_side():
    return lax.rem(lax.axis_index("sub"), 2)


def own_block():
    place, value = lax.axis_index("sub"), 0
    for _ in range(lax.axis_size("sub").bit_length() - 1):
        value = value * 2 + lax.rem(place, 2)
        place = place // 2
    return value


def at(index, size):
    return pl.ds(pl.multiple_of(index * size, 8), size)


def call(body, outs, *operands, flops, spaces=None, out_space=pltpu.VMEM, scratch=()):
    spaces = spaces or [pltpu.VMEM] * len(operands)
    size = sum(a.dtype.itemsize * a.size for a in operands)
    outs = [out if isinstance(out, jax.ShapeDtypeStruct) else jax.ShapeDtypeStruct(out, FLOAT) for out in outs]
    return pl.pallas_call(
        body,
        out_shape=outs,
        in_specs=[pl.BlockSpec(memory_space=space) for space in spaces],
        out_specs=[pl.BlockSpec(memory_space=out_space)] * len(outs),
        scratch_shapes=list(scratch),
        compiler_params=pltpu.CompilerParams(vmem_limit_bytes=VMEM_LIMIT),
        cost_estimate=pl.CostEstimate(flops=flops, bytes_accessed=size, transcendentals=0),
    )(*operands)


def pair(*shape):
    return [jax.ShapeDtypeStruct(shape, jnp.bfloat16)] * 2


def store(refs, value):
    for ref, part in zip(refs, halves(value)):
        ref[...] = part


def swap(array, axis, bit):
    return lax.ppermute(array, axis, [(i, i ^ 1 << bit) for i in range(lax.axis_size(axis))])


def partial_sums(array, axis, bits):
    bits = list(bits)
    if not bits:
        return [array]
    for bit in bits[:-1]:
        array = array + swap(array, axis, bit)
    return [array, swap(array, axis, bits[-1])]


def add_all(parts):
    return functools.reduce(lambda a, b: a + b, parts)


def shards(queries, row_scale, leaf_basis, leaf_cores, level_basis, level_cores):
    levels = level_basis.shape[0]
    count = levels + 1
    top = levels
    rows_here, rank = leaf_basis.shape
    columns = queries.shape[1]
    groups, sub = lax.axis_size("rows"), lax.axis_size("sub")
    heights = [None] + [levels + 1 - e for e in range(1, count)]
    widths = [1] + [groups // 2 ** heights[e] for e in range(1, count)]
    head = sum(w == 1 for w in widths)
    bits = [range(0)] + [
        range(widths[e - 1].bit_length() - 1, widths[e].bit_length() - 1) for e in range(1, count)
    ]
    blocks = [list(range(e + 1, count)) for e in range(count)]
    coarse = count - head
    sub_bits = sub.bit_length() - 1
    leaf_bits = range(1, sub_bits)
    mine = columns // sub
    half = rank // 2
    small = 2 * 3 * rank**3

    scale = row_scale.reshape(-1, rank)
    starts = [sum(len(b) for b in blocks[:e]) * rank for e in range(count + 1)]

    def gram_body(*refs):
        sources, (out_ref, core_ref), (scale_ref, leaf_ref, level_ref, sems) = refs[:5], refs[5:7], refs[7:]
        scale_hbm, leaf_hbm, level_hbm, leaf_core_hbm, core_hbm = sources
        targets = [(scale_hbm, scale_ref), (leaf_hbm, leaf_ref)]
        targets += [(level_hbm.at[e], level_ref.at[e]) for e in reversed(range(levels))]
        place = lax.axis_index("rows")
        targets.append((leaf_core_hbm.at[0], core_ref.at[0]))
        for e in range(1, count):
            targets.append((core_hbm.at[2 ** heights[e] - 2 + place // widths[e]], core_ref.at[e]))
        copies = [pltpu.make_async_copy(a, b, sems.at[i]) for i, (a, b) in enumerate(targets)]
        for copy in copies:
            copy.start()
        for copy in copies[: 2 + levels]:
            copy.wait()
        vectors = [column_scale(scale_ref[...]) * leaf_ref[...]]
        vectors += [level_ref[levels - e] for e in range(1, count)]
        parts = [halves(v) for v in vectors]
        side = core_side()
        for e in range(count):
            group = ([e] if e >= head else []) + blocks[e]
            right = [lanes([parts[f][i] for f in group]) for i in range(2)]
            value = dot_parts(halves(vectors[e].T), right)
            for h in range(2):
                rows = value[h * half : (h + 1) * half]
                if e >= head:
                    place = starts[count] + (e - head) * rank
                    out_ref[at(h ^ side, half), place : place + rank] = rows[:, :rank]
                    rows = rows[:, rank:]
                if blocks[e]:
                    out_ref[at(h ^ side, half), starts[e] : starts[e + 1]] = rows
        for copy in copies[2 + levels :]:
            copy.wait()

    gram, cores = call(
        gram_body,
        [(rank, starts[count] + coarse * rank), (count, rank, rank)],
        *[
            pltpu.with_memory_space_constraint(array, pltpu.HBM)
            for array in (scale, leaf_basis, level_basis, leaf_cores, level_cores)
        ],
        flops=small * (starts[count] // rank + coarse) * rows_here // rank,
        spaces=[pltpu.HBM] * 5,
        scratch=[
            pltpu.VMEM(scale.shape, FLOAT),
            pltpu.VMEM(leaf_basis.shape, FLOAT),
            pltpu.VMEM(level_basis.shape, FLOAT),
            pltpu.SemaphoreType.DMA((2 + levels + count,)),
        ],
    )
    gram_chip = gram[:half] + swap(gram[half:], "sub", 0)
    early = add_all(partial_sums(gram_chip[:, : starts[count]], "sub", leaf_bits))
    diagonal = []
    for e in reversed(range(head, count)):
        place = starts[count] + (e - head) * rank
        diagonal = lanes([gram_chip[:, place : place + rank], *diagonal])
        diagonal = [add_all(partial_sums(diagonal, "rows", bits[e]))]
    diagonal = diagonal[0]

    def moment_body(scale_ref, queries_ref, leaf_ref, level_ref, out_ref, *basis_refs):
        spread = column_scale(scale_ref[...])
        right = halves(lanes([leaf_ref[...]] + [spread * level_ref[levels - e] for e in range(1, count)]))
        for basis_ref, part in zip(basis_refs, right):
            basis_ref[...] = part
        value = dot_parts(halves(queries_ref[...].T), right)
        own = own_block()
        for i in range(sub):
            out_ref[at(i ^ own, mine), :] = value[i * mine : (i + 1) * mine]

    value, *basis = call(
        moment_body,
        [(columns, count * rank), *pair(rows_here, count * rank)],
        scale,
        queries,
        leaf_basis,
        level_basis,
        flops=small * count * 2 * rows_here // rank,
    )
    size = columns
    for bit in range(sub_bits):
        size //= 2
        sent, moment_parts = value[size:], [value[:size], swap(value[size:], "sub", bit)]
        value = add_all(moment_parts)
        if bit == 0:
            moment_chip = value

    late_rows = columns // 2 + head * half

    def late_body(scale_ref, queries_ref, leaf_ref, level_ref, out_ref, *scaled_refs):
        spread = column_scale(scale_ref[...])
        vectors = spread * leaf_ref[...]
        side = core_side()
        scaled = halves(spread * vectors)
        for scaled_ref, part in zip(scaled_refs, scaled):
            scaled_ref[...] = part
        value = dot_parts(halves(queries_ref[...].T), scaled)
        for h in range(2):
            base = (h ^ side) * late_rows
            part = value[h * columns // 2 : (h + 1) * columns // 2]
            out_ref[pl.ds(pl.multiple_of(base, 8), columns // 2), :] = part
        for e in range(head):
            basis = vectors if e == 0 else level_ref[levels - e]
            value = dot(basis.T, basis)
            for h in range(2):
                base = (h ^ side) * late_rows + columns // 2 + e * half
                out_ref[pl.ds(pl.multiple_of(base, 8), half), :] = value[h * half : (h + 1) * half]

    late, *scaled = call(
        late_body,
        [(2 * late_rows, rank), *pair(rows_here, rank)],
        scale,
        queries,
        leaf_basis,
        level_basis,
        flops=small * (2 + head) * rows_here // rank,
    )
    late_chip = late[:late_rows] + swap(late[late_rows:], "sub", 0)

    def stacked(array, size):
        return [
            array[i : i + size, j : j + rank]
            for i in range(0, array.shape[0], size)
            for j in range(0, array.shape[1], rank)
        ]

    late_chip = [late_chip, *stacked(diagonal, half)]
    if len(leaf_bits) == 1:
        late = jnp.concatenate([*late_chip, *stacked(moment_parts[0][:, : head * rank], mine)], axis=0)
        got = swap(late, "sub", leaf_bits[0])
        late_size = late_rows + coarse * half
        others = jnp.concatenate(stacked(sent[:, : head * rank], mine), axis=0)
        late = jnp.concatenate(
            [
                late[:late_size] + got[:late_size],
                *stacked(value[:, : head * rank], mine),
                others + got[late_size:],
            ],
            axis=0,
        )
    else:
        late = jnp.concatenate([*late_chip, *stacked(moment_chip[:, : head * rank], mine)], axis=0)
        late_size = late_rows + coarse * half
        late = add_all(partial_sums(late, "sub", leaf_bits))
    late_parts = [late, swap(late, "sub", 0)]

    def product_body(group, own_ref, other_ref, core_ref, *refs):
        out_refs, stack_ref = refs[:-1], refs[-1]
        side = core_side()
        stack_ref[at(side, half), :] = own_ref[...]
        stack_ref[at(1 - side, half), :] = other_ref[...]
        base = starts[group[0]]
        for i, e in enumerate(group):
            block = stack_ref[:, starts[e] - base : starts[e + 1] - base]
            store(out_refs[2 * i : 2 * i + 2], dot(core_ref[e].T, block))

    def products(group, own):
        out = call(
            functools.partial(product_body, group),
            [part for e in group for part in pair(rank, starts[e + 1] - starts[e])],
            own,
            swap(own, "sub", 0),
            cores,
            flops=small * sum(len(blocks[e]) for e in group),
            scratch=[pltpu.VMEM((rank, own.shape[1]), FLOAT)],
        )
        return [out[2 * i : 2 * i + 2] for i in range(len(group))]

    factors = products(list(range(head)), early[:, : starts[head]])
    remaining = early[:, starts[head] :]
    for e in range(head, top):
        remaining = add_all(partial_sums(remaining, "rows", bits[e]))
        size = starts[e + 1] - starts[e]
        factors += products([e], remaining[:, :size])
        remaining = remaining[:, size:]

    def flat(group):
        return [part for factor in group for part in factor]

    def paired(refs):
        return [refs[i : i + 2] for i in range(0, len(refs), 2)]

    def take(factor, start, size):
        return [ref[:, start : start + size] for ref in factor]

    def head_body(*refs):
        part_refs, factor_refs, rest_ref = refs[: len(moment_parts)], paired(refs[len(moment_parts) : -1]), refs[-1]
        rest = add_all([part[...] for part in part_refs])
        for e in range(head):
            own, rest = rest[:, :rank], rest[:, rank:]
            rest = rest - dot_parts(halves(own), take(factor_refs[e], 0, rest.shape[1]))
        rest_ref[...] = rest

    (rest,) = call(
        head_body,
        [(mine, coarse * rank)],
        *moment_parts,
        *flat(factors[:head]),
        flops=small * sum(map(len, blocks[:head])),
    )

    def step_body(number, *refs):
        part_refs, factor, (own_ref, rest_ref) = refs[:number], refs[number:-2], refs[-2:]
        total = add_all([part[...] for part in part_refs])
        own, rest = total[:, :rank], total[:, rank:]
        own_ref[...] = own
        rest_ref[...] = rest - dot_parts(halves(own), take(factor, 0, rest.shape[1]))

    def scatter(parts, number, stack_ref):
        own, slot = own_block(), 0
        for part in parts:
            for i in range(part.shape[0] // (number * mine)):
                for e in range(number):
                    start = (i * number + e) * mine
                    stack_ref[at(slot ^ own, mine), e * rank : (e + 1) * rank] = part[start : start + mine, :]
                slot += 1

    found = []
    for e in range(head, top):
        parts = partial_sums(rest, "rows", bits[e])
        own, rest = call(
            functools.partial(step_body, len(parts)),
            [(mine, rank), (mine, (top - e) * rank)],
            *parts,
            *factors[e],
            flops=small * (top - e),
        )
        found.append(own)
    found.append(rest)
    found[-1] = add_all(partial_sums(rest, "rows", bits[top]))
    found = jnp.concatenate(found, axis=0)
    for bit in reversed(leaf_bits):
        found = jnp.concatenate([found, swap(found, "sub", bit)], axis=0)
    found_parts = [found, swap(found, "sub", 0)]

    def answer_body(*refs):
        factor_refs, basis_refs, out_refs = paired(refs[:-4]), refs[-4:-2], refs[-2:]
        rows = {}
        for f in reversed(range(count)):
            if f + 1 < count:
                stack = jnp.concatenate([rows[g] for g in range(f + 1, count)], axis=0)
                row = -dot_parts(take(factor_refs[f], 0, stack.shape[0]), halves(stack))
            else:
                row = jnp.zeros((rank, coarse * rank), FLOAT)
            if f >= head:
                line = lax.broadcasted_iota(jnp.int32, row.shape, 0) + (f - head) * rank
                row = row + jnp.where(line == lax.broadcasted_iota(jnp.int32, row.shape, 1), 1.0, 0.0)
            rows[f] = row
        gains = jnp.concatenate([rows[f] for f in range(count)], axis=0)
        store(out_refs, dot_parts([ref[...] for ref in basis_refs], halves(gains)))

    answer = call(
        answer_body,
        pair(rows_here, coarse * rank),
        *flat(factors),
        *basis,
        flops=small * coarse * count * rows_here // rank,
    )

    def base_body(scale_ref, queries_ref, own_ref, other_ref, core_ref, *refs):
        factor_refs, basis_refs, scaled_refs = paired(refs[: 2 * head]), refs[2 * head : -7], refs[-7:-5]
        out_ref, *gain_refs, stack_ref, gram_ref = refs[-5:]
        scatter([own_ref.at[late_size:], other_ref.at[late_size:]], head, stack_ref)
        side = core_side()
        for late_ref, place in ((own_ref, side), (other_ref, 1 - side)):
            stack_ref[at(place, columns // 2), head * rank :] = late_ref[: columns // 2]
            for e in range(count):
                start = columns // 2 + e * half
                gram_ref[at(place, half), e * rank : (e + 1) * rank] = late_ref[start : start + half]
        products = [dot(core_ref[e].T, gram_ref[:, e * rank : (e + 1) * rank]) for e in range(count)]
        gains = [core_ref[e] + core_ref[e].T - dot(products[e], core_ref[e]) for e in range(1, count)]
        store(gain_refs, lanes(gains[head - 1 :]))
        rest = stack_ref[:, : head * rank]
        moments = []
        for e in range(head):
            own, rest = rest[:, :rank], rest[:, rank:]
            moments.append(own)
            if e + 1 < head:
                rest = rest - dot_parts(halves(own), take(factor_refs[e], 0, rest.shape[1]))
        first = dot(moments[0], core_ref[0], 1)
        found = [dot(stack_ref[:, head * rank :], core_ref[0]) - dot(first, products[0], 1)]
        found += [dot(moments[e], gains[e - 1], 1) for e in range(1, head)]
        for e in reversed(range(head - 1)):
            size = (head - 1 - e) * rank
            found[e] = found[e] - dot_parts(halves(lanes(found[e + 1 :])), take(factor_refs[e], 0, size), 1)
        left = [lanes([a[...], b[:, : head * rank]]) for a, b in zip(scaled_refs, basis_refs)]
        square = column_scale(scale_ref[...] * scale_ref[...])
        square = lanes([square] * (columns // rank))
        out_ref[...] = square * queries_ref[...] - dot_parts(left, halves(lanes([first, *found])), 1)

    base, *gains = call(
        base_body,
        [(rows_here, columns), *pair(rank, coarse * rank)],
        scale,
        queries,
        *late_parts,
        cores,
        *flat(factors[:head]),
        *basis,
        *scaled,
        flops=small * 2 * (head + 1) * rows_here // rank,
        scratch=[pltpu.VMEM((columns, (head + 1) * rank), FLOAT), pltpu.VMEM((rank, count * rank), FLOAT)],
    )

    chunk = rows_here // 4

    def last_body(base_ref, high_ref, low_ref, *refs):
        gain_refs, (own_ref, other_ref, out_hbm, stack_ref, out_ref, sems) = refs[:2], refs[2:]
        scatter([own_ref, other_ref], coarse, stack_ref)
        right = []
        for e in range(coarse):
            where = slice(e * rank, (e + 1) * rank)
            right.append(dot_parts(halves(stack_ref[:, where]), [ref[:, where] for ref in gain_refs], 1))
        right = halves(lanes(right))
        copies = []
        for i in range(4):
            rows = pl.ds(i * chunk, chunk)
            out_ref[rows, :] = base_ref[rows, :] - dot_parts([high_ref[rows, :], low_ref[rows, :]], right, 1)
            copies.append(pltpu.make_async_copy(out_ref.at[rows, :], out_hbm.at[rows, :], sems.at[i]))
            copies[-1].start()
        for copy in copies:
            copy.wait()

    (out,) = call(
        last_body,
        [(rows_here, columns)],
        base,
        *answer,
        *gains,
        *found_parts,
        flops=small * 2 * coarse * rows_here // rank,
        out_space=pltpu.HBM,
        scratch=[
            pltpu.VMEM((columns, coarse * rank), FLOAT),
            pltpu.VMEM((rows_here, columns), FLOAT),
            pltpu.SemaphoreType.DMA((4,)),
        ],
    )
    return out


def solution(mesh):
    in_specs = (
        P(("rows", "sub"), None),
        P(("rows", "sub")),
        P(("rows", "sub"), None),
        P("rows", None, None),
        P(None, ("rows", "sub"), None),
        P(),
    )
    out_specs = P(("rows", "sub"), None)

    return jax.shard_map(shards, mesh=mesh, in_specs=in_specs, out_specs=out_specs, check_vma=False)
```

```python
import functools

import jax
import jax.numpy as jnp
from jax import lax
from jax.experimental import pallas as pl
from jax.experimental.pallas import tpu as pltpu
from jax.sharding import PartitionSpec as P


FLOAT = jnp.float32
VMEM_LIMIT = 16 << 20


def halves(value):
    high = value.astype(jnp.bfloat16)
    return high, (value - high.astype(FLOAT)).astype(jnp.bfloat16)


def dot_parts(left, right, right_dim=0):
    mult = functools.partial(
        lax.dot_general,
        dimension_numbers=(((1,), (right_dim,)), ((), ())),
        preferred_element_type=FLOAT,
    )
    return mult(left[0], right[0]) + (mult(left[0], right[1]) + mult(left[1], right[0]))


def dot(left, right, right_dim=0):
    return dot_parts(halves(left), halves(right), right_dim)


def lanes(values):
    return values[0] if len(values) == 1 else jnp.concatenate(values, axis=1)


def column_scale(scale):
    size = scale.shape[1]
    return jnp.concatenate(
        [jnp.broadcast_to(scale[i : i + 1, :], (size, size)).T for i in range(scale.shape[0])], axis=0
    )


def core_side():
    return lax.rem(lax.axis_index("sub"), 2)


def at(index, size):
    return pl.ds(pl.multiple_of(index * size, 8), size)


def call(body, outs, *operands, flops, spaces=None, out_space=pltpu.VMEM, scratch=()):
    spaces = spaces or [pltpu.VMEM] * len(operands)
    size = sum(a.dtype.itemsize * a.size for a in operands)
    outs = [out if isinstance(out, jax.ShapeDtypeStruct) else jax.ShapeDtypeStruct(out, FLOAT) for out in outs]
    return pl.pallas_call(
        body,
        out_shape=outs,
        in_specs=[pl.BlockSpec(memory_space=space) for space in spaces],
        out_specs=[pl.BlockSpec(memory_space=out_space)] * len(outs),
        scratch_shapes=list(scratch),
        compiler_params=pltpu.CompilerParams(vmem_limit_bytes=VMEM_LIMIT),
        cost_estimate=pl.CostEstimate(flops=flops, bytes_accessed=size, transcendentals=0),
    )(*operands)


def pair(*shape):
    return [jax.ShapeDtypeStruct(shape, jnp.bfloat16)] * 2


def store(refs, value):
    for ref, part in zip(refs, halves(value)):
        ref[...] = part


def swap(array, axis, bit):
    return lax.ppermute(array, axis, [(i, i ^ 1 << bit) for i in range(lax.axis_size(axis))])


def partial_sums(array, axis, bits):
    bits = list(bits)
    if not bits:
        return [array]
    for bit in bits[:-1]:
        array = array + swap(array, axis, bit)
    return [array, swap(array, axis, bits[-1])]


def add_all(parts):
    return functools.reduce(lambda a, b: a + b, parts)


def shards(queries, row_scale, leaf_basis, leaf_cores, level_basis, level_cores):
    levels = level_basis.shape[0]
    count = levels + 1
    top = levels
    rows_here, rank = leaf_basis.shape
    columns = queries.shape[1]
    groups, sub = lax.axis_size("rows"), lax.axis_size("sub")
    heights = [None] + [levels + 1 - e for e in range(1, count)]
    widths = [1] + [groups // 2 ** heights[e] for e in range(1, count)]
    head = sum(w == 1 for w in widths)
    bits = [range(0)] + [
        range(widths[e - 1].bit_length() - 1, widths[e].bit_length() - 1) for e in range(1, count)
    ]
    blocks = [list(range(e + 1, count)) for e in range(count)]
    coarse = count - head
    leaf_bits = range(1, sub.bit_length() - 1)
    mine = columns // 2
    half = rank // 2
    small = 2 * 3 * rank**3

    scale = row_scale.reshape(-1, rank)
    starts = [sum(len(b) for b in blocks[:e]) * rank for e in range(count + 1)]

    def gram_body(*refs):
        sources, (out_ref, core_ref), (scale_ref, leaf_ref, level_ref, sems) = refs[:5], refs[5:7], refs[7:]
        scale_hbm, leaf_hbm, level_hbm, leaf_core_hbm, core_hbm = sources
        targets = [(scale_hbm, scale_ref), (leaf_hbm, leaf_ref)]
        targets += [(level_hbm.at[e], level_ref.at[e]) for e in reversed(range(levels))]
        place = lax.axis_index("rows")
        targets.append((leaf_core_hbm.at[0], core_ref.at[0]))
        for e in range(1, count):
            targets.append((core_hbm.at[2 ** heights[e] - 2 + place // widths[e]], core_ref.at[e]))
        copies = [pltpu.make_async_copy(a, b, sems.at[i]) for i, (a, b) in enumerate(targets)]
        for copy in copies:
            copy.start()
        for copy in copies[: 2 + levels]:
            copy.wait()
        vectors = [column_scale(scale_ref[...]) * leaf_ref[...]]
        vectors += [level_ref[levels - e] for e in range(1, count)]
        parts = [halves(v) for v in vectors]
        side = core_side()
        for e in range(count):
            group = ([e] if e >= head else []) + blocks[e]
            right = [lanes([parts[f][i] for f in group]) for i in range(2)]
            value = dot_parts(halves(vectors[e].T), right)
            for h in range(2):
                rows = value[h * half : (h + 1) * half]
                if e >= head:
                    place = starts[count] + (e - head) * rank
                    out_ref[at(h ^ side, half), place : place + rank] = rows[:, :rank]
                    rows = rows[:, rank:]
                if blocks[e]:
                    out_ref[at(h ^ side, half), starts[e] : starts[e + 1]] = rows
        for copy in copies[2 + levels :]:
            copy.wait()

    gram, cores = call(
        gram_body,
        [(rank, starts[count] + coarse * rank), (count, rank, rank)],
        *[
            pltpu.with_memory_space_constraint(array, pltpu.HBM)
            for array in (scale, leaf_basis, level_basis, leaf_cores, level_cores)
        ],
        flops=small * (starts[count] // rank + coarse) * rows_here // rank,
        spaces=[pltpu.HBM] * 5,
        scratch=[
            pltpu.VMEM(scale.shape, FLOAT),
            pltpu.VMEM(leaf_basis.shape, FLOAT),
            pltpu.VMEM(level_basis.shape, FLOAT),
            pltpu.SemaphoreType.DMA((2 + levels + count,)),
        ],
    )
    gram_chip = gram[:half] + swap(gram[half:], "sub", 0)
    early = add_all(partial_sums(gram_chip[:, : starts[count]], "sub", leaf_bits))
    diagonal = []
    for e in reversed(range(head, count)):
        place = starts[count] + (e - head) * rank
        diagonal = lanes([gram_chip[:, place : place + rank], *diagonal])
        diagonal = [add_all(partial_sums(diagonal, "rows", bits[e]))]
    diagonal = diagonal[0]

    def moment_body(scale_ref, queries_ref, leaf_ref, level_ref, out_ref, *basis_refs):
        spread = column_scale(scale_ref[...])
        right = halves(lanes([leaf_ref[...]] + [spread * level_ref[levels - e] for e in range(1, count)]))
        for basis_ref, part in zip(basis_refs, right):
            basis_ref[...] = part
        value = dot_parts(halves(queries_ref[...].T), right)
        side = core_side()
        for h in range(2):
            out_ref[at(h ^ side, mine), :] = value[h * mine : (h + 1) * mine]

    value, *basis = call(
        moment_body,
        [(columns, count * rank), *pair(rows_here, count * rank)],
        scale,
        queries,
        leaf_basis,
        level_basis,
        flops=small * count * 2 * rows_here // rank,
    )
    moment_chip = value[:mine] + swap(value[mine:], "sub", 0)
    moment_parts = partial_sums(moment_chip, "sub", leaf_bits)

    late_rows = columns // 2 + head * half

    def late_body(scale_ref, queries_ref, leaf_ref, level_ref, out_ref, *scaled_refs):
        spread = column_scale(scale_ref[...])
        vectors = spread * leaf_ref[...]
        side = core_side()
        scaled = halves(spread * vectors)
        for scaled_ref, part in zip(scaled_refs, scaled):
            scaled_ref[...] = part
        value = dot_parts(halves(queries_ref[...].T), scaled)
        for h in range(2):
            base = (h ^ side) * late_rows
            part = value[h * columns // 2 : (h + 1) * columns // 2]
            out_ref[pl.ds(pl.multiple_of(base, 8), columns // 2), :] = part
        for e in range(head):
            basis = vectors if e == 0 else level_ref[levels - e]
            value = dot(basis.T, basis)
            for h in range(2):
                base = (h ^ side) * late_rows + columns // 2 + e * half
                out_ref[pl.ds(pl.multiple_of(base, 8), half), :] = value[h * half : (h + 1) * half]

    late, *scaled = call(
        late_body,
        [(2 * late_rows, rank), *pair(rows_here, rank)],
        scale,
        queries,
        leaf_basis,
        level_basis,
        flops=small * (2 + head) * rows_here // rank,
    )
    late_chip = late[:late_rows] + swap(late[late_rows:], "sub", 0)

    def stacked(array, size):
        return [array[:, j : j + size] for j in range(0, array.shape[1], size)]

    late = jnp.concatenate([late_chip, *stacked(diagonal, rank)], axis=0)
    late_size = late.shape[0]
    late = add_all(partial_sums(late, "sub", leaf_bits))

    def product_body(group, own_ref, other_ref, core_ref, *refs):
        out_refs, stack_ref = refs[:-1], refs[-1]
        side = core_side()
        stack_ref[at(side, half), :] = own_ref[...]
        stack_ref[at(1 - side, half), :] = other_ref[...]
        base = starts[group[0]]
        for i, e in enumerate(group):
            block = stack_ref[:, starts[e] - base : starts[e + 1] - base]
            store(out_refs[2 * i : 2 * i + 2], dot(core_ref[e].T, block))

    def products(group, own):
        out = call(
            functools.partial(product_body, group),
            [part for e in group for part in pair(rank, starts[e + 1] - starts[e])],
            own,
            swap(own, "sub", 0),
            cores,
            flops=small * sum(len(blocks[e]) for e in group),
            scratch=[pltpu.VMEM((rank, own.shape[1]), FLOAT)],
        )
        return [out[2 * i : 2 * i + 2] for i in range(len(group))]

    factors = products(list(range(head)), early[:, : starts[head]])
    remaining = early[:, starts[head] :]
    for e in range(head, top):
        remaining = add_all(partial_sums(remaining, "rows", bits[e]))
        size = starts[e + 1] - starts[e]
        factors += products([e], remaining[:, :size])
        remaining = remaining[:, size:]

    def flat(group):
        return [part for factor in group for part in factor]

    def paired(refs):
        return [refs[i : i + 2] for i in range(0, len(refs), 2)]

    def take(factor, start, size):
        return [ref[:, start : start + size] for ref in factor]

    def head_body(*refs):
        part_refs, factor_refs = refs[: len(moment_parts)], paired(refs[len(moment_parts) : -2])
        own_ref, rest_ref = refs[-2:]
        rest = add_all([part[...] for part in part_refs])
        for e in range(head):
            own, rest = rest[:, :rank], rest[:, rank:]
            own_ref[e * mine : (e + 1) * mine, :] = own
            rest = rest - dot_parts(halves(own), take(factor_refs[e], 0, rest.shape[1]))
        rest_ref[...] = rest

    head_moments, rest = call(
        head_body,
        [(head * mine, rank), (mine, coarse * rank)],
        *moment_parts,
        *flat(factors[:head]),
        flops=small * sum(map(len, blocks[:head])),
    )
    late = jnp.concatenate([late, head_moments], axis=0)
    late_parts = [late, swap(late, "sub", 0)]

    def step_body(number, *refs):
        part_refs, factor, (own_ref, rest_ref) = refs[:number], refs[number:-2], refs[-2:]
        total = add_all([part[...] for part in part_refs])
        own, rest = total[:, :rank], total[:, rank:]
        own_ref[...] = own
        rest_ref[...] = rest - dot_parts(halves(own), take(factor, 0, rest.shape[1]))

    def scatter(parts, number, stack_ref):
        side = core_side()
        for part, place in zip(parts, (side, 1 - side)):
            for e in range(number):
                stack_ref[at(place, mine), e * rank : (e + 1) * rank] = part[e * mine : (e + 1) * mine, :]

    found = []
    for e in range(head, top):
        parts = partial_sums(rest, "rows", bits[e])
        own, rest = call(
            functools.partial(step_body, len(parts)),
            [(mine, rank), (mine, (top - e) * rank)],
            *parts,
            *factors[e],
            flops=small * (top - e),
        )
        found.append(own)
    found.append(rest)
    found[-1] = add_all(partial_sums(rest, "rows", bits[top]))
    found = jnp.concatenate(found, axis=0)
    found_parts = [found, swap(found, "sub", 0)]

    def answer_body(*refs):
        factor_refs, basis_refs, out_refs = paired(refs[:-4]), refs[-4:-2], refs[-2:]
        rows = {}
        for f in reversed(range(count)):
            if f + 1 < count:
                stack = jnp.concatenate([rows[g] for g in range(f + 1, count)], axis=0)
                row = -dot_parts(take(factor_refs[f], 0, stack.shape[0]), halves(stack))
            else:
                row = jnp.zeros((rank, coarse * rank), FLOAT)
            if f >= head:
                line = lax.broadcasted_iota(jnp.int32, row.shape, 0) + (f - head) * rank
                row = row + jnp.where(line == lax.broadcasted_iota(jnp.int32, row.shape, 1), 1.0, 0.0)
            rows[f] = row
        gains = jnp.concatenate([rows[f] for f in range(count)], axis=0)
        store(out_refs, dot_parts([ref[...] for ref in basis_refs], halves(gains)))

    answer = call(
        answer_body,
        pair(rows_here, coarse * rank),
        *flat(factors),
        *basis,
        flops=small * coarse * count * rows_here // rank,
    )

    def base_body(scale_ref, queries_ref, own_ref, other_ref, core_ref, *refs):
        factor_refs, basis_refs, scaled_refs = paired(refs[: 2 * head]), refs[2 * head : -7], refs[-7:-5]
        out_ref, *gain_refs, stack_ref, gram_ref = refs[-5:]
        scatter([own_ref.at[late_size:], other_ref.at[late_size:]], head, stack_ref)
        side = core_side()
        for late_ref, place in ((own_ref, side), (other_ref, 1 - side)):
            stack_ref[at(place, columns // 2), head * rank :] = late_ref[: columns // 2]
            for e in range(count):
                start = columns // 2 + e * half
                gram_ref[at(place, half), e * rank : (e + 1) * rank] = late_ref[start : start + half]
        products = [dot(core_ref[e].T, gram_ref[:, e * rank : (e + 1) * rank]) for e in range(count)]
        gains = [core_ref[e] + core_ref[e].T - dot(products[e], core_ref[e]) for e in range(1, count)]
        store(gain_refs, lanes(gains[head - 1 :]))
        moments = [stack_ref[:, e * rank : (e + 1) * rank] for e in range(head)]
        first = dot(moments[0], core_ref[0], 1)
        found = [dot(stack_ref[:, head * rank :], core_ref[0]) - dot(first, products[0], 1)]
        found += [dot(moments[e], gains[e - 1], 1) for e in range(1, head)]
        for e in reversed(range(head - 1)):
            size = (head - 1 - e) * rank
            found[e] = found[e] - dot_parts(halves(lanes(found[e + 1 :])), take(factor_refs[e], 0, size), 1)
        left = [lanes([a[...], b[:, : head * rank]]) for a, b in zip(scaled_refs, basis_refs)]
        square = column_scale(scale_ref[...] * scale_ref[...])
        square = lanes([square] * (columns // rank))
        out_ref[...] = square * queries_ref[...] - dot_parts(left, halves(lanes([first, *found])), 1)

    base, *gains = call(
        base_body,
        [(rows_here, columns), *pair(rank, coarse * rank)],
        scale,
        queries,
        *late_parts,
        cores,
        *flat(factors[:head]),
        *basis,
        *scaled,
        flops=small * 2 * (head + 1) * rows_here // rank,
        scratch=[pltpu.VMEM((columns, (head + 1) * rank), FLOAT), pltpu.VMEM((rank, count * rank), FLOAT)],
    )

    chunk = rows_here // 4

    def last_body(base_ref, high_ref, low_ref, *refs):
        gain_refs, (own_ref, other_ref, out_hbm, stack_ref, out_ref, sems) = refs[:2], refs[2:]
        scatter([own_ref, other_ref], coarse, stack_ref)
        right = []
        for e in range(coarse):
            where = slice(e * rank, (e + 1) * rank)
            right.append(dot_parts(halves(stack_ref[:, where]), [ref[:, where] for ref in gain_refs], 1))
        right = halves(lanes(right))
        copies = []
        for i in range(4):
            rows = pl.ds(i * chunk, chunk)
            out_ref[rows, :] = base_ref[rows, :] - dot_parts([high_ref[rows, :], low_ref[rows, :]], right, 1)
            copies.append(pltpu.make_async_copy(out_ref.at[rows, :], out_hbm.at[rows, :], sems.at[i]))
            copies[-1].start()
        for copy in copies:
            copy.wait()

    (out,) = call(
        last_body,
        [(rows_here, columns)],
        base,
        *answer,
        *gains,
        *found_parts,
        flops=small * 2 * coarse * rows_here // rank,
        out_space=pltpu.HBM,
        scratch=[
            pltpu.VMEM((columns, coarse * rank), FLOAT),
            pltpu.VMEM((rows_here, columns), FLOAT),
            pltpu.SemaphoreType.DMA((4,)),
        ],
    )
    return out


def solution(mesh):
    in_specs = (
        P(("rows", "sub"), None),
        P(("rows", "sub")),
        P(("rows", "sub"), None),
        P("rows", None, None),
        P(None, ("rows", "sub"), None),
        P(),
    )
    out_specs = P(("rows", "sub"), None)

    return jax.shard_map(shards, mesh=mesh, in_specs=in_specs, out_specs=out_specs, check_vma=False)
```

```python
import functools

import jax
import jax.numpy as jnp
from jax import lax
from jax.experimental import pallas as pl
from jax.experimental.pallas import tpu as pltpu
from jax.sharding import PartitionSpec as P


FLOAT = jnp.float32
VMEM_LIMIT = 16 << 20


def halves(value):
    high = value.astype(jnp.bfloat16)
    return high, (value - high.astype(FLOAT)).astype(jnp.bfloat16)


def dot_parts(left, right, right_dim=0):
    mult = functools.partial(
        lax.dot_general,
        dimension_numbers=(((1,), (right_dim,)), ((), ())),
        preferred_element_type=FLOAT,
    )
    return mult(left[0], right[0]) + (mult(left[0], right[1]) + mult(left[1], right[0]))


def dot(left, right, right_dim=0):
    return dot_parts(halves(left), halves(right), right_dim)


def lanes(values):
    return values[0] if len(values) == 1 else jnp.concatenate(values, axis=1)


def column_scale(scale):
    size = scale.shape[1]
    return jnp.concatenate(
        [jnp.broadcast_to(scale[i : i + 1, :], (size, size)).T for i in range(scale.shape[0])], axis=0
    )


def core_side():
    return lax.rem(lax.axis_index("sub"), 2)


def at(index, size):
    return pl.ds(pl.multiple_of(index * size, 8), size)


def call(body, outs, *operands, flops, spaces=None, out_space=pltpu.VMEM, scratch=()):
    spaces = spaces or [pltpu.VMEM] * len(operands)
    size = sum(a.dtype.itemsize * a.size for a in operands)
    outs = [out if isinstance(out, jax.ShapeDtypeStruct) else jax.ShapeDtypeStruct(out, FLOAT) for out in outs]
    return pl.pallas_call(
        body,
        out_shape=outs,
        in_specs=[pl.BlockSpec(memory_space=space) for space in spaces],
        out_specs=[pl.BlockSpec(memory_space=out_space)] * len(outs),
        scratch_shapes=list(scratch),
        compiler_params=pltpu.CompilerParams(vmem_limit_bytes=VMEM_LIMIT),
        cost_estimate=pl.CostEstimate(flops=flops, bytes_accessed=size, transcendentals=0),
    )(*operands)


def pair(*shape):
    return [jax.ShapeDtypeStruct(shape, jnp.bfloat16)] * 2


def store(refs, value):
    for ref, part in zip(refs, halves(value)):
        ref[...] = part


def swap(array, axis, bit):
    return lax.ppermute(array, axis, [(i, i ^ 1 << bit) for i in range(lax.axis_size(axis))])


def partial_sums(array, axis, bits):
    bits = list(bits)
    if not bits:
        return [array]
    for bit in bits[:-1]:
        array = array + swap(array, axis, bit)
    return [array, swap(array, axis, bits[-1])]


def add_all(parts):
    return functools.reduce(lambda a, b: a + b, parts)


def shards(queries, row_scale, leaf_basis, leaf_cores, level_basis, level_cores):
    levels = level_basis.shape[0]
    count = levels + 1
    top = levels
    rows_here, rank = leaf_basis.shape
    columns = queries.shape[1]
    groups, sub = lax.axis_size("rows"), lax.axis_size("sub")
    heights = [None] + [levels + 1 - e for e in range(1, count)]
    widths = [1] + [groups // 2 ** heights[e] for e in range(1, count)]
    head = sum(w == 1 for w in widths)
    bits = [range(0)] + [
        range(widths[e - 1].bit_length() - 1, widths[e].bit_length() - 1) for e in range(1, count)
    ]
    blocks = [list(range(e + 1, count)) for e in range(count)]
    coarse = count - head
    leaf_bits = range(1, sub.bit_length() - 1)
    mine = columns // 2
    half = rank // 2
    batches = 2
    batch = mine // batches
    small = 2 * 3 * rank**3

    scale = row_scale.reshape(-1, rank)
    starts = [sum(len(b) for b in blocks[:e]) * rank for e in range(count + 1)]

    def gram_body(*refs):
        scale_hbm, leaf_hbm, level_hbm, queries_hbm, leaf_core_hbm, core_hbm = refs[:6]
        out_ref, scale_ref, leaf_ref, level_ref, queries_ref, core_ref, sems = refs[6:]
        targets = [(scale_hbm, scale_ref), (leaf_hbm, leaf_ref)]
        targets += [(level_hbm.at[e], level_ref.at[e]) for e in reversed(range(levels))]
        place = lax.axis_index("rows")
        targets += [(queries_hbm, queries_ref), (leaf_core_hbm.at[0], core_ref.at[0])]
        for e in range(1, count):
            targets.append((core_hbm.at[2 ** heights[e] - 2 + place // widths[e]], core_ref.at[e]))
        copies = [pltpu.make_async_copy(a, b, sems.at[i]) for i, (a, b) in enumerate(targets)]
        for copy in copies:
            copy.start()
        for copy in copies[: 2 + levels]:
            copy.wait()
        vectors = [column_scale(scale_ref[...]) * leaf_ref[...]]
        vectors += [level_ref[levels - e] for e in range(1, count)]
        parts = [halves(v) for v in vectors]
        side = core_side()
        for e in range(count):
            group = ([e] if e >= head else []) + blocks[e]
            right = [lanes([parts[f][i] for f in group]) for i in range(2)]
            value = dot_parts(halves(vectors[e].T), right)
            for h in range(2):
                rows = value[h * half : (h + 1) * half]
                if e >= head:
                    place = starts[count] + (e - head) * rank
                    out_ref[at(h ^ side, half), place : place + rank] = rows[:, :rank]
                    rows = rows[:, rank:]
                if blocks[e]:
                    out_ref[at(h ^ side, half), starts[e] : starts[e + 1]] = rows
        for copy in copies[2 + levels :]:
            copy.wait()

    gram, scale, leaf_basis, level_basis, queries, cores = call(
        gram_body,
        [
            (rank, starts[count] + coarse * rank),
            *[array.shape for array in (scale, leaf_basis, level_basis, queries)],
            (count, rank, rank),
        ],
        *[
            pltpu.with_memory_space_constraint(array, pltpu.HBM)
            for array in (scale, leaf_basis, level_basis, queries, leaf_cores, level_cores)
        ],
        flops=small * (starts[count] // rank + coarse) * rows_here // rank,
        spaces=[pltpu.HBM] * 6,
        scratch=[pltpu.SemaphoreType.DMA((3 + levels + count,))],
    )
    gram_chip = gram[:half] + swap(gram[half:], "sub", 0)
    early = add_all(partial_sums(gram_chip[:, : starts[count]], "sub", leaf_bits))
    diagonal = []
    for e in reversed(range(head, count)):
        place = starts[count] + (e - head) * rank
        diagonal = lanes([gram_chip[:, place : place + rank], *diagonal])
        diagonal = [add_all(partial_sums(diagonal, "rows", bits[e]))]
    diagonal = diagonal[0]

    def moment_body(scale_ref, queries_ref, leaf_ref, level_ref, out_ref, *basis_refs):
        spread = column_scale(scale_ref[...])
        right = halves(lanes([leaf_ref[...]] + [spread * level_ref[levels - e] for e in range(1, count)]))
        for basis_ref, part in zip(basis_refs, right):
            basis_ref[...] = part
        value = dot_parts(halves(queries_ref[...].T), right)
        side = core_side()
        for h in range(2):
            out_ref[at(h ^ side, mine), :] = value[h * mine : (h + 1) * mine]

    value, *basis = call(
        moment_body,
        [(columns, count * rank), *pair(rows_here, count * rank)],
        scale,
        queries,
        leaf_basis,
        level_basis,
        flops=small * count * 2 * rows_here // rank,
    )
    moment_chip = value[:mine] + swap(value[mine:], "sub", 0)
    moment_parts = [partial_sums(moment_chip[b * batch : (b + 1) * batch], "sub", leaf_bits) for b in range(batches)]

    late_rows = columns // 2 + head * half

    def late_body(scale_ref, queries_ref, leaf_ref, level_ref, out_ref, *scaled_refs):
        spread = column_scale(scale_ref[...])
        vectors = spread * leaf_ref[...]
        side = core_side()
        scaled = halves(spread * vectors)
        for scaled_ref, part in zip(scaled_refs, scaled):
            scaled_ref[...] = part
        value = dot_parts(halves(queries_ref[...].T), scaled)
        for h in range(2):
            base = (h ^ side) * late_rows
            part = value[h * columns // 2 : (h + 1) * columns // 2]
            out_ref[pl.ds(pl.multiple_of(base, 8), columns // 2), :] = part
        for e in range(head):
            basis = vectors if e == 0 else level_ref[levels - e]
            value = dot(basis.T, basis)
            for h in range(2):
                base = (h ^ side) * late_rows + columns // 2 + e * half
                out_ref[pl.ds(pl.multiple_of(base, 8), half), :] = value[h * half : (h + 1) * half]

    late, *scaled = call(
        late_body,
        [(2 * late_rows, rank), *pair(rows_here, rank)],
        scale,
        queries,
        leaf_basis,
        level_basis,
        flops=small * (2 + head) * rows_here // rank,
    )
    late_chip = late[:late_rows] + swap(late[late_rows:], "sub", 0)

    def stacked(array, size):
        return [array[:, j : j + size] for j in range(0, array.shape[1], size)]

    late = jnp.concatenate([late_chip, *stacked(diagonal, rank)], axis=0)
    late_size = late.shape[0]
    late = add_all(partial_sums(late, "sub", leaf_bits))

    def product_body(group, own_ref, other_ref, core_ref, *refs):
        out_refs, stack_ref = refs[:-1], refs[-1]
        side = core_side()
        stack_ref[at(side, half), :] = own_ref[...]
        stack_ref[at(1 - side, half), :] = other_ref[...]
        base = starts[group[0]]
        for i, e in enumerate(group):
            block = stack_ref[:, starts[e] - base : starts[e + 1] - base]
            store(out_refs[2 * i : 2 * i + 2], dot(core_ref[e].T, block))

    def products(group, own):
        out = call(
            functools.partial(product_body, group),
            [part for e in group for part in pair(rank, starts[e + 1] - starts[e])],
            own,
            swap(own, "sub", 0),
            cores,
            flops=small * sum(len(blocks[e]) for e in group),
            scratch=[pltpu.VMEM((rank, own.shape[1]), FLOAT)],
        )
        return [out[2 * i : 2 * i + 2] for i in range(len(group))]

    factors = products(list(range(head)), early[:, : starts[head]])
    remaining = early[:, starts[head] :]
    for e in range(head, top):
        remaining = add_all(partial_sums(remaining, "rows", bits[e]))
        size = starts[e + 1] - starts[e]
        factors += products([e], remaining[:, :size])
        remaining = remaining[:, size:]

    def flat(group):
        return [part for factor in group for part in factor]

    def paired(refs):
        return [refs[i : i + 2] for i in range(0, len(refs), 2)]

    def take(factor, start, size):
        return [ref[:, start : start + size] for ref in factor]

    def head_body(number, *refs):
        part_refs, factor_refs, (own_ref, rest_ref) = refs[:number], paired(refs[number:-2]), refs[-2:]
        rest = add_all([part[...] for part in part_refs])
        for e in range(head):
            own, rest = rest[:, :rank], rest[:, rank:]
            own_ref[e * batch : (e + 1) * batch, :] = own
            rest = rest - dot_parts(halves(own), take(factor_refs[e], 0, rest.shape[1]))
        rest_ref[...] = rest

    def step_body(number, *refs):
        part_refs, factor, (own_ref, rest_ref) = refs[:number], refs[number:-2], refs[-2:]
        total = add_all([part[...] for part in part_refs])
        own, rest = total[:, :rank], total[:, rank:]
        own_ref[...] = own
        rest_ref[...] = rest - dot_parts(halves(own), take(factor, 0, rest.shape[1]))

    def scatter(parts, number, stack_ref):
        side = core_side()
        for b, part in enumerate(parts):
            for ref, place in zip(part, (side, 1 - side)):
                for e in range(number):
                    stack_ref[at(place * batches + b, batch), e * rank : (e + 1) * rank] = ref[
                        e * batch : (e + 1) * batch, :
                    ]

    head_moments, found_parts = [], []
    for b in range(batches):
        own, rest = call(
            functools.partial(head_body, len(moment_parts[b])),
            [(head * batch, rank), (batch, coarse * rank)],
            *moment_parts[b],
            *flat(factors[:head]),
            flops=small * sum(map(len, blocks[:head])) // batches,
        )
        head_moments.append(own)
        found = []
        for e in range(head, top):
            parts = partial_sums(rest, "rows", bits[e])
            own, rest = call(
                functools.partial(step_body, len(parts)),
                [(batch, rank), (batch, (top - e) * rank)],
                *parts,
                *factors[e],
                flops=small * (top - e) // batches,
            )
            found.append(own)
        found.append(add_all(partial_sums(rest, "rows", bits[top])))
        found = jnp.concatenate(found, axis=0)
        found_parts.append([found, swap(found, "sub", 0)])
    late = jnp.concatenate([late, *head_moments], axis=0)
    late_parts = [late, swap(late, "sub", 0)]

    def answer_body(*refs):
        factor_refs, basis_refs, out_refs = paired(refs[:-4]), refs[-4:-2], refs[-2:]
        rows = {}
        for f in reversed(range(count)):
            if f + 1 < count:
                stack = jnp.concatenate([rows[g] for g in range(f + 1, count)], axis=0)
                row = -dot_parts(take(factor_refs[f], 0, stack.shape[0]), halves(stack))
            else:
                row = jnp.zeros((rank, coarse * rank), FLOAT)
            if f >= head:
                line = lax.broadcasted_iota(jnp.int32, row.shape, 0) + (f - head) * rank
                row = row + jnp.where(line == lax.broadcasted_iota(jnp.int32, row.shape, 1), 1.0, 0.0)
            rows[f] = row
        gains = jnp.concatenate([rows[f] for f in range(count)], axis=0)
        store(out_refs, dot_parts([ref[...] for ref in basis_refs], halves(gains)))

    answer = call(
        answer_body,
        pair(rows_here, coarse * rank),
        *flat(factors),
        *basis,
        flops=small * coarse * count * rows_here // rank,
    )

    def base_body(scale_ref, queries_ref, own_ref, other_ref, core_ref, *refs):
        factor_refs, basis_refs, scaled_refs = paired(refs[: 2 * head]), refs[2 * head : -7], refs[-7:-5]
        out_ref, *gain_refs, stack_ref, gram_ref = refs[-5:]
        pieces = [pl.ds(late_size + b * head * batch, head * batch) for b in range(batches)]
        scatter([(own_ref.at[piece], other_ref.at[piece]) for piece in pieces], head, stack_ref)
        side = core_side()
        for late_ref, place in ((own_ref, side), (other_ref, 1 - side)):
            stack_ref[at(place, columns // 2), head * rank :] = late_ref[: columns // 2]
            for e in range(count):
                start = columns // 2 + e * half
                gram_ref[at(place, half), e * rank : (e + 1) * rank] = late_ref[start : start + half]
        products = [dot(core_ref[e].T, gram_ref[:, e * rank : (e + 1) * rank]) for e in range(count)]
        gains = [core_ref[e] + core_ref[e].T - dot(products[e], core_ref[e]) for e in range(1, count)]
        store(gain_refs, lanes(gains[head - 1 :]))
        moments = [stack_ref[:, e * rank : (e + 1) * rank] for e in range(head)]
        first = dot(moments[0], core_ref[0], 1)
        found = [dot(stack_ref[:, head * rank :], core_ref[0]) - dot(first, products[0], 1)]
        found += [dot(moments[e], gains[e - 1], 1) for e in range(1, head)]
        for e in reversed(range(head - 1)):
            size = (head - 1 - e) * rank
            found[e] = found[e] - dot_parts(halves(lanes(found[e + 1 :])), take(factor_refs[e], 0, size), 1)
        left = [lanes([a[...], b[:, : head * rank]]) for a, b in zip(scaled_refs, basis_refs)]
        square = column_scale(scale_ref[...] * scale_ref[...])
        square = lanes([square] * (columns // rank))
        out_ref[...] = square * queries_ref[...] - dot_parts(left, halves(lanes([first, *found])), 1)

    base, *gains = call(
        base_body,
        [(rows_here, columns), *pair(rank, coarse * rank)],
        scale,
        queries,
        *late_parts,
        cores,
        *flat(factors[:head]),
        *basis,
        *scaled,
        flops=small * 2 * (head + 1) * rows_here // rank,
        scratch=[pltpu.VMEM((columns, (head + 1) * rank), FLOAT), pltpu.VMEM((rank, count * rank), FLOAT)],
    )

    def last_body(base_ref, high_ref, low_ref, *refs):
        gain_refs, part_refs, (out_ref, stack_ref) = refs[:2], paired(refs[2:-2]), refs[-2:]
        scatter(part_refs, coarse, stack_ref)
        right = []
        for e in range(coarse):
            where = slice(e * rank, (e + 1) * rank)
            right.append(dot_parts(halves(stack_ref[:, where]), [ref[:, where] for ref in gain_refs], 1))
        out_ref[...] = base_ref[...] - dot_parts([high_ref[...], low_ref[...]], halves(lanes(right)), 1)

    (out,) = call(
        last_body,
        [(rows_here, columns)],
        base,
        *answer,
        *gains,
        *flat(found_parts),
        flops=small * 2 * coarse * rows_here // rank,
        scratch=[pltpu.VMEM((columns, coarse * rank), FLOAT)],
    )
    return out


def solution(mesh):
    in_specs = (
        P(("rows", "sub"), None),
        P(("rows", "sub")),
        P(("rows", "sub"), None),
        P("rows", None, None),
        P(None, ("rows", "sub"), None),
        P(),
    )
    out_specs = P(("rows", "sub"), None)

    return jax.shard_map(shards, mesh=mesh, in_specs=in_specs, out_specs=out_specs, check_vma=False)
```

```python
import functools

import jax
import jax.numpy as jnp
from jax import lax
from jax.experimental import pallas as pl
from jax.experimental.pallas import tpu as pltpu
from jax.sharding import PartitionSpec as P


FLOAT = jnp.float32
VMEM_LIMIT = 16 << 20


def halves(value):
    high = value.astype(jnp.bfloat16)
    return high, (value - high.astype(FLOAT)).astype(jnp.bfloat16)


def dot_parts(left, right, right_dim=0):
    mult = functools.partial(
        lax.dot_general,
        dimension_numbers=(((1,), (right_dim,)), ((), ())),
        preferred_element_type=FLOAT,
    )
    return mult(left[0], right[0]) + (mult(left[0], right[1]) + mult(left[1], right[0]))


def dot(left, right, right_dim=0):
    return dot_parts(halves(left), halves(right), right_dim)


def lanes(values):
    return values[0] if len(values) == 1 else jnp.concatenate(values, axis=1)


def column_scale(scale):
    size = scale.shape[1]
    return jnp.concatenate(
        [jnp.broadcast_to(scale[i : i + 1, :], (size, size)).T for i in range(scale.shape[0])], axis=0
    )


def core_side():
    return lax.rem(lax.axis_index("sub"), 2)


def at(index, size):
    return pl.ds(pl.multiple_of(index * size, 8), size)


def call(body, outs, *operands, flops, spaces=None, out_space=pltpu.VMEM, scratch=()):
    spaces = spaces or [pltpu.VMEM] * len(operands)
    size = sum(a.dtype.itemsize * a.size for a in operands)
    outs = [out if isinstance(out, jax.ShapeDtypeStruct) else jax.ShapeDtypeStruct(out, FLOAT) for out in outs]
    return pl.pallas_call(
        body,
        out_shape=outs,
        in_specs=[pl.BlockSpec(memory_space=space) for space in spaces],
        out_specs=[pl.BlockSpec(memory_space=out_space)] * len(outs),
        scratch_shapes=list(scratch),
        compiler_params=pltpu.CompilerParams(vmem_limit_bytes=VMEM_LIMIT),
        cost_estimate=pl.CostEstimate(flops=flops, bytes_accessed=size, transcendentals=0),
    )(*operands)


def pair(*shape):
    return [jax.ShapeDtypeStruct(shape, jnp.bfloat16)] * 2


def store(refs, value):
    for ref, part in zip(refs, halves(value)):
        ref[...] = part


def swap(array, axis, bit):
    return lax.ppermute(array, axis, [(i, i ^ 1 << bit) for i in range(lax.axis_size(axis))])


def partial_sums(array, axis, bits):
    bits = list(bits)
    if not bits:
        return [array]
    for bit in bits[:-1]:
        array = array + swap(array, axis, bit)
    return [array, swap(array, axis, bits[-1])]


def add_all(parts):
    return functools.reduce(lambda a, b: a + b, parts)


def shards(queries, row_scale, leaf_basis, leaf_cores, level_basis, level_cores):
    levels = level_basis.shape[0]
    count = levels + 1
    top = levels
    rows_here, rank = leaf_basis.shape
    columns = queries.shape[1]
    nodes, sub = lax.axis_size("rows"), lax.axis_size("sub")
    heights = [None] + [levels + 1 - e for e in range(1, count)]
    widths = [1] + [nodes // 2 ** heights[e] for e in range(1, count)]
    head = sum(w == 1 for w in widths)
    bits = [range(0)] + [
        range(widths[e - 1].bit_length() - 1, widths[e].bit_length() - 1) for e in range(1, count)
    ]
    blocks = [list(range(e + 1, count)) for e in range(count)]
    coarse = count - head
    leaf_bits = range(1, sub.bit_length() - 1)
    mine = columns // 2
    half = rank // 2
    batches = 2
    batch = mine // batches
    small = 2 * 3 * rank**3

    scale = row_scale.reshape(-1, rank)
    groups = [([e] if e >= head else []) + blocks[e] for e in range(count)]
    starts = [sum(len(b) for b in groups[:e]) * rank for e in range(count + 1)]

    def gram_body(*refs):
        scale_hbm, leaf_hbm, level_hbm, queries_hbm, leaf_core_hbm, core_hbm = refs[:6]
        out_ref, scale_ref, leaf_ref, level_ref, queries_ref, core_ref, sems = refs[6:]
        targets = [(scale_hbm, scale_ref), (leaf_hbm, leaf_ref)]
        targets += [(level_hbm.at[e], level_ref.at[e]) for e in reversed(range(levels))]
        place = lax.axis_index("rows")
        targets += [(queries_hbm, queries_ref), (leaf_core_hbm.at[0], core_ref.at[0])]
        for e in range(1, count):
            targets.append((core_hbm.at[2 ** heights[e] - 2 + place // widths[e]], core_ref.at[e]))
        copies = [pltpu.make_async_copy(a, b, sems.at[i]) for i, (a, b) in enumerate(targets)]
        for copy in copies:
            copy.start()
        for copy in copies[: 2 + levels]:
            copy.wait()
        vectors = [column_scale(scale_ref[...]) * leaf_ref[...]]
        vectors += [level_ref[levels - e] for e in range(1, count)]
        parts = [halves(v) for v in vectors]
        side = core_side()
        for e in range(count):
            right = [lanes([parts[f][i] for f in groups[e]]) for i in range(2)]
            value = dot_parts(halves(vectors[e].T), right)
            for h in range(2):
                out_ref[at(h ^ side, half), starts[e] : starts[e + 1]] = value[h * half : (h + 1) * half]
        for copy in copies[2 + levels :]:
            copy.wait()

    gram, scale, leaf_basis, level_basis, queries, cores = call(
        gram_body,
        [
            (rank, starts[count]),
            *[array.shape for array in (scale, leaf_basis, level_basis, queries)],
            (count, rank, rank),
        ],
        *[
            pltpu.with_memory_space_constraint(array, pltpu.HBM)
            for array in (scale, leaf_basis, level_basis, queries, leaf_cores, level_cores)
        ],
        flops=small * starts[count] // rank * rows_here // rank,
        spaces=[pltpu.HBM] * 6,
        scratch=[pltpu.SemaphoreType.DMA((3 + levels + count,))],
    )
    gram_chip = gram[:half] + swap(gram[half:], "sub", 0)
    early = add_all(partial_sums(gram_chip[:, : starts[head]], "sub", leaf_bits))
    remaining, diagonal, coupling = gram_chip[:, starts[head] :], [], []
    for e in range(head, count):
        remaining = add_all(partial_sums(remaining, "rows", bits[e]))
        size = starts[e + 1] - starts[e]
        diagonal.append(remaining[:, :rank])
        coupling.append(remaining[:, rank:size])
        remaining = remaining[:, size:]
    coupling = lanes(coupling[:-1])

    def moment_body(scale_ref, queries_ref, leaf_ref, level_ref, out_ref, *basis_refs):
        spread = column_scale(scale_ref[...])
        right = halves(lanes([leaf_ref[...]] + [spread * level_ref[levels - e] for e in range(1, count)]))
        for basis_ref, part in zip(basis_refs, right):
            basis_ref[...] = part
        value = dot_parts(halves(queries_ref[...].T), right)
        side = core_side()
        for h in range(2):
            out_ref[at(h ^ side, mine), :] = value[h * mine : (h + 1) * mine]

    value, *basis = call(
        moment_body,
        [(columns, count * rank), *pair(rows_here, count * rank)],
        scale,
        queries,
        leaf_basis,
        level_basis,
        flops=small * count * 2 * rows_here // rank,
    )
    moment_chip = value[:mine] + swap(value[mine:], "sub", 0)
    moment_parts = [moment_chip[b * batch : (b + 1) * batch] for b in range(batches)]
    moment_parts[-1] = lanes([moment_parts[-1], coupling])
    moment_parts = [partial_sums(moment_parts[b], "sub", leaf_bits) for b in range(batches)]
    coupling = add_all([part[:, count * rank :] for part in moment_parts[-1]])

    late_rows = columns // 2 + head * half

    def late_body(scale_ref, queries_ref, leaf_ref, level_ref, out_ref, *scaled_refs):
        spread = column_scale(scale_ref[...])
        vectors = spread * leaf_ref[...]
        side = core_side()
        scaled = halves(spread * vectors)
        for scaled_ref, part in zip(scaled_refs, scaled):
            scaled_ref[...] = part
        value = dot_parts(halves(queries_ref[...].T), scaled)
        for h in range(2):
            base = (h ^ side) * late_rows
            part = value[h * columns // 2 : (h + 1) * columns // 2]
            out_ref[pl.ds(pl.multiple_of(base, 8), columns // 2), :] = part
        for e in range(head):
            basis = vectors if e == 0 else level_ref[levels - e]
            value = dot(basis.T, basis)
            for h in range(2):
                base = (h ^ side) * late_rows + columns // 2 + e * half
                out_ref[pl.ds(pl.multiple_of(base, 8), half), :] = value[h * half : (h + 1) * half]

    late, *scaled = call(
        late_body,
        [(2 * late_rows, rank), *pair(rows_here, rank)],
        scale,
        queries,
        leaf_basis,
        level_basis,
        flops=small * (2 + head) * rows_here // rank,
    )
    late_chip = late[:late_rows] + swap(late[late_rows:], "sub", 0)

    late = jnp.concatenate([late_chip, *diagonal], axis=0)
    late_size = late.shape[0]
    late = add_all(partial_sums(late, "sub", leaf_bits))

    def product_body(group, own_ref, other_ref, core_ref, *refs):
        out_refs, stack_ref = refs[:-1], refs[-1]
        side = core_side()
        stack_ref[at(side, half), :] = own_ref[...]
        stack_ref[at(1 - side, half), :] = other_ref[...]
        place = 0
        for i, e in enumerate(group):
            block = stack_ref[:, place : place + len(blocks[e]) * rank]
            store(out_refs[2 * i : 2 * i + 2], dot(core_ref[e].T, block))
            place += len(blocks[e]) * rank

    def products(group, own):
        out = call(
            functools.partial(product_body, group),
            [part for e in group for part in pair(rank, len(blocks[e]) * rank)],
            own,
            swap(own, "sub", 0),
            cores,
            flops=small * sum(len(blocks[e]) for e in group),
            scratch=[pltpu.VMEM((rank, own.shape[1]), FLOAT)],
        )
        return [out[2 * i : 2 * i + 2] for i in range(len(group))]

    factors = products(list(range(head)), early)
    factors += products(list(range(head, top)), coupling)

    def flat(group):
        return [part for factor in group for part in factor]

    def paired(refs):
        return [refs[i : i + 2] for i in range(0, len(refs), 2)]

    def take(factor, start, size):
        return [ref[:, start : start + size] for ref in factor]

    def head_body(number, *refs):
        part_refs, factor_refs, (own_ref, rest_ref) = refs[:number], paired(refs[number:-2]), refs[-2:]
        rest = add_all([part[:, : count * rank] for part in part_refs])
        for e in range(head):
            own, rest = rest[:, :rank], rest[:, rank:]
            own_ref[e * batch : (e + 1) * batch, :] = own
            rest = rest - dot_parts(halves(own), take(factor_refs[e], 0, rest.shape[1]))
        rest_ref[...] = rest

    def step_body(number, *refs):
        part_refs, factor, (own_ref, rest_ref) = refs[:number], refs[number:-2], refs[-2:]
        total = add_all([part[...] for part in part_refs])
        own, rest = total[:, :rank], total[:, rank:]
        own_ref[...] = own
        rest_ref[...] = rest - dot_parts(halves(own), take(factor, 0, rest.shape[1]))

    def scatter(parts, number, stack_ref):
        side = core_side()
        for b, part in enumerate(parts):
            for ref, place in zip(part, (side, 1 - side)):
                for e in range(number):
                    stack_ref[at(place * batches + b, batch), e * rank : (e + 1) * rank] = ref[
                        e * batch : (e + 1) * batch, :
                    ]

    head_moments, found_parts = [], []
    for b in range(batches):
        own, rest = call(
            functools.partial(head_body, len(moment_parts[b])),
            [(head * batch, rank), (batch, coarse * rank)],
            *moment_parts[b],
            *flat(factors[:head]),
            flops=small * sum(map(len, blocks[:head])) // batches,
        )
        head_moments.append(own)
        found = []
        for e in range(head, top):
            parts = partial_sums(rest, "rows", bits[e])
            own, rest = call(
                functools.partial(step_body, len(parts)),
                [(batch, rank), (batch, (top - e) * rank)],
                *parts,
                *factors[e],
                flops=small * (top - e) // batches,
            )
            found.append(own)
        found.append(add_all(partial_sums(rest, "rows", bits[top])))
        found = jnp.concatenate(found, axis=0)
        found_parts.append([found, swap(found, "sub", 0)])
    late = jnp.concatenate([late, *head_moments], axis=0)
    late_parts = [late, swap(late, "sub", 0)]

    def answer_body(*refs):
        factor_refs, basis_refs, out_refs = paired(refs[:-4]), refs[-4:-2], refs[-2:]
        rows = {}
        for f in reversed(range(count)):
            if f + 1 < count:
                stack = jnp.concatenate([rows[g] for g in range(f + 1, count)], axis=0)
                row = -dot_parts(take(factor_refs[f], 0, stack.shape[0]), halves(stack))
            else:
                row = jnp.zeros((rank, coarse * rank), FLOAT)
            if f >= head:
                line = lax.broadcasted_iota(jnp.int32, row.shape, 0) + (f - head) * rank
                row = row + jnp.where(line == lax.broadcasted_iota(jnp.int32, row.shape, 1), 1.0, 0.0)
            rows[f] = row
        gains = jnp.concatenate([rows[f] for f in range(count)], axis=0)
        store(out_refs, dot_parts([ref[...] for ref in basis_refs], halves(gains)))

    answer = call(
        answer_body,
        pair(rows_here, coarse * rank),
        *flat(factors),
        *basis,
        flops=small * coarse * count * rows_here // rank,
    )

    def base_body(scale_ref, queries_ref, own_ref, other_ref, core_ref, *refs):
        factor_refs, basis_refs, scaled_refs = paired(refs[: 2 * head]), refs[2 * head : -7], refs[-7:-5]
        out_ref, *gain_refs, stack_ref, gram_ref = refs[-5:]
        pieces = [pl.ds(late_size + b * head * batch, head * batch) for b in range(batches)]
        scatter([(own_ref.at[piece], other_ref.at[piece]) for piece in pieces], head, stack_ref)
        side = core_side()
        for late_ref, place in ((own_ref, side), (other_ref, 1 - side)):
            stack_ref[at(place, columns // 2), head * rank :] = late_ref[: columns // 2]
            for e in range(count):
                start = columns // 2 + e * half
                gram_ref[at(place, half), e * rank : (e + 1) * rank] = late_ref[start : start + half]
        products = [dot(core_ref[e].T, gram_ref[:, e * rank : (e + 1) * rank]) for e in range(count)]
        gains = [core_ref[e] + core_ref[e].T - dot(products[e], core_ref[e]) for e in range(1, count)]
        store(gain_refs, lanes(gains[head - 1 :]))
        moments = [stack_ref[:, e * rank : (e + 1) * rank] for e in range(head)]
        first = dot(moments[0], core_ref[0], 1)
        found = [dot(stack_ref[:, head * rank :], core_ref[0]) - dot(first, products[0], 1)]
        found += [dot(moments[e], gains[e - 1], 1) for e in range(1, head)]
        for e in reversed(range(head - 1)):
            size = (head - 1 - e) * rank
            found[e] = found[e] - dot_parts(halves(lanes(found[e + 1 :])), take(factor_refs[e], 0, size), 1)
        left = [lanes([a[...], b[:, : head * rank]]) for a, b in zip(scaled_refs, basis_refs)]
        square = column_scale(scale_ref[...] * scale_ref[...])
        square = lanes([square] * (columns // rank))
        out_ref[...] = square * queries_ref[...] - dot_parts(left, halves(lanes([first, *found])), 1)

    base, *gains = call(
        base_body,
        [(rows_here, columns), *pair(rank, coarse * rank)],
        scale,
        queries,
        *late_parts,
        cores,
        *flat(factors[:head]),
        *basis,
        *scaled,
        flops=small * 2 * (head + 1) * rows_here // rank,
        scratch=[pltpu.VMEM((columns, (head + 1) * rank), FLOAT), pltpu.VMEM((rank, count * rank), FLOAT)],
    )

    def last_body(base_ref, high_ref, low_ref, *refs):
        gain_refs, part_refs, (out_ref, stack_ref) = refs[:2], paired(refs[2:-2]), refs[-2:]
        scatter(part_refs, coarse, stack_ref)
        right = []
        for e in range(coarse):
            where = slice(e * rank, (e + 1) * rank)
            right.append(dot_parts(halves(stack_ref[:, where]), [ref[:, where] for ref in gain_refs], 1))
        out_ref[...] = base_ref[...] - dot_parts([high_ref[...], low_ref[...]], halves(lanes(right)), 1)

    (out,) = call(
        last_body,
        [(rows_here, columns)],
        base,
        *answer,
        *gains,
        *flat(found_parts),
        flops=small * 2 * coarse * rows_here // rank,
        scratch=[pltpu.VMEM((columns, coarse * rank), FLOAT)],
    )
    return out


def solution(mesh):
    in_specs = (
        P(("rows", "sub"), None),
        P(("rows", "sub")),
        P(("rows", "sub"), None),
        P("rows", None, None),
        P(None, ("rows", "sub"), None),
        P(),
    )
    out_specs = P(("rows", "sub"), None)

    return jax.shard_map(shards, mesh=mesh, in_specs=in_specs, out_specs=out_specs, check_vma=False)
```

```python
import functools

import jax
import jax.numpy as jnp
from jax import lax
from jax.experimental import pallas as pl
from jax.experimental.pallas import tpu as pltpu
from jax.sharding import PartitionSpec as P


FLOAT = jnp.float32
VMEM_LIMIT = 16 << 20


def halves(value):
    high = value.astype(jnp.bfloat16)
    return high, (value - high.astype(FLOAT)).astype(jnp.bfloat16)


def dot_parts(left, right, right_dim=0):
    mult = functools.partial(
        lax.dot_general,
        dimension_numbers=(((1,), (right_dim,)), ((), ())),
        preferred_element_type=FLOAT,
    )
    return mult(left[0], right[0]) + (mult(left[0], right[1]) + mult(left[1], right[0]))


def dot(left, right, right_dim=0):
    return dot_parts(halves(left), halves(right), right_dim)


def lanes(values):
    return values[0] if len(values) == 1 else jnp.concatenate(values, axis=1)


def column_scale(scale):
    size = scale.shape[1]
    return jnp.concatenate(
        [jnp.broadcast_to(scale[i : i + 1, :], (size, size)).T for i in range(scale.shape[0])], axis=0
    )


def core_side():
    return lax.rem(lax.axis_index("sub"), 2)


def at(index, size):
    return pl.ds(pl.multiple_of(index * size, 8), size)


def call(body, outs, *operands, flops, spaces=None, out_space=pltpu.VMEM, scratch=()):
    spaces = spaces or [pltpu.VMEM] * len(operands)
    size = sum(a.dtype.itemsize * a.size for a in operands)
    outs = [out if isinstance(out, jax.ShapeDtypeStruct) else jax.ShapeDtypeStruct(out, FLOAT) for out in outs]
    return pl.pallas_call(
        body,
        out_shape=outs,
        in_specs=[pl.BlockSpec(memory_space=space) for space in spaces],
        out_specs=[pl.BlockSpec(memory_space=out_space)] * len(outs),
        scratch_shapes=list(scratch),
        compiler_params=pltpu.CompilerParams(vmem_limit_bytes=VMEM_LIMIT),
        cost_estimate=pl.CostEstimate(flops=flops, bytes_accessed=size, transcendentals=0),
    )(*operands)


def pair(*shape):
    return [jax.ShapeDtypeStruct(shape, jnp.bfloat16)] * 2


def store(refs, value):
    for ref, part in zip(refs, halves(value)):
        ref[...] = part


def swap(array, axis, bit):
    return lax.ppermute(array, axis, [(i, i ^ 1 << bit) for i in range(lax.axis_size(axis))])


def partial_sums(array, axis, bits):
    bits = list(bits)
    if not bits:
        return [array]
    for bit in bits[:-1]:
        array = array + swap(array, axis, bit)
    return [array, swap(array, axis, bits[-1])]


def add_all(parts):
    return functools.reduce(lambda a, b: a + b, parts)


def shards(queries, row_scale, leaf_basis, leaf_cores, level_basis, level_cores):
    levels = level_basis.shape[0]
    count = levels + 1
    top = levels
    rows_here, rank = leaf_basis.shape
    columns = queries.shape[1]
    nodes, sub = lax.axis_size("rows"), lax.axis_size("sub")
    heights = [None] + [levels + 1 - e for e in range(1, count)]
    widths = [1] + [nodes // 2 ** heights[e] for e in range(1, count)]
    head = sum(w == 1 for w in widths)
    bits = [range(0)] + [
        range(widths[e - 1].bit_length() - 1, widths[e].bit_length() - 1) for e in range(1, count)
    ]
    blocks = [list(range(e + 1, count)) for e in range(count)]
    coarse = count - head
    leaf_bits = range(1, sub.bit_length() - 1)
    mine = columns // 2
    half = rank // 2
    batches = 2
    batch = mine // batches
    small = 2 * 3 * rank**3

    scale = row_scale.reshape(-1, rank)
    groups = [([e] if e >= head else []) + blocks[e] for e in range(count)]
    starts = [sum(len(b) for b in groups[:e]) * rank for e in range(count + 1)]

    def gram_body(*refs):
        scale_hbm, leaf_hbm, level_hbm, queries_hbm, leaf_core_hbm, core_hbm = refs[:6]
        out_ref, scale_ref, leaf_ref, level_ref, queries_ref, core_ref, sems = refs[6:]
        targets = [(scale_hbm, scale_ref), (leaf_hbm, leaf_ref)]
        targets += [(level_hbm.at[e], level_ref.at[e]) for e in reversed(range(levels))]
        place = lax.axis_index("rows")
        targets += [(queries_hbm, queries_ref), (leaf_core_hbm.at[0], core_ref.at[0])]
        for e in range(1, count):
            targets.append((core_hbm.at[2 ** heights[e] - 2 + place // widths[e]], core_ref.at[e]))
        copies = [pltpu.make_async_copy(a, b, sems.at[i]) for i, (a, b) in enumerate(targets)]
        for copy in copies:
            copy.start()
        for copy in copies[: 2 + levels]:
            copy.wait()
        vectors = [column_scale(scale_ref[...]) * leaf_ref[...]]
        vectors += [level_ref[levels - e] for e in range(1, count)]
        parts = [halves(v) for v in vectors]
        side = core_side()
        for e in range(count):
            right = [lanes([parts[f][i] for f in groups[e]]) for i in range(2)]
            value = dot_parts(halves(vectors[e].T), right)
            for h in range(2):
                out_ref[at(h ^ side, half), starts[e] : starts[e + 1]] = value[h * half : (h + 1) * half]
        for copy in copies[2 + levels :]:
            copy.wait()

    gram, scale, leaf_basis, level_basis, queries, cores = call(
        gram_body,
        [
            (rank, starts[count]),
            *[array.shape for array in (scale, leaf_basis, level_basis, queries)],
            (count, rank, rank),
        ],
        *[
            pltpu.with_memory_space_constraint(array, pltpu.HBM)
            for array in (scale, leaf_basis, level_basis, queries, leaf_cores, level_cores)
        ],
        flops=small * starts[count] // rank * rows_here // rank,
        spaces=[pltpu.HBM] * 6,
        scratch=[pltpu.SemaphoreType.DMA((3 + levels + count,))],
    )
    gram_chip = gram[:half] + swap(gram[half:], "sub", 0)
    early = add_all(partial_sums(gram_chip[:, : starts[head]], "sub", leaf_bits))
    remaining, diagonal, coupling = gram_chip[:, starts[head] :], [], []
    for e in range(head, count):
        remaining = add_all(partial_sums(remaining, "rows", bits[e]))
        size = starts[e + 1] - starts[e]
        pieces = [remaining[:, :rank]]
        if e < top:
            pieces = lax.optimization_barrier([*pieces, remaining[:, rank:size], remaining[:, size:]])
            coupling.append(pieces[1])
            remaining = pieces[2]
        diagonal.append(pieces[0])
    coupling = lanes(coupling)

    def moment_body(scale_ref, queries_ref, leaf_ref, level_ref, out_ref, *basis_refs):
        spread = column_scale(scale_ref[...])
        right = halves(lanes([leaf_ref[...]] + [spread * level_ref[levels - e] for e in range(1, count)]))
        for basis_ref, part in zip(basis_refs, right):
            basis_ref[...] = part
        value = dot_parts(halves(queries_ref[...].T), right)
        side = core_side()
        for h in range(2):
            out_ref[at(h ^ side, mine), :] = value[h * mine : (h + 1) * mine]

    value, *basis = call(
        moment_body,
        [(columns, count * rank), *pair(rows_here, count * rank)],
        scale,
        queries,
        leaf_basis,
        level_basis,
        flops=small * count * 2 * rows_here // rank,
    )
    moment_chip = value[:mine] + swap(value[mine:], "sub", 0)
    moment_parts = [moment_chip[b * batch : (b + 1) * batch] for b in range(batches)]
    moment_parts[-1] = lanes([moment_parts[-1], coupling])
    moment_parts = [partial_sums(moment_parts[b], "sub", leaf_bits) for b in range(batches)]

    late_rows = columns // 2 + head * half

    def late_body(scale_ref, queries_ref, leaf_ref, level_ref, out_ref, *scaled_refs):
        spread = column_scale(scale_ref[...])
        vectors = spread * leaf_ref[...]
        side = core_side()
        scaled = halves(spread * vectors)
        for scaled_ref, part in zip(scaled_refs, scaled):
            scaled_ref[...] = part
        value = dot_parts(halves(queries_ref[...].T), scaled)
        for h in range(2):
            base = (h ^ side) * late_rows
            part = value[h * columns // 2 : (h + 1) * columns // 2]
            out_ref[pl.ds(pl.multiple_of(base, 8), columns // 2), :] = part
        for e in range(head):
            basis = vectors if e == 0 else level_ref[levels - e]
            value = dot(basis.T, basis)
            for h in range(2):
                base = (h ^ side) * late_rows + columns // 2 + e * half
                out_ref[pl.ds(pl.multiple_of(base, 8), half), :] = value[h * half : (h + 1) * half]

    late, *scaled = call(
        late_body,
        [(2 * late_rows, rank), *pair(rows_here, rank)],
        scale,
        queries,
        leaf_basis,
        level_basis,
        flops=small * (2 + head) * rows_here // rank,
    )
    late_chip = late[:late_rows] + swap(late[late_rows:], "sub", 0)

    late = jnp.concatenate([late_chip, *diagonal], axis=0)
    late_size = late.shape[0]
    late = add_all(partial_sums(late, "sub", leaf_bits))

    def product_body(group, own_ref, other_ref, core_ref, *refs):
        out_refs, stack_ref = refs[:-1], refs[-1]
        side = core_side()
        stack_ref[at(side, half), :] = own_ref[...]
        stack_ref[at(1 - side, half), :] = other_ref[...]
        place = 0
        for i, e in enumerate(group):
            block = stack_ref[:, place : place + len(blocks[e]) * rank]
            store(out_refs[2 * i : 2 * i + 2], dot(core_ref[e].T, block))
            place += len(blocks[e]) * rank

    def products(group, own):
        out = call(
            functools.partial(product_body, group),
            [part for e in group for part in pair(rank, len(blocks[e]) * rank)],
            own,
            swap(own, "sub", 0),
            cores,
            flops=small * sum(len(blocks[e]) for e in group),
            scratch=[pltpu.VMEM((rank, own.shape[1]), FLOAT)],
        )
        return [out[2 * i : 2 * i + 2] for i in range(len(group))]

    factors = products(list(range(head)), early)

    def flat(group):
        return [part for factor in group for part in factor]

    def paired(refs):
        return [refs[i : i + 2] for i in range(0, len(refs), 2)]

    def take(factor, start, size):
        return [ref[:, start : start + size] for ref in factor]

    def head_body(number, *refs):
        part_refs, factor_refs = refs[:number], paired(refs[number : number + 2 * head])
        own_ref, rest_ref, *coupling_refs = refs[number + 2 * head :]
        total = add_all([part[...] for part in part_refs])
        rest = total[:, : count * rank]
        for ref in coupling_refs:
            ref[...] = total[:, count * rank :]
        for e in range(head):
            own, rest = rest[:, :rank], rest[:, rank:]
            own_ref[e * batch : (e + 1) * batch, :] = own
            rest = rest - dot_parts(halves(own), take(factor_refs[e], 0, rest.shape[1]))
        rest_ref[...] = rest

    def step_body(number, *refs):
        part_refs, factor, (own_ref, rest_ref) = refs[:number], refs[number:-2], refs[-2:]
        total = add_all([part[...] for part in part_refs])
        own, rest = total[:, :rank], total[:, rank:]
        own_ref[...] = own
        rest_ref[...] = rest - dot_parts(halves(own), take(factor, 0, rest.shape[1]))

    def scatter(parts, number, stack_ref):
        side = core_side()
        for b, part in enumerate(parts):
            for ref, place in zip(part, (side, 1 - side)):
                for e in range(number):
                    stack_ref[at(place * batches + b, batch), e * rank : (e + 1) * rank] = ref[
                        e * batch : (e + 1) * batch, :
                    ]

    head_moments, rests, found_parts = [], [], []
    for b in range(batches):
        extra = moment_parts[b][0].shape[1] - count * rank
        own, rest, *coupling = call(
            functools.partial(head_body, len(moment_parts[b])),
            [(head * batch, rank), (batch, coarse * rank)] + ([(batch, extra)] if extra else []),
            *moment_parts[b],
            *flat(factors[:head]),
            flops=small * sum(map(len, blocks[:head])) // batches,
        )
        head_moments.append(own)
        rests.append(rest)
    factors += products(list(range(head, top)), coupling[0])
    for b in range(batches):
        rest, found = rests[b], []
        for e in range(head, top):
            parts = partial_sums(rest, "rows", bits[e])
            own, rest = call(
                functools.partial(step_body, len(parts)),
                [(batch, rank), (batch, (top - e) * rank)],
                *parts,
                *factors[e],
                flops=small * (top - e) // batches,
            )
            found.append(own)
        found.append(add_all(partial_sums(rest, "rows", bits[top])))
        found = jnp.concatenate(found, axis=0)
        found_parts.append([found, swap(found, "sub", 0)])
    late = jnp.concatenate([late, *head_moments], axis=0)
    late_parts = [late, swap(late, "sub", 0)]

    def answer_body(*refs):
        factor_refs, basis_refs, out_refs = paired(refs[:-4]), refs[-4:-2], refs[-2:]
        rows = {}
        for f in reversed(range(count)):
            if f + 1 < count:
                stack = jnp.concatenate([rows[g] for g in range(f + 1, count)], axis=0)
                row = -dot_parts(take(factor_refs[f], 0, stack.shape[0]), halves(stack))
            else:
                row = jnp.zeros((rank, coarse * rank), FLOAT)
            if f >= head:
                line = lax.broadcasted_iota(jnp.int32, row.shape, 0) + (f - head) * rank
                row = row + jnp.where(line == lax.broadcasted_iota(jnp.int32, row.shape, 1), 1.0, 0.0)
            rows[f] = row
        gains = jnp.concatenate([rows[f] for f in range(count)], axis=0)
        store(out_refs, dot_parts([ref[...] for ref in basis_refs], halves(gains)))

    answer = call(
        answer_body,
        pair(rows_here, coarse * rank),
        *flat(factors),
        *basis,
        flops=small * coarse * count * rows_here // rank,
    )

    def base_body(scale_ref, queries_ref, own_ref, other_ref, core_ref, *refs):
        factor_refs, basis_refs, scaled_refs = paired(refs[: 2 * head]), refs[2 * head : -7], refs[-7:-5]
        out_ref, *gain_refs, stack_ref, gram_ref = refs[-5:]
        pieces = [pl.ds(late_size + b * head * batch, head * batch) for b in range(batches)]
        scatter([(own_ref.at[piece], other_ref.at[piece]) for piece in pieces], head, stack_ref)
        side = core_side()
        for late_ref, place in ((own_ref, side), (other_ref, 1 - side)):
            stack_ref[at(place, columns // 2), head * rank :] = late_ref[: columns // 2]
            for e in range(count):
                start = columns // 2 + e * half
                gram_ref[at(place, half), e * rank : (e + 1) * rank] = late_ref[start : start + half]
        products = [dot(core_ref[e].T, gram_ref[:, e * rank : (e + 1) * rank]) for e in range(count)]
        gains = [core_ref[e] + core_ref[e].T - dot(products[e], core_ref[e]) for e in range(1, count)]
        store(gain_refs, lanes(gains[head - 1 :]))
        moments = [stack_ref[:, e * rank : (e + 1) * rank] for e in range(head)]
        first = dot(moments[0], core_ref[0], 1)
        found = [dot(stack_ref[:, head * rank :], core_ref[0]) - dot(first, products[0], 1)]
        found += [dot(moments[e], gains[e - 1], 1) for e in range(1, head)]
        for e in reversed(range(head - 1)):
            size = (head - 1 - e) * rank
            found[e] = found[e] - dot_parts(halves(lanes(found[e + 1 :])), take(factor_refs[e], 0, size), 1)
        left = [lanes([a[...], b[:, : head * rank]]) for a, b in zip(scaled_refs, basis_refs)]
        square = column_scale(scale_ref[...] * scale_ref[...])
        square = lanes([square] * (columns // rank))
        out_ref[...] = square * queries_ref[...] - dot_parts(left, halves(lanes([first, *found])), 1)

    base, *gains = call(
        base_body,
        [(rows_here, columns), *pair(rank, coarse * rank)],
        scale,
        queries,
        *late_parts,
        cores,
        *flat(factors[:head]),
        *basis,
        *scaled,
        flops=small * 2 * (head + 1) * rows_here // rank,
        scratch=[pltpu.VMEM((columns, (head + 1) * rank), FLOAT), pltpu.VMEM((rank, count * rank), FLOAT)],
    )

    def last_body(base_ref, high_ref, low_ref, *refs):
        gain_refs, part_refs, (out_ref, stack_ref) = refs[:2], paired(refs[2:-2]), refs[-2:]
        scatter(part_refs, coarse, stack_ref)
        right = []
        for e in range(coarse):
            where = slice(e * rank, (e + 1) * rank)
            right.append(dot_parts(halves(stack_ref[:, where]), [ref[:, where] for ref in gain_refs], 1))
        out_ref[...] = base_ref[...] - dot_parts([high_ref[...], low_ref[...]], halves(lanes(right)), 1)

    (out,) = call(
        last_body,
        [(rows_here, columns)],
        base,
        *answer,
        *gains,
        *flat(found_parts),
        flops=small * 2 * coarse * rows_here // rank,
        scratch=[pltpu.VMEM((columns, coarse * rank), FLOAT)],
    )
    return out


def solution(mesh):
    in_specs = (
        P(("rows", "sub"), None),
        P(("rows", "sub")),
        P(("rows", "sub"), None),
        P("rows", None, None),
        P(None, ("rows", "sub"), None),
        P(),
    )
    out_specs = P(("rows", "sub"), None)

    return jax.shard_map(shards, mesh=mesh, in_specs=in_specs, out_specs=out_specs, check_vma=False)
```

```python
import functools

import jax
import jax.numpy as jnp
from jax import lax
from jax.experimental import pallas as pl
from jax.experimental.pallas import tpu as pltpu
from jax.sharding import PartitionSpec as P


FLOAT = jnp.float32
VMEM_LIMIT = 16 << 20


def halves(value):
    high = value.astype(jnp.bfloat16)
    return high, (value - high.astype(FLOAT)).astype(jnp.bfloat16)


def dot_parts(left, right, right_dim=0):
    mult = functools.partial(
        lax.dot_general,
        dimension_numbers=(((1,), (right_dim,)), ((), ())),
        preferred_element_type=FLOAT,
    )
    return mult(left[0], right[0]) + (mult(left[0], right[1]) + mult(left[1], right[0]))


def dot(left, right, right_dim=0):
    return dot_parts(halves(left), halves(right), right_dim)


def lanes(values):
    return values[0] if len(values) == 1 else jnp.concatenate(values, axis=1)


def column_scale(scale):
    size = scale.shape[1]
    return jnp.concatenate(
        [jnp.broadcast_to(scale[i : i + 1, :], (size, size)).T for i in range(scale.shape[0])], axis=0
    )


def core_side():
    return lax.rem(lax.axis_index("sub"), 2)


def at(index, size):
    return pl.ds(pl.multiple_of(index * size, 8), size)


def call(body, outs, *operands, flops, spaces=None, out_space=pltpu.VMEM, scratch=()):
    spaces = spaces or [pltpu.VMEM] * len(operands)
    size = sum(a.dtype.itemsize * a.size for a in operands)
    outs = [out if isinstance(out, jax.ShapeDtypeStruct) else jax.ShapeDtypeStruct(out, FLOAT) for out in outs]
    return pl.pallas_call(
        body,
        out_shape=outs,
        in_specs=[pl.BlockSpec(memory_space=space) for space in spaces],
        out_specs=[pl.BlockSpec(memory_space=out_space)] * len(outs),
        scratch_shapes=list(scratch),
        compiler_params=pltpu.CompilerParams(vmem_limit_bytes=VMEM_LIMIT),
        cost_estimate=pl.CostEstimate(flops=flops, bytes_accessed=size, transcendentals=0),
    )(*operands)


def pair(*shape):
    return [jax.ShapeDtypeStruct(shape, jnp.bfloat16)] * 2


def store(refs, value):
    for ref, part in zip(refs, halves(value)):
        ref[...] = part


def swap(array, axis, bit):
    return lax.ppermute(array, axis, [(i, i ^ 1 << bit) for i in range(lax.axis_size(axis))])


def partial_sums(array, axis, bits):
    bits = list(bits)
    if not bits:
        return [array]
    for bit in bits[:-1]:
        array = array + swap(array, axis, bit)
    return [array, swap(array, axis, bits[-1])]


def add_all(parts):
    return functools.reduce(lambda a, b: a + b, parts)


def shards(queries, row_scale, leaf_basis, leaf_cores, level_basis, level_cores):
    levels = level_basis.shape[0]
    count = levels + 1
    top = levels
    rows_here, rank = leaf_basis.shape
    columns = queries.shape[1]
    nodes, sub = lax.axis_size("rows"), lax.axis_size("sub")
    heights = [None] + [levels + 1 - e for e in range(1, count)]
    widths = [1] + [nodes // 2 ** heights[e] for e in range(1, count)]
    head = sum(w == 1 for w in widths)
    bits = [range(0)] + [
        range(widths[e - 1].bit_length() - 1, widths[e].bit_length() - 1) for e in range(1, count)
    ]
    blocks = [list(range(e + 1, count)) for e in range(count)]
    coarse = count - head
    leaf_bits = range(1, sub.bit_length() - 1)
    mine = columns // 2
    half = rank // 2
    batches = 2
    batch = mine // batches
    small = 2 * 3 * rank**3

    scale = row_scale.reshape(-1, rank)
    groups = [([e] if e >= head else []) + blocks[e] for e in range(count)]
    starts = [sum(len(b) for b in groups[:e]) * rank for e in range(count + 1)]

    def gram_body(*refs):
        scale_hbm, leaf_hbm, level_hbm, queries_hbm, leaf_core_hbm, core_hbm = refs[:6]
        out_ref, scale_ref, leaf_ref, level_ref, queries_ref, core_ref, sems = refs[6:]
        targets = [(scale_hbm, scale_ref), (leaf_hbm, leaf_ref)]
        targets += [(level_hbm.at[e], level_ref.at[e]) for e in reversed(range(levels))]
        place = lax.axis_index("rows")
        targets += [(queries_hbm, queries_ref), (leaf_core_hbm.at[0], core_ref.at[0])]
        for e in range(1, count):
            targets.append((core_hbm.at[2 ** heights[e] - 2 + place // widths[e]], core_ref.at[e]))
        copies = [pltpu.make_async_copy(a, b, sems.at[i]) for i, (a, b) in enumerate(targets)]
        for copy in copies:
            copy.start()
        for copy in copies[: 2 + levels]:
            copy.wait()
        vectors = [column_scale(scale_ref[...]) * leaf_ref[...]]
        vectors += [level_ref[levels - e] for e in range(1, count)]
        parts = [halves(v) for v in vectors]
        side = core_side()
        for e in range(count):
            right = [lanes([parts[f][i] for f in groups[e]]) for i in range(2)]
            value = dot_parts(halves(vectors[e].T), right)
            for h in range(2):
                out_ref[at(h ^ side, half), starts[e] : starts[e + 1]] = value[h * half : (h + 1) * half]
        for copy in copies[2 + levels :]:
            copy.wait()

    gram, scale, leaf_basis, level_basis, queries, cores = call(
        gram_body,
        [
            (rank, starts[count]),
            *[array.shape for array in (scale, leaf_basis, level_basis, queries)],
            (count, rank, rank),
        ],
        *[
            pltpu.with_memory_space_constraint(array, pltpu.HBM)
            for array in (scale, leaf_basis, level_basis, queries, leaf_cores, level_cores)
        ],
        flops=small * starts[count] // rank * rows_here // rank,
        spaces=[pltpu.HBM] * 6,
        scratch=[pltpu.SemaphoreType.DMA((3 + levels + count,))],
    )
    gram_chip = gram[:half] + swap(gram[half:], "sub", 0)
    early = add_all(partial_sums(gram_chip[:, : starts[head]], "sub", leaf_bits))
    remaining, diagonal, coupling = gram_chip[:, starts[head] :], [], []
    for e in range(head, top):
        remaining = add_all(partial_sums(remaining, "rows", bits[e]))
        size = starts[e + 1] - starts[e]
        pieces = [remaining[:, :rank], remaining[:, rank:size], remaining[:, size:]]
        pieces = lax.optimization_barrier(pieces)
        diagonal.append(pieces[0])
        coupling.append(pieces[1])
        remaining = pieces[2]
    coupling = add_all(partial_sums(lanes([*coupling, remaining]), "sub", leaf_bits))
    top_block, coupling = coupling[:, -rank:], coupling[:, :-rank]

    def moment_body(scale_ref, queries_ref, leaf_ref, level_ref, out_ref, *basis_refs):
        spread = column_scale(scale_ref[...])
        right = halves(lanes([leaf_ref[...]] + [spread * level_ref[levels - e] for e in range(1, count)]))
        for basis_ref, part in zip(basis_refs, right):
            basis_ref[...] = part
        value = dot_parts(halves(queries_ref[...].T), right)
        side = core_side()
        for h in range(2):
            out_ref[at(h ^ side, mine), :] = value[h * mine : (h + 1) * mine]

    value, *basis = call(
        moment_body,
        [(columns, count * rank), *pair(rows_here, count * rank)],
        scale,
        queries,
        leaf_basis,
        level_basis,
        flops=small * count * 2 * rows_here // rank,
    )
    moment_chip = value[:mine] + swap(value[mine:], "sub", 0)
    moment_parts = [moment_chip[b * batch : (b + 1) * batch] for b in range(batches)]
    moment_parts = [partial_sums(moment_parts[b], "sub", leaf_bits) for b in range(batches)]

    late_rows = columns // 2 + head * half

    def late_body(scale_ref, queries_ref, leaf_ref, level_ref, out_ref, *scaled_refs):
        spread = column_scale(scale_ref[...])
        vectors = spread * leaf_ref[...]
        side = core_side()
        scaled = halves(spread * vectors)
        for scaled_ref, part in zip(scaled_refs, scaled):
            scaled_ref[...] = part
        value = dot_parts(halves(queries_ref[...].T), scaled)
        for h in range(2):
            base = (h ^ side) * late_rows
            part = value[h * columns // 2 : (h + 1) * columns // 2]
            out_ref[pl.ds(pl.multiple_of(base, 8), columns // 2), :] = part
        for e in range(head):
            basis = vectors if e == 0 else level_ref[levels - e]
            value = dot(basis.T, basis)
            for h in range(2):
                base = (h ^ side) * late_rows + columns // 2 + e * half
                out_ref[pl.ds(pl.multiple_of(base, 8), half), :] = value[h * half : (h + 1) * half]

    late, *scaled = call(
        late_body,
        [(2 * late_rows, rank), *pair(rows_here, rank)],
        scale,
        queries,
        leaf_basis,
        level_basis,
        flops=small * (2 + head) * rows_here // rank,
    )
    late_chip = late[:late_rows] + swap(late[late_rows:], "sub", 0)

    late = jnp.concatenate([late_chip, *diagonal], axis=0)
    late_size = late.shape[0]
    late = add_all(partial_sums(late, "sub", leaf_bits))

    def product_body(group, own_ref, other_ref, core_ref, *refs):
        out_refs, stack_ref = refs[:-1], refs[-1]
        side = core_side()
        stack_ref[at(side, half), :] = own_ref[...]
        stack_ref[at(1 - side, half), :] = other_ref[...]
        place = 0
        for i, e in enumerate(group):
            block = stack_ref[:, place : place + len(blocks[e]) * rank]
            store(out_refs[2 * i : 2 * i + 2], dot(core_ref[e].T, block))
            place += len(blocks[e]) * rank

    def products(group, own):
        out = call(
            functools.partial(product_body, group),
            [part for e in group for part in pair(rank, len(blocks[e]) * rank)],
            own,
            swap(own, "sub", 0),
            cores,
            flops=small * sum(len(blocks[e]) for e in group),
            scratch=[pltpu.VMEM((rank, own.shape[1]), FLOAT)],
        )
        return [out[2 * i : 2 * i + 2] for i in range(len(group))]

    factors = products(list(range(head)), early)

    def flat(group):
        return [part for factor in group for part in factor]

    def paired(refs):
        return [refs[i : i + 2] for i in range(0, len(refs), 2)]

    def take(factor, start, size):
        return [ref[:, start : start + size] for ref in factor]

    def head_body(number, *refs):
        part_refs, factor_refs = refs[:number], paired(refs[number : number + 2 * head])
        own_ref, rest_ref = refs[number + 2 * head :]
        rest = add_all([part[...] for part in part_refs])
        for e in range(head):
            own, rest = rest[:, :rank], rest[:, rank:]
            own_ref[e * batch : (e + 1) * batch, :] = own
            rest = rest - dot_parts(halves(own), take(factor_refs[e], 0, rest.shape[1]))
        rest_ref[...] = rest

    def step_body(number, *refs):
        part_refs, factor, (own_ref, rest_ref) = refs[:number], refs[number:-2], refs[-2:]
        total = add_all([part[...] for part in part_refs])
        own, rest = total[:, :rank], total[:, rank:]
        own_ref[...] = own
        rest_ref[...] = rest - dot_parts(halves(own), take(factor, 0, rest.shape[1]))

    def scatter(parts, number, stack_ref):
        side = core_side()
        for b, part in enumerate(parts):
            for ref, place in zip(part, (side, 1 - side)):
                for e in range(number):
                    stack_ref[at(place * batches + b, batch), e * rank : (e + 1) * rank] = ref[
                        e * batch : (e + 1) * batch, :
                    ]

    factors += products(list(range(head, top)), coupling)
    head_moments, found_parts = [], []
    for b in range(batches):
        own, rest = call(
            functools.partial(head_body, len(moment_parts[b])),
            [(head * batch, rank), (batch, coarse * rank)],
            *moment_parts[b],
            *flat(factors[:head]),
            flops=small * sum(map(len, blocks[:head])) // batches,
        )
        head_moments.append(own)
        found = []
        for e in range(head, top):
            parts = partial_sums(rest, "rows", bits[e])
            own, rest = call(
                functools.partial(step_body, len(parts)),
                [(batch, rank), (batch, (top - e) * rank)],
                *parts,
                *factors[e],
                flops=small * (top - e) // batches,
            )
            found.append(own)
        if b == 0:
            rest = jnp.concatenate([rest, top_block], axis=0)
        found.append(add_all(partial_sums(rest, "rows", bits[top])))
        found = jnp.concatenate(found, axis=0)
        found_parts.append([found, swap(found, "sub", 0)])
    late = jnp.concatenate([late, *head_moments], axis=0)
    late_parts = [late, swap(late, "sub", 0)]

    def answer_body(*refs):
        factor_refs, basis_refs, out_refs = paired(refs[:-4]), refs[-4:-2], refs[-2:]
        rows = {}
        for f in reversed(range(count)):
            if f + 1 < count:
                stack = jnp.concatenate([rows[g] for g in range(f + 1, count)], axis=0)
                row = -dot_parts(take(factor_refs[f], 0, stack.shape[0]), halves(stack))
            else:
                row = jnp.zeros((rank, coarse * rank), FLOAT)
            if f >= head:
                line = lax.broadcasted_iota(jnp.int32, row.shape, 0) + (f - head) * rank
                row = row + jnp.where(line == lax.broadcasted_iota(jnp.int32, row.shape, 1), 1.0, 0.0)
            rows[f] = row
        gains = jnp.concatenate([rows[f] for f in range(count)], axis=0)
        store(out_refs, dot_parts([ref[...] for ref in basis_refs], halves(gains)))

    answer = call(
        answer_body,
        pair(rows_here, coarse * rank),
        *flat(factors),
        *basis,
        flops=small * coarse * count * rows_here // rank,
    )

    def base_body(scale_ref, queries_ref, own_ref, other_ref, own_found_ref, other_found_ref, core_ref, *refs):
        factor_refs, basis_refs, scaled_refs = paired(refs[: 2 * head]), refs[2 * head : -7], refs[-7:-5]
        out_ref, *gain_refs, stack_ref, gram_ref = refs[-5:]
        pieces = [pl.ds(late_size + b * head * batch, head * batch) for b in range(batches)]
        scatter([(own_ref.at[piece], other_ref.at[piece]) for piece in pieces], head, stack_ref)
        side = core_side()
        sources = ((own_ref, own_found_ref, side), (other_ref, other_found_ref, 1 - side))
        for late_ref, found_ref, place in sources:
            stack_ref[at(place, columns // 2), head * rank :] = late_ref[: columns // 2]
            gram_ref[at(place, half), top * rank :] = found_ref[coarse * batch :]
            for e in range(top):
                start = columns // 2 + e * half
                gram_ref[at(place, half), e * rank : (e + 1) * rank] = late_ref[start : start + half]
        products = [dot(core_ref[e].T, gram_ref[:, e * rank : (e + 1) * rank]) for e in range(count)]
        gains = [core_ref[e] + core_ref[e].T - dot(products[e], core_ref[e]) for e in range(1, count)]
        store(gain_refs, lanes(gains[head - 1 :]))
        moments = [stack_ref[:, e * rank : (e + 1) * rank] for e in range(head)]
        first = dot(moments[0], core_ref[0], 1)
        found = [dot(stack_ref[:, head * rank :], core_ref[0]) - dot(first, products[0], 1)]
        found += [dot(moments[e], gains[e - 1], 1) for e in range(1, head)]
        for e in reversed(range(head - 1)):
            size = (head - 1 - e) * rank
            found[e] = found[e] - dot_parts(halves(lanes(found[e + 1 :])), take(factor_refs[e], 0, size), 1)
        left = [lanes([a[...], b[:, : head * rank]]) for a, b in zip(scaled_refs, basis_refs)]
        square = column_scale(scale_ref[...] * scale_ref[...])
        square = lanes([square] * (columns // rank))
        out_ref[...] = square * queries_ref[...] - dot_parts(left, halves(lanes([first, *found])), 1)

    base, *gains = call(
        base_body,
        [(rows_here, columns), *pair(rank, coarse * rank)],
        scale,
        queries,
        *late_parts,
        *found_parts[0],
        cores,
        *flat(factors[:head]),
        *basis,
        *scaled,
        flops=small * 2 * (head + 1) * rows_here // rank,
        scratch=[pltpu.VMEM((columns, (head + 1) * rank), FLOAT), pltpu.VMEM((rank, count * rank), FLOAT)],
    )

    def last_body(base_ref, high_ref, low_ref, *refs):
        gain_refs, part_refs, (out_ref, stack_ref) = refs[:2], paired(refs[2:-2]), refs[-2:]
        scatter(part_refs, coarse, stack_ref)
        right = []
        for e in range(coarse):
            where = slice(e * rank, (e + 1) * rank)
            right.append(dot_parts(halves(stack_ref[:, where]), [ref[:, where] for ref in gain_refs], 1))
        out_ref[...] = base_ref[...] - dot_parts([high_ref[...], low_ref[...]], halves(lanes(right)), 1)

    (out,) = call(
        last_body,
        [(rows_here, columns)],
        base,
        *answer,
        *gains,
        *flat(found_parts),
        flops=small * 2 * coarse * rows_here // rank,
        scratch=[pltpu.VMEM((columns, coarse * rank), FLOAT)],
    )
    return out


def solution(mesh):
    in_specs = (
        P(("rows", "sub"), None),
        P(("rows", "sub")),
        P(("rows", "sub"), None),
        P("rows", None, None),
        P(None, ("rows", "sub"), None),
        P(),
    )
    out_specs = P(("rows", "sub"), None)

    return jax.shard_map(shards, mesh=mesh, in_specs=in_specs, out_specs=out_specs, check_vma=False)
```

```python
import functools

import jax
import jax.numpy as jnp
from jax import lax
from jax.experimental import pallas as pl
from jax.experimental.pallas import tpu as pltpu
from jax.sharding import PartitionSpec as P


FLOAT = jnp.float32
VMEM_LIMIT = 16 << 20


def halves(value):
    high = value.astype(jnp.bfloat16)
    return high, (value - high.astype(FLOAT)).astype(jnp.bfloat16)


def dot_parts(left, right, right_dim=0):
    mult = functools.partial(
        lax.dot_general,
        dimension_numbers=(((1,), (right_dim,)), ((), ())),
        preferred_element_type=FLOAT,
    )
    return mult(left[0], right[0]) + (mult(left[0], right[1]) + mult(left[1], right[0]))


def dot(left, right, right_dim=0):
    return dot_parts(halves(left), halves(right), right_dim)


def lanes(values):
    return values[0] if len(values) == 1 else jnp.concatenate(values, axis=1)


def column_scale(scale):
    size = scale.shape[1]
    return jnp.concatenate(
        [jnp.broadcast_to(scale[i : i + 1, :], (size, size)).T for i in range(scale.shape[0])], axis=0
    )


def core_side():
    return lax.rem(lax.axis_index("sub"), 2)


def at(index, size):
    return pl.ds(pl.multiple_of(index * size, 8), size)


def call(body, outs, *operands, flops, spaces=None, out_space=pltpu.VMEM, scratch=()):
    spaces = spaces or [pltpu.VMEM] * len(operands)
    size = sum(a.dtype.itemsize * a.size for a in operands)
    outs = [out if isinstance(out, jax.ShapeDtypeStruct) else jax.ShapeDtypeStruct(out, FLOAT) for out in outs]
    return pl.pallas_call(
        body,
        out_shape=outs,
        in_specs=[pl.BlockSpec(memory_space=space) for space in spaces],
        out_specs=[pl.BlockSpec(memory_space=out_space)] * len(outs),
        scratch_shapes=list(scratch),
        compiler_params=pltpu.CompilerParams(vmem_limit_bytes=VMEM_LIMIT),
        cost_estimate=pl.CostEstimate(flops=flops, bytes_accessed=size, transcendentals=0),
    )(*operands)


def pair(*shape):
    return [jax.ShapeDtypeStruct(shape, jnp.bfloat16)] * 2


def store(refs, value):
    for ref, part in zip(refs, halves(value)):
        ref[...] = part


def swap(array, axis, bit):
    return lax.ppermute(array, axis, [(i, i ^ 1 << bit) for i in range(lax.axis_size(axis))])


def partial_sums(array, axis, bits):
    bits = list(bits)
    if not bits:
        return [array]
    for bit in bits[:-1]:
        array = array + swap(array, axis, bit)
    return [array, swap(array, axis, bits[-1])]


def add_all(parts):
    return functools.reduce(lambda a, b: a + b, parts)


def shards(queries, row_scale, leaf_basis, leaf_cores, level_basis, level_cores):
    levels = level_basis.shape[0]
    count = levels + 1
    top = levels
    rows_here, rank = leaf_basis.shape
    columns = queries.shape[1]
    nodes, sub = lax.axis_size("rows"), lax.axis_size("sub")
    heights = [None] + [levels + 1 - e for e in range(1, count)]
    widths = [1] + [nodes // 2 ** heights[e] for e in range(1, count)]
    head = sum(w == 1 for w in widths)
    bits = [range(0)] + [
        range(widths[e - 1].bit_length() - 1, widths[e].bit_length() - 1) for e in range(1, count)
    ]
    blocks = [list(range(e + 1, count)) for e in range(count)]
    coarse = count - head
    leaf_bits = range(1, sub.bit_length() - 1)
    mine = columns // 2
    half = rank // 2
    batches = 2
    batch = mine // batches
    small = 2 * 3 * rank**3

    scale = row_scale.reshape(-1, rank)
    groups = [([e] if e >= head else []) + blocks[e] for e in range(count)]
    starts = [sum(len(b) for b in groups[:e]) * rank for e in range(count + 1)]

    def gram_body(*refs):
        scale_hbm, leaf_hbm, level_hbm, queries_hbm, leaf_core_hbm, core_hbm = refs[:6]
        out_ref, scale_ref, leaf_ref, level_ref, queries_ref, core_ref, sems = refs[6:]
        targets = [(scale_hbm, scale_ref), (leaf_hbm, leaf_ref)]
        targets += [(level_hbm.at[e], level_ref.at[e]) for e in reversed(range(levels))]
        place = lax.axis_index("rows")
        targets += [(queries_hbm, queries_ref), (leaf_core_hbm.at[0], core_ref.at[0])]
        for e in range(1, count):
            targets.append((core_hbm.at[2 ** heights[e] - 2 + place // widths[e]], core_ref.at[e]))
        copies = [pltpu.make_async_copy(a, b, sems.at[i]) for i, (a, b) in enumerate(targets)]
        for copy in copies:
            copy.start()
        for copy in copies[: 2 + levels]:
            copy.wait()
        vectors = [column_scale(scale_ref[...]) * leaf_ref[...]]
        vectors += [level_ref[levels - e] for e in range(1, count)]
        parts = [halves(v) for v in vectors]
        side = core_side()
        for e in range(count):
            right = [lanes([parts[f][i] for f in groups[e]]) for i in range(2)]
            value = dot_parts(halves(vectors[e].T), right)
            for h in range(2):
                out_ref[at(h ^ side, half), starts[e] : starts[e + 1]] = value[h * half : (h + 1) * half]
        for copy in copies[2 + levels :]:
            copy.wait()

    gram, scale, leaf_basis, level_basis, queries, cores = call(
        gram_body,
        [
            (rank, starts[count]),
            *[array.shape for array in (scale, leaf_basis, level_basis, queries)],
            (count, rank, rank),
        ],
        *[
            pltpu.with_memory_space_constraint(array, pltpu.HBM)
            for array in (scale, leaf_basis, level_basis, queries, leaf_cores, level_cores)
        ],
        flops=small * starts[count] // rank * rows_here // rank,
        spaces=[pltpu.HBM] * 6,
        scratch=[pltpu.SemaphoreType.DMA((3 + levels + count,))],
    )
    gram_chip = gram[:half] + swap(gram[half:], "sub", 0)
    early = add_all(partial_sums(gram_chip[:, : starts[head]], "sub", leaf_bits))
    remaining, diagonal, coupling = gram_chip[:, starts[head] :], [], []
    for e in range(head, top):
        remaining = add_all(partial_sums(remaining, "rows", bits[e]))
        size = starts[e + 1] - starts[e]
        pieces = [remaining[:, :rank], remaining[:, rank:size], remaining[:, size:]]
        pieces = lax.optimization_barrier(pieces)
        diagonal.append(pieces[0])
        coupling.append(pieces[1])
        remaining = pieces[2]
    coupling = add_all(partial_sums(lanes([*coupling, remaining]), "sub", leaf_bits))
    top_block, coupling = coupling[:, -rank:], coupling[:, :-rank]

    def moment_body(scale_ref, queries_ref, leaf_ref, level_ref, out_ref, *basis_refs):
        spread = column_scale(scale_ref[...])
        right = halves(lanes([leaf_ref[...]] + [spread * level_ref[levels - e] for e in range(1, count)]))
        for basis_ref, part in zip(basis_refs, right):
            basis_ref[...] = part
        value = dot_parts(halves(queries_ref[...].T), right)
        side = core_side()
        for h in range(2):
            out_ref[at(h ^ side, mine), :] = value[h * mine : (h + 1) * mine]

    value, *basis = call(
        moment_body,
        [(columns, count * rank), *pair(rows_here, count * rank)],
        scale,
        queries,
        leaf_basis,
        level_basis,
        flops=small * count * 2 * rows_here // rank,
    )
    moment_chip = value[:mine] + swap(value[mine:], "sub", 0)
    moment_parts = [moment_chip[b * batch : (b + 1) * batch] for b in range(batches)]
    moment_parts = [partial_sums(moment_parts[b], "sub", leaf_bits) for b in range(batches)]

    late_rows = columns // 2 + head * half

    def late_body(scale_ref, queries_ref, leaf_ref, level_ref, out_ref, *scaled_refs):
        spread = column_scale(scale_ref[...])
        vectors = spread * leaf_ref[...]
        side = core_side()
        scaled = halves(spread * vectors)
        for scaled_ref, part in zip(scaled_refs, scaled):
            scaled_ref[...] = part
        value = dot_parts(halves(queries_ref[...].T), scaled)
        for h in range(2):
            base = (h ^ side) * late_rows
            part = value[h * columns // 2 : (h + 1) * columns // 2]
            out_ref[pl.ds(pl.multiple_of(base, 8), columns // 2), :] = part
        for e in range(head):
            basis = vectors if e == 0 else level_ref[levels - e]
            value = dot(basis.T, basis)
            for h in range(2):
                base = (h ^ side) * late_rows + columns // 2 + e * half
                out_ref[pl.ds(pl.multiple_of(base, 8), half), :] = value[h * half : (h + 1) * half]

    late, *scaled = call(
        late_body,
        [(2 * late_rows, rank), *pair(rows_here, rank)],
        scale,
        queries,
        leaf_basis,
        level_basis,
        flops=small * (2 + head) * rows_here // rank,
    )
    late_chip = late[:late_rows] + swap(late[late_rows:], "sub", 0)

    late = jnp.concatenate([late_chip, *diagonal], axis=0)
    late_size = late.shape[0]
    late = add_all(partial_sums(late, "sub", leaf_bits))

    def product_body(group, own_ref, other_ref, core_ref, *refs):
        out_refs, stack_ref = refs[:-1], refs[-1]
        side = core_side()
        stack_ref[at(side, half), :] = own_ref[...]
        stack_ref[at(1 - side, half), :] = other_ref[...]
        place = 0
        for i, e in enumerate(group):
            block = stack_ref[:, place : place + len(blocks[e]) * rank]
            store(out_refs[2 * i : 2 * i + 2], dot(core_ref[e].T, block))
            place += len(blocks[e]) * rank

    def products(group, own):
        out = call(
            functools.partial(product_body, group),
            [part for e in group for part in pair(rank, len(blocks[e]) * rank)],
            own,
            swap(own, "sub", 0),
            cores,
            flops=small * sum(len(blocks[e]) for e in group),
            scratch=[pltpu.VMEM((rank, own.shape[1]), FLOAT)],
        )
        return [out[2 * i : 2 * i + 2] for i in range(len(group))]

    factors = products(list(range(head)), early)

    def flat(group):
        return [part for factor in group for part in factor]

    def paired(refs):
        return [refs[i : i + 2] for i in range(0, len(refs), 2)]

    def take(factor, start, size):
        return [ref[:, start : start + size] for ref in factor]

    def head_body(number, *refs):
        part_refs, factor_refs = refs[:number], paired(refs[number : number + 2 * head])
        own_ref, rest_ref = refs[number + 2 * head :]
        rest = add_all([part[...] for part in part_refs])
        for e in range(head):
            own, rest = rest[:, :rank], rest[:, rank:]
            own_ref[e * batch : (e + 1) * batch, :] = own
            rest = rest - dot_parts(halves(own), take(factor_refs[e], 0, rest.shape[1]))
        rest_ref[...] = rest

    def step_body(number, *refs):
        part_refs, factor, (own_ref, rest_ref) = refs[:number], refs[number:-2], refs[-2:]
        total = add_all([part[...] for part in part_refs])
        own, rest = total[:, :rank], total[:, rank:]
        own_ref[...] = own
        rest_ref[...] = rest - dot_parts(halves(own), take(factor, 0, rest.shape[1]))

    def scatter(parts, number, stack_ref):
        side = core_side()
        for b, part in enumerate(parts):
            for ref, place in zip(part, (side, 1 - side)):
                for e in range(number):
                    stack_ref[at(place * batches + b, batch), e * rank : (e + 1) * rank] = ref[
                        e * batch : (e + 1) * batch, :
                    ]

    factors += products(list(range(head, top)), coupling)
    head_moments, found_parts = [], []
    for b in range(batches):
        own, rest = call(
            functools.partial(head_body, len(moment_parts[b])),
            [(head * batch, rank), (batch, coarse * rank)],
            *moment_parts[b],
            *flat(factors[:head]),
            flops=small * sum(map(len, blocks[:head])) // batches,
        )
        head_moments.append(own)
        found = []
        for e in range(head, top):
            parts = partial_sums(rest, "rows", bits[e])
            own, rest = call(
                functools.partial(step_body, len(parts)),
                [(batch, rank), (batch, (top - e) * rank)],
                *parts,
                *factors[e],
                flops=small * (top - e) // batches,
            )
            found.append(own)
        if b == 0:
            rest = jnp.concatenate([rest, top_block], axis=0)
        found.append(add_all(partial_sums(rest, "rows", bits[top])))
        found = jnp.concatenate(found, axis=0)
        found_parts.append([found, swap(found, "sub", 0)])
    late = jnp.concatenate([late, *head_moments], axis=0)
    late_parts = [late, swap(late, "sub", 0)]

    def answer_body(*refs):
        factor_refs, basis_refs, out_refs = paired(refs[:-4]), refs[-4:-2], refs[-2:]
        shape = (coarse * rank, coarse * rank)
        line, column = (lax.broadcasted_iota(jnp.int32, shape, i) for i in range(2))
        gains = jnp.where(line == column, 1.0, 0.0)
        for f in reversed(range(head)):
            row = -dot_parts(take(factor_refs[f], 0, gains.shape[0]), halves(gains))
            gains = jnp.concatenate([row, gains], axis=0)
        store(out_refs, dot_parts([ref[...] for ref in basis_refs], halves(gains)))

    answer = call(
        answer_body,
        pair(rows_here, coarse * rank),
        *flat(factors[:head]),
        *basis,
        flops=small * coarse * count * rows_here // rank,
    )

    def gain_body(own_ref, other_ref, own_found_ref, other_found_ref, core_ref, *refs):
        out_refs, gram_ref = refs[:2], refs[2]
        side = core_side()
        sources = ((own_ref, own_found_ref, side), (other_ref, other_found_ref, 1 - side))
        for late_ref, found_ref, place in sources:
            gram_ref[at(place, half), (coarse - 1) * rank :] = found_ref[coarse * batch :]
            for e in range(head, top):
                start = columns // 2 + e * half
                where = slice((e - head) * rank, (e - head + 1) * rank)
                gram_ref[at(place, half), where] = late_ref[start : start + half]
        gains = []
        for e in range(head, count):
            core = core_ref[e]
            gram = gram_ref[:, (e - head) * rank : (e - head + 1) * rank]
            gains.append(core + core.T - dot(dot(core.T, gram), core))
        store(out_refs, lanes(gains))

    gains = call(
        gain_body,
        pair(rank, coarse * rank),
        *late_parts,
        *found_parts[0],
        cores,
        flops=small * 2 * coarse,
        scratch=[pltpu.VMEM((rank, coarse * rank), FLOAT)],
    )

    def base_body(scale_ref, queries_ref, own_ref, other_ref, core_ref, *refs):
        factor_refs, basis_refs, scaled_refs = paired(refs[: 2 * head]), refs[2 * head : -5], refs[-5:-3]
        out_ref, stack_ref, gram_ref = refs[-3:]
        pieces = [pl.ds(late_size + b * head * batch, head * batch) for b in range(batches)]
        scatter([(own_ref.at[piece], other_ref.at[piece]) for piece in pieces], head, stack_ref)
        side = core_side()
        for late_ref, place in ((own_ref, side), (other_ref, 1 - side)):
            stack_ref[at(place, columns // 2), head * rank :] = late_ref[: columns // 2]
            for e in range(head):
                start = columns // 2 + e * half
                gram_ref[at(place, half), e * rank : (e + 1) * rank] = late_ref[start : start + half]
        products = [dot(core_ref[e].T, gram_ref[:, e * rank : (e + 1) * rank]) for e in range(head)]
        gains = [core_ref[e] + core_ref[e].T - dot(products[e], core_ref[e]) for e in range(1, head)]
        moments = [stack_ref[:, e * rank : (e + 1) * rank] for e in range(head)]
        first = dot(moments[0], core_ref[0], 1)
        found = [dot(stack_ref[:, head * rank :], core_ref[0]) - dot(first, products[0], 1)]
        found += [dot(moments[e], gains[e - 1], 1) for e in range(1, head)]
        for e in reversed(range(head - 1)):
            size = (head - 1 - e) * rank
            found[e] = found[e] - dot_parts(halves(lanes(found[e + 1 :])), take(factor_refs[e], 0, size), 1)
        left = [lanes([a[...], b[:, : head * rank]]) for a, b in zip(scaled_refs, basis_refs)]
        square = column_scale(scale_ref[...] * scale_ref[...])
        square = lanes([square] * (columns // rank))
        out_ref[...] = square * queries_ref[...] - dot_parts(left, halves(lanes([first, *found])), 1)

    (base,) = call(
        base_body,
        [(rows_here, columns)],
        scale,
        queries,
        *late_parts,
        cores,
        *flat(factors[:head]),
        *basis,
        *scaled,
        flops=small * 2 * (head + 1) * rows_here // rank,
        scratch=[pltpu.VMEM((columns, (head + 1) * rank), FLOAT), pltpu.VMEM((rank, head * rank), FLOAT)],
    )

    def last_body(base_ref, high_ref, low_ref, *refs):
        gain_refs, (out_ref, stack_ref) = refs[:2], refs[-2:]
        part_refs, factor_refs = paired(refs[2 : 2 + 2 * batches]), paired(refs[2 + 2 * batches : -2])
        scatter(part_refs, coarse, stack_ref)
        found = []
        for e in reversed(range(coarse)):
            where = slice(e * rank, (e + 1) * rank)
            value = dot_parts(halves(stack_ref[:, where]), [ref[:, where] for ref in gain_refs], 1)
            if found:
                value = value - dot_parts(halves(lanes(found)), [ref[...] for ref in factor_refs[e]], 1)
            found.insert(0, value)
        out_ref[...] = base_ref[...] - dot_parts([high_ref[...], low_ref[...]], halves(lanes(found)), 1)

    (out,) = call(
        last_body,
        [(rows_here, columns)],
        base,
        *answer,
        *gains,
        *flat(found_parts),
        *flat(factors[head:]),
        flops=small * 2 * coarse * rows_here // rank,
        scratch=[pltpu.VMEM((columns, coarse * rank), FLOAT)],
    )
    return out


def solution(mesh):
    in_specs = (
        P(("rows", "sub"), None),
        P(("rows", "sub")),
        P(("rows", "sub"), None),
        P("rows", None, None),
        P(None, ("rows", "sub"), None),
        P(),
    )
    out_specs = P(("rows", "sub"), None)

    return jax.shard_map(shards, mesh=mesh, in_specs=in_specs, out_specs=out_specs, check_vma=False)
```

```python
import functools

import jax
import jax.numpy as jnp
from jax import lax
from jax.experimental import pallas as pl
from jax.experimental.pallas import tpu as pltpu
from jax.sharding import PartitionSpec as P


FLOAT = jnp.float32
VMEM_LIMIT = 16 << 20


def halves(value):
    high = value.astype(jnp.bfloat16)
    return high, (value - high.astype(FLOAT)).astype(jnp.bfloat16)


def dot_parts(left, right, right_dim=0):
    mult = functools.partial(
        lax.dot_general,
        dimension_numbers=(((1,), (right_dim,)), ((), ())),
        preferred_element_type=FLOAT,
    )
    return mult(left[0], right[0]) + (mult(left[0], right[1]) + mult(left[1], right[0]))


def dot(left, right, right_dim=0):
    return dot_parts(halves(left), halves(right), right_dim)


def lanes(values):
    return values[0] if len(values) == 1 else jnp.concatenate(values, axis=1)


def column_scale(scale):
    size = scale.shape[1]
    return jnp.concatenate(
        [jnp.broadcast_to(scale[i : i + 1, :], (size, size)).T for i in range(scale.shape[0])], axis=0
    )


def core_side():
    return lax.rem(lax.axis_index("sub"), 2)


def at(index, size):
    return pl.ds(pl.multiple_of(index * size, 8), size)


def call(body, outs, *operands, flops, spaces=None, out_space=pltpu.VMEM, scratch=()):
    spaces = spaces or [pltpu.VMEM] * len(operands)
    size = sum(a.dtype.itemsize * a.size for a in operands)
    outs = [out if isinstance(out, jax.ShapeDtypeStruct) else jax.ShapeDtypeStruct(out, FLOAT) for out in outs]
    return pl.pallas_call(
        body,
        out_shape=outs,
        in_specs=[pl.BlockSpec(memory_space=space) for space in spaces],
        out_specs=[pl.BlockSpec(memory_space=out_space)] * len(outs),
        scratch_shapes=list(scratch),
        compiler_params=pltpu.CompilerParams(vmem_limit_bytes=VMEM_LIMIT),
        cost_estimate=pl.CostEstimate(flops=flops, bytes_accessed=size, transcendentals=0),
    )(*operands)


def pair(*shape):
    return [jax.ShapeDtypeStruct(shape, jnp.bfloat16)] * 2


def store(refs, value):
    for ref, part in zip(refs, halves(value)):
        ref[...] = part


def swap(array, axis, bit):
    return lax.ppermute(array, axis, [(i, i ^ 1 << bit) for i in range(lax.axis_size(axis))])


def partial_sums(array, axis, bits):
    bits = list(bits)
    if not bits:
        return [array]
    for bit in bits[:-1]:
        array = array + swap(array, axis, bit)
    return [array, swap(array, axis, bits[-1])]


def add_all(parts):
    return functools.reduce(lambda a, b: a + b, parts)


def shards(queries, row_scale, leaf_basis, leaf_cores, level_basis, level_cores):
    levels = level_basis.shape[0]
    count = levels + 1
    top = levels
    rows_here, rank = leaf_basis.shape
    columns = queries.shape[1]
    nodes, sub = lax.axis_size("rows"), lax.axis_size("sub")
    heights = [None] + [levels + 1 - e for e in range(1, count)]
    widths = [1] + [nodes // 2 ** heights[e] for e in range(1, count)]
    head = sum(w == 1 for w in widths)
    bits = [range(0)] + [
        range(widths[e - 1].bit_length() - 1, widths[e].bit_length() - 1) for e in range(1, count)
    ]
    blocks = [list(range(e + 1, count)) for e in range(count)]
    coarse = count - head
    leaf_bits = range(1, sub.bit_length() - 1)
    mine = columns // 2
    half = rank // 2
    batches = 2
    batch = mine // batches
    small = 2 * 3 * rank**3

    scale = row_scale.reshape(-1, rank)
    groups = [([e] if e >= head else []) + blocks[e] for e in range(count)]
    starts = [sum(len(b) for b in groups[:e]) * rank for e in range(count + 1)]

    def store_blocks(out_ref, vectors, group):
        parts = [None if v is None else halves(v) for v in vectors]
        side = core_side()
        for e in group:
            right = [lanes([parts[f][i] for f in groups[e]]) for i in range(2)]
            value = dot_parts(halves(vectors[e].T), right)
            where = slice(starts[e] - starts[group[0]], starts[e + 1] - starts[group[0]])
            for h in range(2):
                out_ref[at(h ^ side, half), where] = value[h * half : (h + 1) * half]

    def gram_body(*refs):
        scale_hbm, leaf_hbm, level_hbm, queries_hbm, leaf_core_hbm, core_hbm = refs[:6]
        out_ref, scale_ref, leaf_ref, level_ref, queries_ref, core_ref, sems = refs[6:]
        targets = [(scale_hbm, scale_ref), (leaf_hbm, leaf_ref)]
        targets += [(level_hbm.at[e], level_ref.at[e]) for e in reversed(range(levels))]
        place = lax.axis_index("rows")
        targets += [(queries_hbm, queries_ref), (leaf_core_hbm.at[0], core_ref.at[0])]
        for e in range(1, count):
            targets.append((core_hbm.at[2 ** heights[e] - 2 + place // widths[e]], core_ref.at[e]))
        copies = [pltpu.make_async_copy(a, b, sems.at[i]) for i, (a, b) in enumerate(targets)]
        for copy in copies:
            copy.start()
        for copy in copies[: 2 + levels]:
            copy.wait()
        vectors = [column_scale(scale_ref[...]) * leaf_ref[...]]
        vectors += [level_ref[levels - e] for e in range(1, count)]
        store_blocks(out_ref, vectors, range(head))
        for copy in copies[2 + levels :]:
            copy.wait()

    gram, scale, leaf_basis, level_basis, queries, cores = call(
        gram_body,
        [
            (rank, starts[head]),
            *[array.shape for array in (scale, leaf_basis, level_basis, queries)],
            (count, rank, rank),
        ],
        *[
            pltpu.with_memory_space_constraint(array, pltpu.HBM)
            for array in (scale, leaf_basis, level_basis, queries, leaf_cores, level_cores)
        ],
        flops=small * starts[head] // rank * rows_here // rank,
        spaces=[pltpu.HBM] * 6,
        scratch=[pltpu.SemaphoreType.DMA((3 + levels + count,))],
    )
    gram_chip = gram[:half] + swap(gram[half:], "sub", 0)
    early = add_all(partial_sums(gram_chip, "sub", leaf_bits))

    def moment_body(scale_ref, queries_ref, leaf_ref, level_ref, tail_ref, out_ref, *basis_refs):
        vectors = [level_ref[levels - e] if e >= head else None for e in range(count)]
        store_blocks(tail_ref, vectors, range(head, count))
        spread = column_scale(scale_ref[...])
        right = halves(lanes([leaf_ref[...]] + [spread * level_ref[levels - e] for e in range(1, count)]))
        for basis_ref, part in zip(basis_refs, right):
            basis_ref[...] = part
        value = dot_parts(halves(queries_ref[...].T), right)
        side = core_side()
        for h in range(2):
            out_ref[at(h ^ side, mine), :] = value[h * mine : (h + 1) * mine]

    tail, value, *basis = call(
        moment_body,
        [(rank, starts[count] - starts[head]), (columns, count * rank), *pair(rows_here, count * rank)],
        scale,
        queries,
        leaf_basis,
        level_basis,
        flops=small * count * 2 * rows_here // rank,
    )
    remaining, diagonal, coupling = tail[:half] + swap(tail[half:], "sub", 0), [], []
    for e in range(head, top):
        remaining = add_all(partial_sums(remaining, "rows", bits[e]))
        size = starts[e + 1] - starts[e]
        pieces = [remaining[:, :rank], remaining[:, rank:size], remaining[:, size:]]
        pieces = lax.optimization_barrier(pieces)
        diagonal.append(pieces[0])
        coupling.append(pieces[1])
        remaining = pieces[2]
    coupling = add_all(partial_sums(lanes([*coupling, remaining]), "sub", leaf_bits))
    top_block, coupling = coupling[:, -rank:], coupling[:, :-rank]

    moment_chip = value[:mine] + swap(value[mine:], "sub", 0)
    moment_parts = [moment_chip[b * batch : (b + 1) * batch] for b in range(batches)]
    moment_parts = [partial_sums(moment_parts[b], "sub", leaf_bits) for b in range(batches)]

    late_rows = columns // 2 + head * half

    def late_body(scale_ref, queries_ref, leaf_ref, level_ref, out_ref, *scaled_refs):
        spread = column_scale(scale_ref[...])
        vectors = spread * leaf_ref[...]
        side = core_side()
        scaled = halves(spread * vectors)
        for scaled_ref, part in zip(scaled_refs, scaled):
            scaled_ref[...] = part
        value = dot_parts(halves(queries_ref[...].T), scaled)
        for h in range(2):
            base = (h ^ side) * late_rows
            part = value[h * columns // 2 : (h + 1) * columns // 2]
            out_ref[pl.ds(pl.multiple_of(base, 8), columns // 2), :] = part
        for e in range(head):
            basis = vectors if e == 0 else level_ref[levels - e]
            value = dot(basis.T, basis)
            for h in range(2):
                base = (h ^ side) * late_rows + columns // 2 + e * half
                out_ref[pl.ds(pl.multiple_of(base, 8), half), :] = value[h * half : (h + 1) * half]

    late, *scaled = call(
        late_body,
        [(2 * late_rows, rank), *pair(rows_here, rank)],
        scale,
        queries,
        leaf_basis,
        level_basis,
        flops=small * (2 + head) * rows_here // rank,
    )
    late_chip = late[:late_rows] + swap(late[late_rows:], "sub", 0)

    late = jnp.concatenate([late_chip, *diagonal], axis=0)
    late_size = late.shape[0]
    late = add_all(partial_sums(late, "sub", leaf_bits))

    def product_body(group, own_ref, other_ref, core_ref, *refs):
        out_refs, stack_ref = refs[:-1], refs[-1]
        side = core_side()
        stack_ref[at(side, half), :] = own_ref[...]
        stack_ref[at(1 - side, half), :] = other_ref[...]
        place = 0
        for i, e in enumerate(group):
            block = stack_ref[:, place : place + len(blocks[e]) * rank]
            store(out_refs[2 * i : 2 * i + 2], dot(core_ref[e].T, block))
            place += len(blocks[e]) * rank

    def products(group, own):
        out = call(
            functools.partial(product_body, group),
            [part for e in group for part in pair(rank, len(blocks[e]) * rank)],
            own,
            swap(own, "sub", 0),
            cores,
            flops=small * sum(len(blocks[e]) for e in group),
            scratch=[pltpu.VMEM((rank, own.shape[1]), FLOAT)],
        )
        return [out[2 * i : 2 * i + 2] for i in range(len(group))]

    factors = products(list(range(head)), early)

    def flat(group):
        return [part for factor in group for part in factor]

    def paired(refs):
        return [refs[i : i + 2] for i in range(0, len(refs), 2)]

    def take(factor, start, size):
        return [ref[:, start : start + size] for ref in factor]

    def head_body(number, *refs):
        part_refs, factor_refs = refs[:number], paired(refs[number : number + 2 * head])
        own_ref, rest_ref = refs[number + 2 * head :]
        rest = add_all([part[...] for part in part_refs])
        for e in range(head):
            own, rest = rest[:, :rank], rest[:, rank:]
            own_ref[e * batch : (e + 1) * batch, :] = own
            rest = rest - dot_parts(halves(own), take(factor_refs[e], 0, rest.shape[1]))
        rest_ref[...] = rest

    def step_body(number, *refs):
        part_refs, factor, (own_ref, rest_ref) = refs[:number], refs[number:-2], refs[-2:]
        total = add_all([part[...] for part in part_refs])
        own, rest = total[:, :rank], total[:, rank:]
        own_ref[...] = own
        rest_ref[...] = rest - dot_parts(halves(own), take(factor, 0, rest.shape[1]))

    def scatter(parts, number, stack_ref):
        side = core_side()
        for b, part in enumerate(parts):
            for ref, place in zip(part, (side, 1 - side)):
                for e in range(number):
                    stack_ref[at(place * batches + b, batch), e * rank : (e + 1) * rank] = ref[
                        e * batch : (e + 1) * batch, :
                    ]

    factors += products(list(range(head, top)), coupling)
    head_moments, found_parts = [], []
    for b in range(batches):
        own, rest = call(
            functools.partial(head_body, len(moment_parts[b])),
            [(head * batch, rank), (batch, coarse * rank)],
            *moment_parts[b],
            *flat(factors[:head]),
            flops=small * sum(map(len, blocks[:head])) // batches,
        )
        head_moments.append(own)
        found = []
        for e in range(head, top):
            parts = partial_sums(rest, "rows", bits[e])
            own, rest = call(
                functools.partial(step_body, len(parts)),
                [(batch, rank), (batch, (top - e) * rank)],
                *parts,
                *factors[e],
                flops=small * (top - e) // batches,
            )
            found.append(own)
        if b == 0:
            rest = jnp.concatenate([rest, top_block], axis=0)
        found.append(add_all(partial_sums(rest, "rows", bits[top])))
        found = jnp.concatenate(found, axis=0)
        found_parts.append([found, swap(found, "sub", 0)])
    late = jnp.concatenate([late, *head_moments], axis=0)
    late_parts = [late, swap(late, "sub", 0)]

    def answer_body(*refs):
        factor_refs, basis_refs, out_refs = paired(refs[:-4]), refs[-4:-2], refs[-2:]
        shape = (coarse * rank, coarse * rank)
        line, column = (lax.broadcasted_iota(jnp.int32, shape, i) for i in range(2))
        gains = jnp.where(line == column, 1.0, 0.0)
        for f in reversed(range(head)):
            row = -dot_parts(take(factor_refs[f], 0, gains.shape[0]), halves(gains))
            gains = jnp.concatenate([row, gains], axis=0)
        store(out_refs, dot_parts([ref[...] for ref in basis_refs], halves(gains)))

    answer = call(
        answer_body,
        pair(rows_here, coarse * rank),
        *flat(factors[:head]),
        *basis,
        flops=small * coarse * count * rows_here // rank,
    )

    def gain_body(own_ref, other_ref, own_found_ref, other_found_ref, core_ref, *refs):
        out_refs, gram_ref = refs[:2], refs[2]
        side = core_side()
        sources = ((own_ref, own_found_ref, side), (other_ref, other_found_ref, 1 - side))
        for late_ref, found_ref, place in sources:
            gram_ref[at(place, half), (coarse - 1) * rank :] = found_ref[coarse * batch :]
            for e in range(head, top):
                start = columns // 2 + e * half
                where = slice((e - head) * rank, (e - head + 1) * rank)
                gram_ref[at(place, half), where] = late_ref[start : start + half]
        gains = []
        for e in range(head, count):
            core = core_ref[e]
            gram = gram_ref[:, (e - head) * rank : (e - head + 1) * rank]
            gains.append(core + core.T - dot(dot(core.T, gram), core))
        store(out_refs, lanes(gains))

    gains = call(
        gain_body,
        pair(rank, coarse * rank),
        *late_parts,
        *found_parts[0],
        cores,
        flops=small * 2 * coarse,
        scratch=[pltpu.VMEM((rank, coarse * rank), FLOAT)],
    )

    def base_body(scale_ref, queries_ref, own_ref, other_ref, core_ref, *refs):
        factor_refs, basis_refs, scaled_refs = paired(refs[: 2 * head]), refs[2 * head : -5], refs[-5:-3]
        out_ref, stack_ref, gram_ref = refs[-3:]
        pieces = [pl.ds(late_size + b * head * batch, head * batch) for b in range(batches)]
        scatter([(own_ref.at[piece], other_ref.at[piece]) for piece in pieces], head, stack_ref)
        side = core_side()
        for late_ref, place in ((own_ref, side), (other_ref, 1 - side)):
            stack_ref[at(place, columns // 2), head * rank :] = late_ref[: columns // 2]
            for e in range(head):
                start = columns // 2 + e * half
                gram_ref[at(place, half), e * rank : (e + 1) * rank] = late_ref[start : start + half]
        products = [dot(core_ref[e].T, gram_ref[:, e * rank : (e + 1) * rank]) for e in range(head)]
        gains = [core_ref[e] + core_ref[e].T - dot(products[e], core_ref[e]) for e in range(1, head)]
        moments = [stack_ref[:, e * rank : (e + 1) * rank] for e in range(head)]
        first = dot(moments[0], core_ref[0], 1)
        found = [dot(stack_ref[:, head * rank :], core_ref[0]) - dot(first, products[0], 1)]
        found += [dot(moments[e], gains[e - 1], 1) for e in range(1, head)]
        for e in reversed(range(head - 1)):
            size = (head - 1 - e) * rank
            found[e] = found[e] - dot_parts(halves(lanes(found[e + 1 :])), take(factor_refs[e], 0, size), 1)
        left = [lanes([a[...], b[:, : head * rank]]) for a, b in zip(scaled_refs, basis_refs)]
        square = column_scale(scale_ref[...] * scale_ref[...])
        square = lanes([square] * (columns // rank))
        out_ref[...] = square * queries_ref[...] - dot_parts(left, halves(lanes([first, *found])), 1)

    (base,) = call(
        base_body,
        [(rows_here, columns)],
        scale,
        queries,
        *late_parts,
        cores,
        *flat(factors[:head]),
        *basis,
        *scaled,
        flops=small * 2 * (head + 1) * rows_here // rank,
        scratch=[pltpu.VMEM((columns, (head + 1) * rank), FLOAT), pltpu.VMEM((rank, head * rank), FLOAT)],
    )

    def last_body(base_ref, high_ref, low_ref, *refs):
        gain_refs, (out_ref, stack_ref) = refs[:2], refs[-2:]
        part_refs, factor_refs = paired(refs[2 : 2 + 2 * batches]), paired(refs[2 + 2 * batches : -2])
        scatter(part_refs, coarse, stack_ref)
        found = []
        for e in reversed(range(coarse)):
            where = slice(e * rank, (e + 1) * rank)
            value = dot_parts(halves(stack_ref[:, where]), [ref[:, where] for ref in gain_refs], 1)
            if found:
                value = value - dot_parts(halves(lanes(found)), [ref[...] for ref in factor_refs[e]], 1)
            found.insert(0, value)
        out_ref[...] = base_ref[...] - dot_parts([high_ref[...], low_ref[...]], halves(lanes(found)), 1)

    (out,) = call(
        last_body,
        [(rows_here, columns)],
        base,
        *answer,
        *gains,
        *flat(found_parts),
        *flat(factors[head:]),
        flops=small * 2 * coarse * rows_here // rank,
        scratch=[pltpu.VMEM((columns, coarse * rank), FLOAT)],
    )
    return out


def solution(mesh):
    in_specs = (
        P(("rows", "sub"), None),
        P(("rows", "sub")),
        P(("rows", "sub"), None),
        P("rows", None, None),
        P(None, ("rows", "sub"), None),
        P(),
    )
    out_specs = P(("rows", "sub"), None)

    return jax.shard_map(shards, mesh=mesh, in_specs=in_specs, out_specs=out_specs, check_vma=False)
```

```python
import functools

import jax
import jax.numpy as jnp
from jax import lax
from jax.experimental import pallas as pl
from jax.experimental.pallas import tpu as pltpu
from jax.sharding import PartitionSpec as P


FLOAT = jnp.float32
VMEM_LIMIT = 16 << 20


def halves(value):
    high = value.astype(jnp.bfloat16)
    return high, (value - high.astype(FLOAT)).astype(jnp.bfloat16)


def dot_parts(left, right, right_dim=0):
    mult = functools.partial(
        lax.dot_general,
        dimension_numbers=(((1,), (right_dim,)), ((), ())),
        preferred_element_type=FLOAT,
    )
    return mult(left[0], right[0]) + (mult(left[0], right[1]) + mult(left[1], right[0]))


def dot(left, right, right_dim=0):
    return dot_parts(halves(left), halves(right), right_dim)


def lanes(values):
    return values[0] if len(values) == 1 else jnp.concatenate(values, axis=1)


def column_scale(scale):
    size = scale.shape[1]
    return jnp.concatenate(
        [jnp.broadcast_to(scale[i : i + 1, :], (size, size)).T for i in range(scale.shape[0])], axis=0
    )


def core_side():
    return lax.rem(lax.axis_index("sub"), 2)


def at(index, size):
    return pl.ds(pl.multiple_of(index * size, 8), size)


def call(body, outs, *operands, flops, spaces=None, out_space=pltpu.VMEM, scratch=()):
    spaces = spaces or [pltpu.VMEM] * len(operands)
    size = sum(a.dtype.itemsize * a.size for a in operands)
    outs = [out if isinstance(out, jax.ShapeDtypeStruct) else jax.ShapeDtypeStruct(out, FLOAT) for out in outs]
    return pl.pallas_call(
        body,
        out_shape=outs,
        in_specs=[pl.BlockSpec(memory_space=space) for space in spaces],
        out_specs=[pl.BlockSpec(memory_space=out_space)] * len(outs),
        scratch_shapes=list(scratch),
        compiler_params=pltpu.CompilerParams(vmem_limit_bytes=VMEM_LIMIT),
        cost_estimate=pl.CostEstimate(flops=flops, bytes_accessed=size, transcendentals=0),
    )(*operands)


def pair(*shape):
    return [jax.ShapeDtypeStruct(shape, jnp.bfloat16)] * 2


def store(refs, value):
    for ref, part in zip(refs, halves(value)):
        ref[...] = part


def swap(array, axis, bit):
    return lax.ppermute(array, axis, [(i, i ^ 1 << bit) for i in range(lax.axis_size(axis))])


def partial_sums(array, axis, bits):
    bits = list(bits)
    if not bits:
        return [array]
    for bit in bits[:-1]:
        array = array + swap(array, axis, bit)
    return [array, swap(array, axis, bits[-1])]


def add_all(parts):
    return functools.reduce(lambda a, b: a + b, parts)


def shards(queries, row_scale, leaf_basis, leaf_cores, level_basis, level_cores):
    levels = level_basis.shape[0]
    count = levels + 1
    top = levels
    rows_here, rank = leaf_basis.shape
    columns = queries.shape[1]
    nodes, sub = lax.axis_size("rows"), lax.axis_size("sub")
    heights = [None] + [levels + 1 - e for e in range(1, count)]
    widths = [1] + [nodes // 2 ** heights[e] for e in range(1, count)]
    head = sum(w == 1 for w in widths)
    bits = [range(0)] + [
        range(widths[e - 1].bit_length() - 1, widths[e].bit_length() - 1) for e in range(1, count)
    ]
    blocks = [list(range(e + 1, count)) for e in range(count)]
    coarse = count - head
    leaf_bits = range(1, sub.bit_length() - 1)
    mine = columns // 2
    half = rank // 2
    sizes = (3 * mine // 4, mine // 4)
    batches = len(sizes)
    offsets = [sum(sizes[:b]) for b in range(batches)]
    small = 2 * 3 * rank**3

    scale = row_scale.reshape(-1, rank)
    groups = [([e] if e >= head else []) + blocks[e] for e in range(count)]
    starts = [sum(len(b) for b in groups[:e]) * rank for e in range(count + 1)]

    def store_blocks(out_ref, vectors, group):
        parts = [None if v is None else halves(v) for v in vectors]
        side = core_side()
        for e in group:
            right = [lanes([parts[f][i] for f in groups[e]]) for i in range(2)]
            value = dot_parts(halves(vectors[e].T), right)
            where = slice(starts[e] - starts[group[0]], starts[e + 1] - starts[group[0]])
            for h in range(2):
                out_ref[at(h ^ side, half), where] = value[h * half : (h + 1) * half]

    def gram_body(*refs):
        scale_hbm, leaf_hbm, level_hbm, queries_hbm, leaf_core_hbm, core_hbm = refs[:6]
        out_ref, scale_ref, leaf_ref, level_ref, queries_ref, core_ref, sems = refs[6:]
        targets = [(scale_hbm, scale_ref), (leaf_hbm, leaf_ref)]
        targets += [(level_hbm.at[e], level_ref.at[e]) for e in reversed(range(levels))]
        place = lax.axis_index("rows")
        targets += [(queries_hbm, queries_ref), (leaf_core_hbm.at[0], core_ref.at[0])]
        for e in range(1, count):
            targets.append((core_hbm.at[2 ** heights[e] - 2 + place // widths[e]], core_ref.at[e]))
        copies = [pltpu.make_async_copy(a, b, sems.at[i]) for i, (a, b) in enumerate(targets)]
        for copy in copies:
            copy.start()
        for copy in copies[: 2 + levels]:
            copy.wait()
        vectors = [column_scale(scale_ref[...]) * leaf_ref[...]]
        vectors += [level_ref[levels - e] for e in range(1, count)]
        store_blocks(out_ref, vectors, range(head))
        for copy in copies[2 + levels :]:
            copy.wait()

    gram, scale, leaf_basis, level_basis, queries, cores = call(
        gram_body,
        [
            (rank, starts[head]),
            *[array.shape for array in (scale, leaf_basis, level_basis, queries)],
            (count, rank, rank),
        ],
        *[
            pltpu.with_memory_space_constraint(array, pltpu.HBM)
            for array in (scale, leaf_basis, level_basis, queries, leaf_cores, level_cores)
        ],
        flops=small * starts[head] // rank * rows_here // rank,
        spaces=[pltpu.HBM] * 6,
        scratch=[pltpu.SemaphoreType.DMA((3 + levels + count,))],
    )
    gram_chip = gram[:half] + swap(gram[half:], "sub", 0)
    early = add_all(partial_sums(gram_chip, "sub", leaf_bits))

    def moment_body(scale_ref, queries_ref, leaf_ref, level_ref, tail_ref, out_ref, *basis_refs):
        vectors = [level_ref[levels - e] if e >= head else None for e in range(count)]
        store_blocks(tail_ref, vectors, range(head, count))
        spread = column_scale(scale_ref[...])
        right = halves(lanes([leaf_ref[...]] + [spread * level_ref[levels - e] for e in range(1, count)]))
        for basis_ref, part in zip(basis_refs, right):
            basis_ref[...] = part
        value = dot_parts(halves(queries_ref[...].T), right)
        side = core_side()
        for h in range(2):
            out_ref[at(h ^ side, mine), :] = value[h * mine : (h + 1) * mine]

    tail, value, *basis = call(
        moment_body,
        [(rank, starts[count] - starts[head]), (columns, count * rank), *pair(rows_here, count * rank)],
        scale,
        queries,
        leaf_basis,
        level_basis,
        flops=small * count * 2 * rows_here // rank,
    )
    remaining, diagonal, coupling = tail[:half] + swap(tail[half:], "sub", 0), [], []
    for e in range(head, top):
        remaining = add_all(partial_sums(remaining, "rows", bits[e]))
        size = starts[e + 1] - starts[e]
        pieces = [remaining[:, :rank], remaining[:, rank:size], remaining[:, size:]]
        pieces = lax.optimization_barrier(pieces)
        diagonal.append(pieces[0])
        coupling.append(pieces[1])
        remaining = pieces[2]
    coupling = add_all(partial_sums(lanes([*coupling, remaining]), "sub", leaf_bits))
    top_block, coupling = coupling[:, -rank:], coupling[:, :-rank]

    moment_chip = value[:mine] + swap(value[mine:], "sub", 0)
    moment_parts = [moment_chip[offsets[b] : offsets[b] + sizes[b]] for b in range(batches)]
    moment_parts = [partial_sums(moment_parts[b], "sub", leaf_bits) for b in range(batches)]

    late_rows = columns // 2 + head * half

    def late_body(scale_ref, queries_ref, leaf_ref, level_ref, out_ref, *scaled_refs):
        spread = column_scale(scale_ref[...])
        vectors = spread * leaf_ref[...]
        side = core_side()
        scaled = halves(spread * vectors)
        for scaled_ref, part in zip(scaled_refs, scaled):
            scaled_ref[...] = part
        value = dot_parts(halves(queries_ref[...].T), scaled)
        for h in range(2):
            base = (h ^ side) * late_rows
            part = value[h * columns // 2 : (h + 1) * columns // 2]
            out_ref[pl.ds(pl.multiple_of(base, 8), columns // 2), :] = part
        for e in range(head):
            basis = vectors if e == 0 else level_ref[levels - e]
            value = dot(basis.T, basis)
            for h in range(2):
                base = (h ^ side) * late_rows + columns // 2 + e * half
                out_ref[pl.ds(pl.multiple_of(base, 8), half), :] = value[h * half : (h + 1) * half]

    late, *scaled = call(
        late_body,
        [(2 * late_rows, rank), *pair(rows_here, rank)],
        scale,
        queries,
        leaf_basis,
        level_basis,
        flops=small * (2 + head) * rows_here // rank,
    )
    late_chip = late[:late_rows] + swap(late[late_rows:], "sub", 0)

    late = jnp.concatenate([late_chip, *diagonal], axis=0)
    late_size = late.shape[0]
    late = add_all(partial_sums(late, "sub", leaf_bits))

    def product_body(group, own_ref, other_ref, core_ref, *refs):
        out_refs, stack_ref = refs[:-1], refs[-1]
        side = core_side()
        stack_ref[at(side, half), :] = own_ref[...]
        stack_ref[at(1 - side, half), :] = other_ref[...]
        place = 0
        for i, e in enumerate(group):
            block = stack_ref[:, place : place + len(blocks[e]) * rank]
            store(out_refs[2 * i : 2 * i + 2], dot(core_ref[e].T, block))
            place += len(blocks[e]) * rank

    def products(group, own):
        out = call(
            functools.partial(product_body, group),
            [part for e in group for part in pair(rank, len(blocks[e]) * rank)],
            own,
            swap(own, "sub", 0),
            cores,
            flops=small * sum(len(blocks[e]) for e in group),
            scratch=[pltpu.VMEM((rank, own.shape[1]), FLOAT)],
        )
        return [out[2 * i : 2 * i + 2] for i in range(len(group))]

    factors = products(list(range(head)), early)

    def flat(group):
        return [part for factor in group for part in factor]

    def paired(refs):
        return [refs[i : i + 2] for i in range(0, len(refs), 2)]

    def take(factor, start, size):
        return [ref[:, start : start + size] for ref in factor]

    def head_body(number, *refs):
        part_refs, factor_refs = refs[:number], paired(refs[number : number + 2 * head])
        own_ref, rest_ref = refs[number + 2 * head :]
        rest = add_all([part[...] for part in part_refs])
        for e in range(head):
            own, rest = rest[:, :rank], rest[:, rank:]
            own_ref[e * own.shape[0] : (e + 1) * own.shape[0], :] = own
            rest = rest - dot_parts(halves(own), take(factor_refs[e], 0, rest.shape[1]))
        rest_ref[...] = rest

    def step_body(number, *refs):
        part_refs, factor, (own_ref, rest_ref) = refs[:number], refs[number:-2], refs[-2:]
        total = add_all([part[...] for part in part_refs])
        own, rest = total[:, :rank], total[:, rank:]
        own_ref[...] = own
        rest_ref[...] = rest - dot_parts(halves(own), take(factor, 0, rest.shape[1]))

    def scatter(parts, number, stack_ref):
        side = core_side()
        for part, size, offset in zip(parts, sizes, offsets):
            for ref, place in zip(part, (side, 1 - side)):
                rows = pl.ds(pl.multiple_of(place * mine + offset, 8), size)
                for e in range(number):
                    stack_ref[rows, e * rank : (e + 1) * rank] = ref[e * size : (e + 1) * size, :]

    factors += products(list(range(head, top)), coupling)
    head_moments, found_parts = [], []
    for b, size in enumerate(sizes):
        own, rest = call(
            functools.partial(head_body, len(moment_parts[b])),
            [(head * size, rank), (size, coarse * rank)],
            *moment_parts[b],
            *flat(factors[:head]),
            flops=small * sum(map(len, blocks[:head])) // batches,
        )
        head_moments.append(own)
        found = []
        for e in range(head, top):
            parts = partial_sums(rest, "rows", bits[e])
            own, rest = call(
                functools.partial(step_body, len(parts)),
                [(size, rank), (size, (top - e) * rank)],
                *parts,
                *factors[e],
                flops=small * (top - e) // batches,
            )
            found.append(own)
        if b == 0:
            rest = jnp.concatenate([rest, top_block], axis=0)
        found.append(add_all(partial_sums(rest, "rows", bits[top])))
        found = jnp.concatenate(found, axis=0)
        found_parts.append([found, swap(found, "sub", 0)])
    late = jnp.concatenate([late, *head_moments], axis=0)
    late_parts = [late, swap(late, "sub", 0)]

    def answer_body(*refs):
        factor_refs, basis_refs, out_refs = paired(refs[:-4]), refs[-4:-2], refs[-2:]
        shape = (coarse * rank, coarse * rank)
        line, column = (lax.broadcasted_iota(jnp.int32, shape, i) for i in range(2))
        gains = jnp.where(line == column, 1.0, 0.0)
        for f in reversed(range(head)):
            row = -dot_parts(take(factor_refs[f], 0, gains.shape[0]), halves(gains))
            gains = jnp.concatenate([row, gains], axis=0)
        store(out_refs, dot_parts([ref[...] for ref in basis_refs], halves(gains)))

    answer = call(
        answer_body,
        pair(rows_here, coarse * rank),
        *flat(factors[:head]),
        *basis,
        flops=small * coarse * count * rows_here // rank,
    )

    def gain_body(own_ref, other_ref, own_found_ref, other_found_ref, core_ref, *refs):
        out_refs, gram_ref = refs[:2], refs[2]
        side = core_side()
        sources = ((own_ref, own_found_ref, side), (other_ref, other_found_ref, 1 - side))
        for late_ref, found_ref, place in sources:
            gram_ref[at(place, half), (coarse - 1) * rank :] = found_ref[coarse * sizes[0] :]
            for e in range(head, top):
                start = columns // 2 + e * half
                where = slice((e - head) * rank, (e - head + 1) * rank)
                gram_ref[at(place, half), where] = late_ref[start : start + half]
        gains = []
        for e in range(head, count):
            core = core_ref[e]
            gram = gram_ref[:, (e - head) * rank : (e - head + 1) * rank]
            gains.append(core + core.T - dot(dot(core.T, gram), core))
        store(out_refs, lanes(gains))

    gains = call(
        gain_body,
        pair(rank, coarse * rank),
        *late_parts,
        *found_parts[0],
        cores,
        flops=small * 2 * coarse,
        scratch=[pltpu.VMEM((rank, coarse * rank), FLOAT)],
    )

    def base_body(scale_ref, queries_ref, own_ref, other_ref, core_ref, *refs):
        factor_refs, basis_refs, scaled_refs = paired(refs[: 2 * head]), refs[2 * head : -5], refs[-5:-3]
        out_ref, stack_ref, gram_ref = refs[-3:]
        pieces = [pl.ds(late_size + head * offset, head * size) for size, offset in zip(sizes, offsets)]
        scatter([(own_ref.at[piece], other_ref.at[piece]) for piece in pieces], head, stack_ref)
        side = core_side()
        for late_ref, place in ((own_ref, side), (other_ref, 1 - side)):
            stack_ref[at(place, columns // 2), head * rank :] = late_ref[: columns // 2]
            for e in range(head):
                start = columns // 2 + e * half
                gram_ref[at(place, half), e * rank : (e + 1) * rank] = late_ref[start : start + half]
        products = [dot(core_ref[e].T, gram_ref[:, e * rank : (e + 1) * rank]) for e in range(head)]
        gains = [core_ref[e] + core_ref[e].T - dot(products[e], core_ref[e]) for e in range(1, head)]
        moments = [stack_ref[:, e * rank : (e + 1) * rank] for e in range(head)]
        first = dot(moments[0], core_ref[0], 1)
        found = [dot(stack_ref[:, head * rank :], core_ref[0]) - dot(first, products[0], 1)]
        found += [dot(moments[e], gains[e - 1], 1) for e in range(1, head)]
        for e in reversed(range(head - 1)):
            size = (head - 1 - e) * rank
            found[e] = found[e] - dot_parts(halves(lanes(found[e + 1 :])), take(factor_refs[e], 0, size), 1)
        left = [lanes([a[...], b[:, : head * rank]]) for a, b in zip(scaled_refs, basis_refs)]
        square = column_scale(scale_ref[...] * scale_ref[...])
        square = lanes([square] * (columns // rank))
        out_ref[...] = square * queries_ref[...] - dot_parts(left, halves(lanes([first, *found])), 1)

    (base,) = call(
        base_body,
        [(rows_here, columns)],
        scale,
        queries,
        *late_parts,
        cores,
        *flat(factors[:head]),
        *basis,
        *scaled,
        flops=small * 2 * (head + 1) * rows_here // rank,
        scratch=[pltpu.VMEM((columns, (head + 1) * rank), FLOAT), pltpu.VMEM((rank, head * rank), FLOAT)],
    )

    def last_body(base_ref, high_ref, low_ref, *refs):
        gain_refs, (out_ref, stack_ref) = refs[:2], refs[-2:]
        part_refs, factor_refs = paired(refs[2 : 2 + 2 * batches]), paired(refs[2 + 2 * batches : -2])
        scatter(part_refs, coarse, stack_ref)
        found = []
        for e in reversed(range(coarse)):
            where = slice(e * rank, (e + 1) * rank)
            value = dot_parts(halves(stack_ref[:, where]), [ref[:, where] for ref in gain_refs], 1)
            if found:
                value = value - dot_parts(halves(lanes(found)), [ref[...] for ref in factor_refs[e]], 1)
            found.insert(0, value)
        out_ref[...] = base_ref[...] - dot_parts([high_ref[...], low_ref[...]], halves(lanes(found)), 1)

    (out,) = call(
        last_body,
        [(rows_here, columns)],
        base,
        *answer,
        *gains,
        *flat(found_parts),
        *flat(factors[head:]),
        flops=small * 2 * coarse * rows_here // rank,
        scratch=[pltpu.VMEM((columns, coarse * rank), FLOAT)],
    )
    return out


def solution(mesh):
    in_specs = (
        P(("rows", "sub"), None),
        P(("rows", "sub")),
        P(("rows", "sub"), None),
        P("rows", None, None),
        P(None, ("rows", "sub"), None),
        P(),
    )
    out_specs = P(("rows", "sub"), None)

    return jax.shard_map(shards, mesh=mesh, in_specs=in_specs, out_specs=out_specs, check_vma=False)
```

```python
import functools

import jax
import jax.numpy as jnp
from jax import lax
from jax.experimental import pallas as pl
from jax.experimental.pallas import tpu as pltpu
from jax.sharding import PartitionSpec as P


FLOAT = jnp.float32
VMEM_LIMIT = 16 << 20


def halves(value):
    high = value.astype(jnp.bfloat16)
    return high, (value - high.astype(FLOAT)).astype(jnp.bfloat16)


def dot_parts(left, right, right_dim=0):
    mult = functools.partial(
        lax.dot_general,
        dimension_numbers=(((1,), (right_dim,)), ((), ())),
        preferred_element_type=FLOAT,
    )
    return mult(left[0], right[0]) + (mult(left[0], right[1]) + mult(left[1], right[0]))


def dot(left, right, right_dim=0):
    return dot_parts(halves(left), halves(right), right_dim)


def lanes(values):
    return values[0] if len(values) == 1 else jnp.concatenate(values, axis=1)


def column_scale(scale):
    size = scale.shape[1]
    return jnp.concatenate(
        [jnp.broadcast_to(scale[i : i + 1, :], (size, size)).T for i in range(scale.shape[0])], axis=0
    )


def core_side():
    return lax.rem(lax.axis_index("sub"), 2)


def at(index, size):
    return pl.ds(pl.multiple_of(index * size, 8), size)


def call(body, outs, *operands, flops, spaces=None, out_space=pltpu.VMEM, scratch=()):
    spaces = spaces or [pltpu.VMEM] * len(operands)
    size = sum(a.dtype.itemsize * a.size for a in operands)
    outs = [out if isinstance(out, jax.ShapeDtypeStruct) else jax.ShapeDtypeStruct(out, FLOAT) for out in outs]
    return pl.pallas_call(
        body,
        out_shape=outs,
        in_specs=[pl.BlockSpec(memory_space=space) for space in spaces],
        out_specs=[pl.BlockSpec(memory_space=out_space)] * len(outs),
        scratch_shapes=list(scratch),
        compiler_params=pltpu.CompilerParams(vmem_limit_bytes=VMEM_LIMIT),
        cost_estimate=pl.CostEstimate(flops=flops, bytes_accessed=size, transcendentals=0),
    )(*operands)


def pair(*shape):
    return [jax.ShapeDtypeStruct(shape, jnp.bfloat16)] * 2


def store(refs, value):
    for ref, part in zip(refs, halves(value)):
        ref[...] = part


def swap(array, axis, bit):
    return lax.ppermute(array, axis, [(i, i ^ 1 << bit) for i in range(lax.axis_size(axis))])


def partial_sums(array, axis, bits):
    bits = list(bits)
    if not bits:
        return [array]
    for bit in bits[:-1]:
        array = array + swap(array, axis, bit)
    return [array, swap(array, axis, bits[-1])]


def add_all(parts):
    return functools.reduce(lambda a, b: a + b, parts)


def shards(queries, row_scale, leaf_basis, leaf_cores, level_basis, level_cores):
    levels = level_basis.shape[0]
    count = levels + 1
    top = levels
    rows_here, rank = leaf_basis.shape
    columns = queries.shape[1]
    nodes, sub = lax.axis_size("rows"), lax.axis_size("sub")
    heights = [None] + [levels + 1 - e for e in range(1, count)]
    widths = [1] + [nodes // 2 ** heights[e] for e in range(1, count)]
    head = sum(w == 1 for w in widths)
    bits = [range(0)] + [
        range(widths[e - 1].bit_length() - 1, widths[e].bit_length() - 1) for e in range(1, count)
    ]
    blocks = [list(range(e + 1, count)) for e in range(count)]
    coarse = count - head
    leaf_bits = range(1, sub.bit_length() - 1)
    mine = columns // 2
    half = rank // 2
    sizes = (5 * mine // 8, 3 * mine // 8)
    batches = len(sizes)
    offsets = [sum(sizes[:b]) for b in range(batches)]
    small = 2 * 3 * rank**3

    scale = row_scale.reshape(-1, rank)
    groups = [([e] if e >= head else []) + blocks[e] for e in range(count)]
    starts = [sum(len(b) for b in groups[:e]) * rank for e in range(count + 1)]

    def store_blocks(out_ref, vectors, group):
        parts = [None if v is None else halves(v) for v in vectors]
        side = core_side()
        for e in group:
            right = [lanes([parts[f][i] for f in groups[e]]) for i in range(2)]
            value = dot_parts(halves(vectors[e].T), right)
            where = slice(starts[e] - starts[group[0]], starts[e + 1] - starts[group[0]])
            for h in range(2):
                out_ref[at(h ^ side, half), where] = value[h * half : (h + 1) * half]

    def gram_body(*refs):
        scale_hbm, leaf_hbm, level_hbm, queries_hbm, leaf_core_hbm, core_hbm = refs[:6]
        out_ref, scale_ref, leaf_ref, level_ref, queries_ref, core_ref, sems = refs[6:]
        targets = [(scale_hbm, scale_ref), (leaf_hbm, leaf_ref)]
        targets += [(level_hbm.at[e], level_ref.at[e]) for e in reversed(range(levels))]
        place = lax.axis_index("rows")
        targets += [(queries_hbm, queries_ref), (leaf_core_hbm.at[0], core_ref.at[0])]
        for e in range(1, count):
            targets.append((core_hbm.at[2 ** heights[e] - 2 + place // widths[e]], core_ref.at[e]))
        copies = [pltpu.make_async_copy(a, b, sems.at[i]) for i, (a, b) in enumerate(targets)]
        for copy in copies[: 2 + levels]:
            copy.start()
        for copy in copies[: 2 + levels]:
            copy.wait()
        for copy in copies[2 + levels :]:
            copy.start()
        vectors = [column_scale(scale_ref[...]) * leaf_ref[...]]
        vectors += [level_ref[levels - e] for e in range(1, count)]
        store_blocks(out_ref, vectors, range(head))
        for copy in copies[2 + levels :]:
            copy.wait()

    gram, scale, leaf_basis, level_basis, queries, cores = call(
        gram_body,
        [
            (rank, starts[head]),
            *[array.shape for array in (scale, leaf_basis, level_basis, queries)],
            (count, rank, rank),
        ],
        *[
            pltpu.with_memory_space_constraint(array, pltpu.HBM)
            for array in (scale, leaf_basis, level_basis, queries, leaf_cores, level_cores)
        ],
        flops=small * starts[head] // rank * rows_here // rank,
        spaces=[pltpu.HBM] * 6,
        scratch=[pltpu.SemaphoreType.DMA((3 + levels + count,))],
    )
    gram_chip = gram[:half] + swap(gram[half:], "sub", 0)
    early = add_all(partial_sums(gram_chip, "sub", leaf_bits))

    def moment_body(scale_ref, queries_ref, leaf_ref, level_ref, tail_ref, out_ref, *basis_refs):
        vectors = [level_ref[levels - e] if e >= head else None for e in range(count)]
        store_blocks(tail_ref, vectors, range(head, count))
        spread = column_scale(scale_ref[...])
        right = halves(lanes([leaf_ref[...]] + [spread * level_ref[levels - e] for e in range(1, count)]))
        for basis_ref, part in zip(basis_refs, right):
            basis_ref[...] = part
        value = dot_parts(halves(queries_ref[...].T), right)
        side = core_side()
        for h in range(2):
            out_ref[at(h ^ side, mine), :] = value[h * mine : (h + 1) * mine]

    tail, value, *basis = call(
        moment_body,
        [(rank, starts[count] - starts[head]), (columns, count * rank), *pair(rows_here, count * rank)],
        scale,
        queries,
        leaf_basis,
        level_basis,
        flops=small * count * 2 * rows_here // rank,
    )
    remaining, diagonal, coupling = tail[:half] + swap(tail[half:], "sub", 0), [], []
    for e in range(head, top):
        remaining = add_all(partial_sums(remaining, "rows", bits[e]))
        size = starts[e + 1] - starts[e]
        pieces = [remaining[:, :rank], remaining[:, rank:size], remaining[:, size:]]
        pieces = lax.optimization_barrier(pieces)
        diagonal.append(pieces[0])
        coupling.append(pieces[1])
        remaining = pieces[2]
    coupling = add_all(partial_sums(lanes([*coupling, remaining]), "sub", leaf_bits))
    top_block, coupling = coupling[:, -rank:], coupling[:, :-rank]

    moment_chip = value[:mine] + swap(value[mine:], "sub", 0)
    moment_parts = [moment_chip[offsets[b] : offsets[b] + sizes[b]] for b in range(batches)]
    moment_parts = [partial_sums(moment_parts[b], "sub", leaf_bits) for b in range(batches)]

    late_rows = columns // 2 + head * half

    def late_body(scale_ref, queries_ref, leaf_ref, level_ref, out_ref, *scaled_refs):
        spread = column_scale(scale_ref[...])
        vectors = spread * leaf_ref[...]
        side = core_side()
        scaled = halves(spread * vectors)
        for scaled_ref, part in zip(scaled_refs, scaled):
            scaled_ref[...] = part
        value = dot_parts(halves(queries_ref[...].T), scaled)
        for h in range(2):
            base = (h ^ side) * late_rows
            part = value[h * columns // 2 : (h + 1) * columns // 2]
            out_ref[pl.ds(pl.multiple_of(base, 8), columns // 2), :] = part
        for e in range(head):
            basis = vectors if e == 0 else level_ref[levels - e]
            value = dot(basis.T, basis)
            for h in range(2):
                base = (h ^ side) * late_rows + columns // 2 + e * half
                out_ref[pl.ds(pl.multiple_of(base, 8), half), :] = value[h * half : (h + 1) * half]

    late, *scaled = call(
        late_body,
        [(2 * late_rows, rank), *pair(rows_here, rank)],
        scale,
        queries,
        leaf_basis,
        level_basis,
        flops=small * (2 + head) * rows_here // rank,
    )
    late_chip = late[:late_rows] + swap(late[late_rows:], "sub", 0)

    late = jnp.concatenate([late_chip, *diagonal], axis=0)
    late_size = late.shape[0]
    late = add_all(partial_sums(late, "sub", leaf_bits))

    def product_body(group, own_ref, other_ref, core_ref, *refs):
        out_refs, stack_ref = refs[:-1], refs[-1]
        side = core_side()
        stack_ref[at(side, half), :] = own_ref[...]
        stack_ref[at(1 - side, half), :] = other_ref[...]
        place = 0
        for i, e in enumerate(group):
            block = stack_ref[:, place : place + len(blocks[e]) * rank]
            store(out_refs[2 * i : 2 * i + 2], dot(core_ref[e].T, block))
            place += len(blocks[e]) * rank

    def products(group, own):
        out = call(
            functools.partial(product_body, group),
            [part for e in group for part in pair(rank, len(blocks[e]) * rank)],
            own,
            swap(own, "sub", 0),
            cores,
            flops=small * sum(len(blocks[e]) for e in group),
            scratch=[pltpu.VMEM((rank, own.shape[1]), FLOAT)],
        )
        return [out[2 * i : 2 * i + 2] for i in range(len(group))]

    factors = products(list(range(head)), early)

    def flat(group):
        return [part for factor in group for part in factor]

    def paired(refs):
        return [refs[i : i + 2] for i in range(0, len(refs), 2)]

    def take(factor, start, size):
        return [ref[:, start : start + size] for ref in factor]

    def head_body(number, *refs):
        part_refs, factor_refs = refs[:number], paired(refs[number : number + 2 * head])
        own_ref, rest_ref = refs[number + 2 * head :]
        rest = add_all([part[...] for part in part_refs])
        for e in range(head):
            own, rest = rest[:, :rank], rest[:, rank:]
            own_ref[e * own.shape[0] : (e + 1) * own.shape[0], :] = own
            rest = rest - dot_parts(halves(own), take(factor_refs[e], 0, rest.shape[1]))
        rest_ref[...] = rest

    def step_body(number, *refs):
        part_refs, factor, (own_ref, rest_ref) = refs[:number], refs[number:-2], refs[-2:]
        total = add_all([part[...] for part in part_refs])
        own, rest = total[:, :rank], total[:, rank:]
        own_ref[...] = own
        rest_ref[...] = rest - dot_parts(halves(own), take(factor, 0, rest.shape[1]))

    def scatter(parts, number, stack_ref):
        side = core_side()
        for part, size, offset in zip(parts, sizes, offsets):
            for ref, place in zip(part, (side, 1 - side)):
                rows = pl.ds(pl.multiple_of(place * mine + offset, 8), size)
                for e in range(number):
                    stack_ref[rows, e * rank : (e + 1) * rank] = ref[e * size : (e + 1) * size, :]

    factors += products(list(range(head, top)), coupling)
    head_moments, found_parts = [], []
    for b, size in enumerate(sizes):
        own, rest = call(
            functools.partial(head_body, len(moment_parts[b])),
            [(head * size, rank), (size, coarse * rank)],
            *moment_parts[b],
            *flat(factors[:head]),
            flops=small * sum(map(len, blocks[:head])) // batches,
        )
        head_moments.append(own)
        found = []
        for e in range(head, top):
            parts = partial_sums(rest, "rows", bits[e])
            own, rest = call(
                functools.partial(step_body, len(parts)),
                [(size, rank), (size, (top - e) * rank)],
                *parts,
                *factors[e],
                flops=small * (top - e) // batches,
            )
            found.append(own)
        if b == 0:
            rest = jnp.concatenate([rest, top_block], axis=0)
        found.append(add_all(partial_sums(rest, "rows", bits[top])))
        found = jnp.concatenate(found, axis=0)
        found_parts.append([found, swap(found, "sub", 0)])
    late = jnp.concatenate([late, *head_moments], axis=0)
    late_parts = [late, swap(late, "sub", 0)]

    def answer_body(*refs):
        factor_refs, basis_refs, out_refs = paired(refs[:-4]), refs[-4:-2], refs[-2:]
        shape = (coarse * rank, coarse * rank)
        line, column = (lax.broadcasted_iota(jnp.int32, shape, i) for i in range(2))
        gains = jnp.where(line == column, 1.0, 0.0)
        for f in reversed(range(head)):
            row = -dot_parts(take(factor_refs[f], 0, gains.shape[0]), halves(gains))
            gains = jnp.concatenate([row, gains], axis=0)
        store(out_refs, dot_parts([ref[...] for ref in basis_refs], halves(gains)))

    answer = call(
        answer_body,
        pair(rows_here, coarse * rank),
        *flat(factors[:head]),
        *basis,
        flops=small * coarse * count * rows_here // rank,
    )

    def gain_body(own_ref, other_ref, own_found_ref, other_found_ref, core_ref, *refs):
        factor_refs, out_refs, gram_ref = paired(refs[:-3]), refs[-3:-1], refs[-1]
        side = core_side()
        sources = ((own_ref, own_found_ref, side), (other_ref, other_found_ref, 1 - side))
        for late_ref, found_ref, place in sources:
            gram_ref[at(place, half), (coarse - 1) * rank :] = found_ref[coarse * sizes[0] :]
            for e in range(head, top):
                start = columns // 2 + e * half
                where = slice((e - head) * rank, (e - head + 1) * rank)
                gram_ref[at(place, half), where] = late_ref[start : start + half]
        gains = None
        for e in reversed(range(head, count)):
            core = core_ref[e]
            gram = gram_ref[:, (e - head) * rank : (e - head + 1) * rank]
            row = core + core.T - dot(dot(core.T, gram), core)
            if gains is not None:
                row = lanes([row, -dot_parts([ref[...] for ref in factor_refs[e - head]], halves(gains))])
                gains = lanes([jnp.zeros((gains.shape[0], rank), FLOAT), gains])
                row = jnp.concatenate([row, gains], axis=0)
            gains = row
        store(out_refs, gains)

    gains = call(
        gain_body,
        pair(coarse * rank, coarse * rank),
        *late_parts,
        *found_parts[0],
        cores,
        *flat(factors[head:]),
        flops=small * 2 * coarse,
        scratch=[pltpu.VMEM((rank, coarse * rank), FLOAT)],
    )

    def base_body(scale_ref, queries_ref, own_ref, other_ref, core_ref, *refs):
        factor_refs, basis_refs, scaled_refs = paired(refs[: 2 * head]), refs[2 * head : -5], refs[-5:-3]
        out_ref, stack_ref, gram_ref = refs[-3:]
        pieces = [pl.ds(late_size + head * offset, head * size) for size, offset in zip(sizes, offsets)]
        scatter([(own_ref.at[piece], other_ref.at[piece]) for piece in pieces], head, stack_ref)
        side = core_side()
        for late_ref, place in ((own_ref, side), (other_ref, 1 - side)):
            stack_ref[at(place, columns // 2), head * rank :] = late_ref[: columns // 2]
            for e in range(head):
                start = columns // 2 + e * half
                gram_ref[at(place, half), e * rank : (e + 1) * rank] = late_ref[start : start + half]
        products = [dot(core_ref[e].T, gram_ref[:, e * rank : (e + 1) * rank]) for e in range(head)]
        gains = [core_ref[e] + core_ref[e].T - dot(products[e], core_ref[e]) for e in range(1, head)]
        moments = [stack_ref[:, e * rank : (e + 1) * rank] for e in range(head)]
        first = dot(moments[0], core_ref[0], 1)
        found = [dot(stack_ref[:, head * rank :], core_ref[0]) - dot(first, products[0], 1)]
        found += [dot(moments[e], gains[e - 1], 1) for e in range(1, head)]
        for e in reversed(range(head - 1)):
            size = (head - 1 - e) * rank
            found[e] = found[e] - dot_parts(halves(lanes(found[e + 1 :])), take(factor_refs[e], 0, size), 1)
        left = [lanes([a[...], b[:, : head * rank]]) for a, b in zip(scaled_refs, basis_refs)]
        square = column_scale(scale_ref[...] * scale_ref[...])
        square = lanes([square] * (columns // rank))
        out_ref[...] = square * queries_ref[...] - dot_parts(left, halves(lanes([first, *found])), 1)

    (base,) = call(
        base_body,
        [(rows_here, columns)],
        scale,
        queries,
        *late_parts,
        cores,
        *flat(factors[:head]),
        *basis,
        *scaled,
        flops=small * 2 * (head + 1) * rows_here // rank,
        scratch=[pltpu.VMEM((columns, (head + 1) * rank), FLOAT), pltpu.VMEM((rank, head * rank), FLOAT)],
    )

    def last_body(base_ref, high_ref, low_ref, *refs):
        gain_refs, part_refs, (out_ref, stack_ref) = refs[:2], paired(refs[2:-2]), refs[-2:]
        scatter(part_refs, coarse, stack_ref)
        found = dot_parts(halves(stack_ref[...]), [ref[...] for ref in gain_refs], 1)
        out_ref[...] = base_ref[...] - dot_parts([high_ref[...], low_ref[...]], halves(found), 1)

    (out,) = call(
        last_body,
        [(rows_here, columns)],
        base,
        *answer,
        *gains,
        *flat(found_parts),
        flops=small * 2 * coarse * rows_here // rank,
        scratch=[pltpu.VMEM((columns, coarse * rank), FLOAT)],
    )
    return out


def solution(mesh):
    in_specs = (
        P(("rows", "sub"), None),
        P(("rows", "sub")),
        P(("rows", "sub"), None),
        P("rows", None, None),
        P(None, ("rows", "sub"), None),
        P(),
    )
    out_specs = P(("rows", "sub"), None)

    return jax.shard_map(shards, mesh=mesh, in_specs=in_specs, out_specs=out_specs, check_vma=False)
```
